32 devices in a mesh: replica: 8 (over z, core), tensor: 4 (over y, x).
Axes of the slice: x: 2, y: 2, z: 4, core: 2. Of those that a mesh axis runs over, the one named last changes fastest.
Arguments:
- hidden: bfloat16 [3, 64, 8192], P(None, None, 'replica'), may hold values from -6 to 6
- parents: int32 [3, 64], replicated, may hold values from 0 to 63, as said below
- input_weight: bfloat16 [8192, 2, 8192], P('replica', None, 'tensor'), may hold values from -0.0625 to 0.0625
- coeff_weight: bfloat16 [8192, 2, 512], P('replica'), may hold values from -0.0625 to 0.0625
- step_weight: bfloat16 [8192, 128], P('replica', 'tensor'), may hold values from -0.0625 to 0.0625
- kernel_x: float32 [4, 8192], P(None, 'tensor'), may hold values from -0.5 to 0.5
- kernel_bias_x: float32 [8192], P('tensor'), may hold values from -0.5 to 0.5
- kernel_coeff: float32 [4, 2, 512], replicated, may hold values from -0.5 to 0.5
- kernel_bias_coeff: float32 [2, 512], replicated, may hold values from -0.5 to 0.5
- step_bias: float32 [128], P('tensor'), may hold values from -3 to 0
- log_rate: float32 [128], P('tensor'), may hold values from -4 to 0.7
- skip_gain: float32 [128], P('tensor'), may hold values from 0.5 to 2
- norm_gain: float32 [8192], P('tensor'), may hold values from 0.1 to 1.9
- output_weight: bfloat16 [8192, 8192], P('tensor', 'replica'), may hold values from -0.0625 to 0.0625
- scan_state: float32 [64, 128, 64, 128], P('replica', 'tensor'), may hold values from -6 to 6
- window_x: float32 [64, 3, 8192], P('replica', None, 'tensor'), may hold values from -6 to 6
- window_coeff: float32 [64, 3, 2, 512], P('replica'), may hold values from -6 to 6
Outputs:
- mixed_out: bfloat16 [3, 64, 8192], P(None, 'tensor', 'replica')
- final_state: float32 [64, 128, 64, 128], P('replica', 'tensor')
- final_window_x: float32 [64, 3, 8192], P('replica', None, 'tensor')
- final_window_coeff: float32 [64, 3, 2, 512], P('replica')
The draws below stay inside these ranges and needn't reach their ends.
Inputs may be any that keep to these rules, and one draw needn't show every extreme that they name: On each step, of the 8 rows of one replica (rows of one aligned block of 8), exactly one has its parent on that same replica; two share one parent on another replica; each of the other 5 has its parent on yet another replica, all these replicas distinct. So no other replica holds the parents of more than 2 rows of one replica, nor more than one distinct parent of them. Rows within a block come in any order.
All inputs are finite; a program needn't handle non-finite values.
Results may differ from the reference program's by a relative error of at most 0.005.
Values may be sent and summed in bfloat16 or wider, within the bound.
A program may use at most 192 MiB of HBM per device.

```python
import jax
import jax.numpy as jnp
from jax import lax

D = 8192
P_SIZE = 64
N = 128
K = 4
H = 128
G = 4
ROWS_DEV = 8
STEPS = 3
INNER = 8192
GS = 2048
ROWS = 64


def draw_parents(key, part):
    replicas = ROWS // ROWS_DEV

    def one_block(block_key, dest_replica):
        first_key, second_key, third_key = jax.random.split(block_key, 3)
        offsets = jax.random.permutation(first_key, replicas - 1)[:ROWS_DEV - 2].astype(jnp.int32) + 1
        local_pick = jax.random.randint(second_key, (ROWS_DEV - 1,), 0, ROWS_DEV).astype(jnp.int32)
        source_offset = jnp.concatenate([offsets[:1], offsets, jnp.zeros((1,), jnp.int32)])
        local_row = jnp.concatenate([local_pick[:1], local_pick])
        source = (dest_replica + source_offset) % replicas
        parent_row = source * ROWS_DEV + local_row
        order = jax.random.permutation(third_key, ROWS_DEV)
        return parent_row[order]
    block_keys = jax.random.split(jax.random.fold_in(key, 17), STEPS * replicas)
    dest_list = jnp.tile(jnp.arange(replicas, dtype=jnp.int32), STEPS)
    blocks = jax.vmap(one_block)(block_keys, dest_list)
    return blocks.reshape(STEPS, ROWS).astype(jnp.int32)


def levels(stream_key, extent, shards, least, high):
    gain, own = 1.0, jax.random.fold_in(stream_key, 6)
    for dim, parts in shards:
        heights = jnp.exp(jax.random.uniform(jax.random.fold_in(own, dim), (parts,), jnp.float32, least / len(shards), high / len(shards)))
        gain = gain * jnp.repeat(heights, extent[dim] // parts).reshape([-1 if axis == dim else 1 for axis in range(len(extent))])
    return gain


def bell_draw(stream_key, shape, scale, most, shards=(), held_as=jnp.bfloat16):
    array = scale * jax.random.normal(stream_key, shape, jnp.float32)
    if shards:
        array = array * levels(stream_key, shape, shards, -0.22, 0.18)
    return jnp.clip(array, -most, most).astype(held_as)


def setup_inputs(seed: int = 0) -> dict:
    streams_of = jax.random.split(jax.random.key(seed), 18)
    hidden = bell_draw(streams_of[0], (STEPS, ROWS, D), 1.0, 6.0, ((2, 8),))
    parents = draw_parents(jax.random.fold_in(streams_of[17], 71), 0)
    input_weight = bell_draw(streams_of[2], (D, 2, INNER), D ** -0.5, 0.0625, ((0, 8), (2, 4)))
    coeff_weight = bell_draw(streams_of[3], (D, 2, G * N), D ** -0.5, 0.0625, ((0, 8),))
    step_weight = bell_draw(streams_of[4], (D, H), D ** -0.5, 0.0625, ((0, 8), (1, 4)))
    kernel_x = jnp.clip(jax.random.uniform(streams_of[5], (K, INNER), jnp.float32, -0.5, 0.5) * levels(streams_of[5], (K, INNER), ((1, 4),), -0.4, 0.0), -0.5, 0.5)
    kernel_bias_x = jnp.clip(jax.random.uniform(streams_of[6], (INNER,), jnp.float32, -0.5, 0.5) * levels(streams_of[6], (INNER,), ((0, 4),), -0.4, 0.0), -0.5, 0.5)
    kernel_coeff = jnp.clip(jax.random.uniform(streams_of[7], (K, 2, G * N), jnp.float32, -0.5, 0.5), -0.5, 0.5)
    kernel_bias_coeff = jnp.clip(jax.random.uniform(streams_of[8], (2, G * N), jnp.float32, -0.5, 0.5), -0.5, 0.5)
    step_bias = jnp.clip(-3.0 + 3.0 * jax.random.uniform(streams_of[9], (H,), jnp.float32) ** levels(streams_of[9], (H,), ((0, 4),), -0.2, 0.2), -3.0, 0.0)
    log_rate = jnp.clip(-4.0 + 4.7 * jax.random.uniform(streams_of[10], (H,), jnp.float32) ** levels(streams_of[10], (H,), ((0, 4),), -0.2, 0.2), -4.0, 0.7)
    skip_gain = jnp.clip(0.5 + 1.5 * jax.random.uniform(streams_of[11], (H,), jnp.float32) ** levels(streams_of[11], (H,), ((0, 4),), -0.2, 0.2), 0.5, 2.0)
    norm_gain = jnp.clip(1.0 + 0.18 * jax.random.normal(streams_of[12], (INNER,), jnp.float32), 0.1, 1.9)
    output_weight = bell_draw(streams_of[13], (INNER, D), INNER ** -0.5, 0.0625, ((0, 4), (1, 8)))
    scan_state = bell_draw(streams_of[14], (ROWS, H, P_SIZE, N), 1.0, 6.0, ((0, 8), (1, 4)), jnp.float32)
    window_x = bell_draw(streams_of[15], (ROWS, K - 1, INNER), 1.0, 6.0, ((0, 8), (2, 4)), jnp.float32)
    window_coeff = bell_draw(streams_of[16], (ROWS, K - 1, 2, G * N), 1.0, 6.0, ((0, 8),), jnp.float32)
    return {"hidden": hidden, "parents": parents, "input_weight": input_weight, "coeff_weight": coeff_weight, "step_weight": step_weight, "kernel_x": kernel_x, "kernel_bias_x": kernel_bias_x, "kernel_coeff": kernel_coeff, "kernel_bias_coeff": kernel_bias_coeff, "step_bias": step_bias, "log_rate": log_rate, "skip_gain": skip_gain, "norm_gain": norm_gain, "output_weight": output_weight, "scan_state": scan_state, "window_x": window_x, "window_coeff": window_coeff}


def reference(hidden, parents, input_weight, coeff_weight, step_weight, kernel_x, kernel_bias_x, kernel_coeff, kernel_bias_coeff, step_bias, log_rate, skip_gain, norm_gain, output_weight, scan_state, window_x, window_coeff):
    state = scan_state
    win_x = window_x
    win_coeff = window_coeff
    rate = jnp.exp(log_rate)
    results = []
    for step_index in range(STEPS):
        picks = parents[step_index].astype(jnp.int32)
        state = jnp.take(state, picks, axis=0)
        win_x = jnp.take(win_x, picks, axis=0)
        win_coeff = jnp.take(win_coeff, picks, axis=0)
        step_input = hidden[step_index]
        gate_x = jnp.dot(step_input, input_weight.reshape(D, 2 * INNER), preferred_element_type=jnp.float32).reshape(ROWS, 2, INNER)
        coeffs = jnp.dot(step_input, coeff_weight.reshape(D, 2 * G * N), preferred_element_type=jnp.float32).reshape(ROWS, 2, G * N)
        step_raw = jnp.dot(step_input, step_weight, preferred_element_type=jnp.float32)
        full_x = jnp.concatenate([win_x, gate_x[:, 1][:, None]], axis=1)
        mixed_x = jax.nn.silu(lax.optimization_barrier(jnp.sum(full_x * kernel_x[None], axis=1)) + kernel_bias_x)
        win_x = full_x[:, 1:]
        full_coeff = jnp.concatenate([win_coeff, coeffs[:, None]], axis=1)
        mixed_coeff = jax.nn.silu(lax.optimization_barrier(jnp.sum(full_coeff * kernel_coeff[None], axis=1)) + kernel_bias_coeff)
        win_coeff = full_coeff[:, 1:]
        step_size = jax.nn.softplus(step_raw + step_bias)
        decay = jnp.exp(-rate * step_size)
        heads_x = mixed_x.reshape(ROWS, H, P_SIZE)
        input_b = jnp.repeat(mixed_coeff[:, 0].reshape(ROWS, G, N), H // G, axis=1)
        output_c = jnp.repeat(mixed_coeff[:, 1].reshape(ROWS, G, N), H // G, axis=1)
        state = decay[:, :, None, None] * state + (step_size[:, :, None] * heads_x)[..., None] * input_b[:, :, None, :]
        heads_y = lax.optimization_barrier(jnp.sum(state * output_c[:, :, None, :], axis=-1)) + skip_gain[None, :, None] * heads_x
        flat_y = heads_y.reshape(ROWS, INNER) * jax.nn.silu(gate_x[:, 0])
        grouped = flat_y.reshape(ROWS, H // G, G, P_SIZE)
        scale = lax.rsqrt(lax.optimization_barrier(jnp.sum(grouped * grouped, axis=(1, 3))) / GS + 1e-05)
        normed = ((grouped * scale[:, None, :, None]).reshape(ROWS, INNER) * norm_gain).astype(jnp.bfloat16)
        results.append(jnp.dot(normed, output_weight, preferred_element_type=jnp.float32).astype(jnp.bfloat16))
    return (jnp.stack(results), state, win_x, win_coeff)
```

```python
import functools

import jax
import jax.numpy as jnp
from jax import lax
from jax.experimental import pallas as pl
from jax.experimental.pallas import tpu as pltpu
from jax.sharding import PartitionSpec as P

BF = jnp.bfloat16
F32 = jnp.float32
I32 = jnp.int32
MESH = pl.DeviceIdType.MESH
LANES = 128


def dot(a, b):
    return jnp.dot(a, b, preferred_element_type=F32)


def dot_exact(a, b):
    return jnp.dot(a, b, preferred_element_type=F32, precision=lax.Precision.HIGHEST)


def halves(v):
    high = v.astype(BF)
    return high, (v - high.astype(F32)).astype(BF)


def shift_of(v):
    assert v & (v - 1) == 0
    return v.bit_length() - 1


def phase_caps(chips):
    return (3,) * (chips - 1) + (2, 2)


def place_lists(steps, past):
    wins = [(s, tau) for s in range(steps) for tau in range(past)]
    news = [(s, t) for s in range(steps) for t in range(s + 1)]
    return wins, news


def plan(parents, replicas, past, win_pad):
    steps, rows = parents.shape
    rows_dev = rows // replicas
    chips = replicas // 2
    chip_rows = 2 * rows_dev
    chip_pad = -(-chips // 8) * 8
    width = max(rows, LANES)
    caps = phase_caps(chips)
    total = sum(caps)
    dev_shift, chip_shift = shift_of(rows_dev), shift_of(chip_rows)
    wins, news = place_lists(steps, past)

    def kernel(par_ref, tab_ref, cols_ref):
        z = lax.axis_index("replica") // 2
        lane = lax.broadcasted_iota(I32, (rows, rows), 1)
        sub = lax.broadcasted_iota(I32, (rows, rows), 0)
        eye = lane == sub
        own = lax.broadcasted_iota(I32, (rows, 1), 0)
        anc = {}
        for s in range(steps):
            anc[s, s + 1] = own
            for t in range(s, -1, -1):
                hit = jnp.where(lane == anc[s, t + 1], par_ref[t : t + 1, :], 0)
                anc[s, t] = jnp.sum(hit, axis=1, keepdims=True)
        columns = []
        for s, tau in wins:
            a = anc[s, 0]
            dev = jnp.right_shift(a, dev_shift)
            columns.append(dev * win_pad + tau * rows_dev + (a - dev * rows_dev))
        for s, t in news:
            a = anc[s, t + 1]
            chip = jnp.right_shift(a, chip_shift)
            columns.append(chip * (steps * chip_rows) + t * chip_rows + (a - chip * chip_rows))
        columns += [anc[s, 0] for s in range(steps)]
        at = lax.broadcasted_iota(I32, (rows, LANES), 1)
        table = jnp.zeros((rows, LANES), I32)
        for k, col in enumerate(columns):
            table = jnp.where(at == k, col, table)
        cols_ref[...] = table

        last = anc[steps - 1, 0]
        hit = lane == last
        row_chip = jnp.right_shift(sub, chip_shift)
        up_to = jnp.max(jnp.where(hit, row_chip, -1), axis=0, keepdims=True)
        down_to = jnp.min(jnp.where(hit, row_chip, chips), axis=0, keepdims=True)
        q = lax.broadcasted_iota(I32, (1, rows), 1)
        q_chip = jnp.right_shift(q, chip_shift)
        q_local = q - q_chip * chip_rows
        at_chip = lax.broadcasted_iota(I32, (chip_pad, rows), 0)
        shift_down = (
            lax.broadcasted_iota(I32, (chip_pad, chip_pad), 0)
            == lax.broadcasted_iota(I32, (chip_pad, chip_pad), 1) + 1
        ).astype(F32)
        src_at = lax.broadcasted_iota(I32, (chip_pad, width), 1)

        def route(home, dest):
            have = ((home == at_chip) & (dest > at_chip)).astype(I32)
            beyond = (dest > at_chip).astype(I32)
            loc = jnp.where(home == at_chip, q_local, 0)
            key = dest * rows + (rows - 1 - q)
            key_col = jnp.sum(jnp.where(eye, key, 0), axis=1, keepdims=True)
            ahead = (key_col > key).astype(F32)
            src = jnp.zeros((chip_pad, width), I32)
            off = 0
            for cap in caps:
                rank = dot(have.astype(F32), ahead).astype(I32)
                picked = have * (rank < cap).astype(I32)
                for k in range(cap):
                    chosen = jnp.where(rank == k, picked * loc, 0)
                    v = jnp.sum(chosen, axis=1, keepdims=True)
                    src = jnp.where(src_at == off + k, v, src)
                sent = picked * (1 + chip_rows + off + rank)
                came = dot(shift_down, sent.astype(F32)).astype(I32)
                loc = jnp.where(came > 0, came - 1, loc)
                have = jnp.where(came > 0, beyond, have - picked)
                off += cap
            return src, loc, jnp.max(have)

        up_src, up_loc, up_over = route(q_chip, up_to)
        down_src, down_loc, down_over = route(chips - 1 - q_chip, chips - 1 - down_to)

        def row_of(v, chip):
            index = lax.broadcasted_iota(I32, v.shape, 0)
            return jnp.sum(jnp.where(index == chip, v, 0), axis=0, keepdims=True)

        here_up = row_of(up_loc, z)
        here_down = row_of(down_loc, chips - 1 - z) + total
        code = jnp.where(q_chip == z, q_local, jnp.where(q_chip < z, here_up, here_down))
        code_col = jnp.sum(jnp.where(hit, code, 0), axis=1, keepdims=True)
        code_row = jnp.sum(jnp.where(eye, code_col, 0), axis=0, keepdims=True)
        tab_ref[...] = jnp.zeros(tab_ref.shape, I32)
        tab_ref[0:1, :] = row_of(up_src, z)
        tab_ref[1:2, :] = row_of(down_src, chips - 1 - z)
        tab_ref[2:3, :rows] = code_row
        tab_ref[3:4, :] = jnp.zeros((1, width), I32) + jnp.maximum(up_over, down_over)

    return pl.pallas_call(
        kernel,
        out_shape=(
            jax.ShapeDtypeStruct((8, width), I32),
            jax.ShapeDtypeStruct((rows, LANES), I32),
        ),
        in_specs=[pl.BlockSpec(memory_space=pltpu.VMEM)],
        out_specs=[pl.BlockSpec(memory_space=pltpu.VMEM)] * 2,
        name="plan",
    )(parents)


def engine(tab, cols, proj, small, win, wc, state, kern_x, bias_x, kern_c, bias_c, head_par, gain, w_out, dims):
    steps, past, groups = dims["steps"], dims["past"], dims["groups"]
    replicas, tensors = dims["replicas"], dims["tensors"]
    rows = cols.shape[0]
    rd, _, hc, n = state.shape
    chips = replicas // 2
    cr = 2 * rd
    sr = steps * rows
    blk = steps * cr
    head_dim = dims["head_dim"]
    hh = hc // head_dim
    taps = past + 1
    win_pad = win.shape[0]
    caps = phase_caps(chips)
    offs = [sum(caps[:i]) for i in range(len(caps))]
    total = sum(caps)
    width = w_out.shape[1]
    rt = rows // tensors
    group_channels = tensors * 2 * hc // groups
    wins, news = place_lists(steps, past)
    n_win, n_new = len(wins), len(news)
    tile = min(256, hc)
    n_out = steps + 1 + past
    pairs = [(k, cc) for k in range(1, tensors) for cc in range(2)]
    head_shift, group_shift = shift_of(head_dim), shift_of(groups)

    def kernel(
        tab_ref, cols_ref, proj_ref, small_ref, win_ref, wc_ref, state_ref, kx_ref, bx_ref, kc_ref, bc_ref,
        hp_ref, gain_ref, wout_ref,
        mixed_ref, moved_ref, x_ref, bo_ref, fc_ref,
        p_own, p_sib, s_sib, send_p, send_s, came_p, came_s, gate, t_new, t_c, t_win, t_wc, w_vm,
        stage, bank, swap, *rest,
    ):
        count = len(caps)
        up_send, up_recv = rest[:count], rest[count : 2 * count]
        dn_send, dn_recv = rest[2 * count : 3 * count], rest[3 * count : 4 * count]
        (
            line_w, line_n, xs, lhs, rhs, base, send_b, came_b, squares, came_q, normed, part, came_m,
            away, x_away, fc_own,
            loc_sem, stage_sem, sib_s, sib_r, win_s, win_r, swap_s, swap_r, rs_s, rs_r, ag_s, ag_r,
            rel_s, rel_r, b_s, b_r, q_s, q_r, f_s, f_r, n_s, n_r, m_s, m_r, x_s, x_r, mv_s, mv_r,
            up_s, up_r, dn_s, dn_r,
        ) = rest[4 * count :]
        me = lax.axis_index("replica")
        mt = lax.axis_index("tensor")
        z = me // 2
        c = me % 2
        sib = me + 1 - 2 * c

        def remote(src, dst, s, r, rep, ten=None):
            return pltpu.make_async_remote_copy(
                src_ref=src, dst_ref=dst, send_sem=s, recv_sem=r,
                device_id=(rep, mt if ten is None else ten), device_id_type=MESH,
            )

        barrier = pltpu.get_barrier_semaphore()
        for k in range(1, replicas):
            pl.semaphore_signal(barrier, inc=1, device_id=((me + k) % replicas, mt), device_id_type=MESH)
        for k, cc in pairs:
            pl.semaphore_signal(
                barrier, inc=1, device_id=(z * 2 + cc, (mt + k) % tensors), device_id_type=MESH
            )
        pl.semaphore_wait(barrier, replicas - 1 + len(pairs))

        sends = []

        def go(copy):
            copy.start()
            sends.append(copy)
            return copy

        def half_cols(h):
            return pl.ds(pl.multiple_of(h * hc, hc), hc)

        own_cols = pltpu.make_async_copy(proj_ref.at[:, :, half_cols(c)], p_own, loc_sem.at[0])
        own_cols.start()
        p_x = go(remote(proj_ref.at[:, :, half_cols(1 - c)], p_sib, sib_s.at[0], sib_r.at[0], sib))
        s_x = go(remote(small_ref.at[1 - c], s_sib, sib_s.at[1], sib_r.at[1], sib))
        w_in = pltpu.make_async_copy(wout_ref, w_vm, loc_sem.at[1])

        def stage_in(i, slot):
            return pltpu.make_async_copy(state_ref.at[i], stage.at[slot], stage_sem.at[slot])

        stage_in(0, 0).start()

        win_x = []
        for k in range(1, replicas):
            peer = (me + k) % replicas
            win_x.append(go(remote(win_ref.at[:, half_cols(peer % 2)], t_win.at[me], win_s.at[0, k - 1], win_r.at[0, k - 1], peer)))
            win_x.append(go(remote(wc_ref, t_wc.at[me], win_s.at[1, k - 1], win_r.at[1, k - 1], peer)))
        t_win[me] = win_ref[:, half_cols(c)]
        t_wc[me] = wc_ref[...]

        step_rows = min(hc, 256)

        def convert(i, carry):
            slot = lax.rem(i, 2)

            @pl.when(i + 1 < rd)
            def _():
                stage_in(i + 1, 1 - slot).start()

            stage_in(i, slot).wait()

            def chunk(j, carry):
                at = pl.ds(pl.multiple_of(j * step_rows, step_rows), step_rows)
                bank[c * rd + i, at, :] = stage[slot, c, at, :].astype(BF)
                swap[i, at, :] = stage[slot, 1 - c, at, :].astype(BF)
                return carry

            return lax.fori_loop(0, hc // step_rows, chunk, carry)

        lax.fori_loop(0, rd, convert, 0)
        swap_x = go(remote(swap, bank.at[pl.ds(c * rd, rd)], swap_s, swap_r, sib))
        w_in.start()

        own_cols.wait()
        p_x.wait_recv()
        s_x.wait_recv()

        def chip_sum(b, carry):
            at = pl.ds(pl.multiple_of(b * blk, blk), blk)
            for k in range(2):
                send_p[b, k] = (p_own[k, at, :] + p_sib[k, at, :]).astype(BF)
            send_s[b] = small_ref[c, at, :] + s_sib[at, :]
            return carry

        lax.fori_loop(0, chips, chip_sum, 0)
        rs_x = []
        for d in range(1, chips):
            to = (z + d) % chips
            rep = to * 2 + c
            rs_x.append(go(remote(send_p.at[to], came_p.at[d - 1], rs_s.at[0, d - 1], rs_r.at[0, d - 1], rep)))
            rs_x.append(go(remote(send_s.at[to], came_s.at[d - 1], rs_s.at[1, d - 1], rs_r.at[1, d - 1], rep)))

        gather_rows = min(hc, 128)

        def gather(dst, index, code, sources):
            def chunk(j, carry):
                at = pl.ds(pl.multiple_of(j * gather_rows, gather_rows), gather_rows)
                v = bank[jnp.minimum(code, cr - 1), at, :]
                for ref, off in sources:
                    i = jnp.clip(code - off, 0, ref.shape[0] - 1)
                    v = jnp.where(code >= off, ref[i, at, :], v)
                dst[index, at, :] = v
                return carry

            lax.fori_loop(0, hc // gather_rows, chunk, 0)

        can_up, can_dn = z < chips - 1, z > 0

        def hop(p, sign):
            send, recv, s, r = (up_send, up_recv, up_s, up_r) if sign > 0 else (dn_send, dn_recv, dn_s, dn_r)
            return remote(send[p], recv[p], s.at[p], r.at[p], (me + 2 * sign + replicas) % replicas)

        def arrived(p):
            @pl.when(can_dn)
            def _():
                hop(p, 1).wait_recv()

            @pl.when(can_up)
            def _():
                hop(p, -1).wait_recv()

        def phase(p):
            if p == 0:
                swap_x.wait_recv()
            else:
                arrived(p - 1)
            for row, sign, send, recv, able in ((0, 1, up_send, up_recv, can_up), (1, -1, dn_send, dn_recv, can_dn)):

                @pl.when(able)
                def _(row=row, sign=sign, send=send, recv=recv):
                    sources = [(recv[e], cr + offs[e]) for e in range(p)]
                    for k in range(caps[p]):
                        gather(send[p], k, tab_ref[row, offs[p] + k], sources)
                    hop(p, sign).start()

        phase(0)

        mine = cols_ref[pl.ds(pl.multiple_of(z * cr, cr), cr), :]

        def pick(columns, entries):
            index = jnp.concatenate(columns, axis=0)
            lane = lax.broadcasted_iota(I32, (index.shape[0], entries), 1)
            return jnp.where(index == lane, 1.0, 0.0).astype(F32)

        for x in win_x:
            x.wait_recv()
        pick_w = pick([mine[:, k : k + 1] for k in range(n_win)], replicas * win_pad)
        pick_n = pick([mine[:, n_win + k : n_win + k + 1] for k in range(n_new)], chips * blk)
        pick_wb, pick_nb = pick_w.astype(BF), pick_n.astype(BF)
        line_w[...] = dot(pick_wb, t_win[...].reshape(replicas * win_pad, hc))
        wc_all = t_wc[...].reshape(replicas * win_pad, 2 * n)
        line_wc = dot_exact(pick_w, wc_all)
        all_cols = cols_ref[...]
        far_w = [(s, tau) for s in range(steps) for tau in range(s, past)]
        pick_fw = pick([all_cols[:, s * past + tau : s * past + tau + 1] for s, tau in far_w], replicas * win_pad)
        far_wc = dot_exact(pick_fw, wc_all[:, n:])

        for x in rs_x:
            x.wait_recv()
        at = pl.ds(pl.multiple_of(z * blk, blk), blk)
        for k in range(2):
            v = p_own[k, at, :] + p_sib[k, at, :]
            for d in range(chips - 1):
                v = v + came_p[d, k].astype(F32)
            if k == 0:
                gate[...] = v
            else:
                t_new[z] = v.astype(BF)
        v = send_s[z]
        for d in range(chips - 1):
            v = v + came_s[d]
        t_c[c, z] = v
        ag_x = []
        for d in range(1, chips):
            rep = ((z + d) % chips) * 2 + c
            ag_x.append(go(remote(t_c.at[c, z], t_c.at[c, z], ag_s.at[0, d - 1], ag_r.at[0, d - 1], rep)))
        for d in range(1, chips):
            rep = ((z + d) % chips) * 2 + c
            ag_x.append(go(remote(t_new.at[z], t_new.at[z], ag_s.at[1, d - 1], ag_r.at[1, d - 1], rep)))

        phase(1)

        def landed(which, d):
            src = (z + chips - d) % chips
            ref = t_c.at[c, src] if which == 0 else t_new.at[src]
            return remote(ref, ref, ag_s.at[which, d - 1], ag_r.at[which, d - 1], src * 2 + c)

        for d in range(1, chips):
            landed(0, d).wait_recv()
        relay_c = go(remote(t_c.at[c], t_c.at[c], rel_s.at[0], rel_r.at[0], sib))
        remote(t_c.at[1 - c], t_c.at[1 - c], rel_s.at[0], rel_r.at[0], sib).wait_recv()

        kc = kc_ref[...]
        bc = bc_ref[...]
        b_new = t_c[0].reshape(chips * blk, -1)
        c_new = t_c[1].reshape(chips * blk, -1)
        raw_new = t_c[c].reshape(chips * blk, -1)
        far_n = [(s, t) for s in range(steps) for t in range(max(0, s - past), s + 1)]
        pick_fn = pick([all_cols[:, n_win + news.index(st) : n_win + news.index(st) + 1] for st in far_n], chips * blk)
        far_nc = dot_exact(pick_fn, c_new[:, :n])
        out_c = []
        for s in range(steps):
            tot = bc[:, n:]
            for j in range(taps):
                tau = s + j
                if tau < past:
                    k = far_w.index((s, tau))
                    v = far_wc[k * rows : (k + 1) * rows]
                else:
                    k = far_n.index((s, tau - past))
                    v = far_nc[k * rows : (k + 1) * rows]
                tot = tot + v * kc[j : j + 1, n:]
            out_c.append(jax.nn.silu(tot))
        c_all = jnp.concatenate(out_c, axis=0)
        c_hi, c_lo = halves(c_all)
        home = jnp.concatenate([all_cols[:, n_win + n_new + s : n_win + n_new + s + 1] for s in range(steps)], axis=0)
        zero = jnp.zeros_like(c_hi)
        for q in range(cr):
            here = home == z * cr + q
            lhs[:sr, q * n : (q + 1) * n] = jnp.where(here, c_hi, zero)
            lhs[sr:, q * n : (q + 1) * n] = jnp.where(here, c_lo, zero)

        def base_tile(j, carry):
            at = pl.ds(pl.multiple_of(j * tile, tile), tile)
            for q in range(cr):
                rhs[:, q * n : (q + 1) * n] = bank[q, at, :]
            got = lax.dot_general(lhs[...], rhs[...], (((1,), (1,)), ((), ())), preferred_element_type=F32)
            got = got[:sr] + got[sr:]
            for s in range(steps):
                for b in range(chips):
                    base[b, s * cr : (s + 1) * cr, at] = got[s * rows + b * cr : s * rows + (b + 1) * cr]
            return carry

        lax.fori_loop(0, hc // tile, base_tile, 0)
        send_b[...] = base[...].astype(BF)
        b_x = []
        for d in range(1, chips):
            to = (z + d) % chips
            b_x.append(go(remote(send_b.at[to], came_b.at[d - 1], b_s.at[d - 1], b_r.at[d - 1], to * 2 + c)))

        phase(2)

        line_nb = dot_exact(pick_n, b_new[:, :n])
        line_nc = dot_exact(pick_n, c_new[:, :n])
        line_nr = dot_exact(pick_n, raw_new[:, n:])

        def coeff_line(s, tau, part_of):
            if tau < past:
                k = wins.index((s, tau))
                return line_wc[k * cr : (k + 1) * cr, part_of * n : (part_of + 1) * n]
            k = news.index((s, tau - past))
            return (line_nb, line_nc)[part_of][k * cr : (k + 1) * cr]

        def coeff(s, t, part_of):
            tot = bc[:, part_of * n : (part_of + 1) * n]
            for j in range(taps):
                tot = tot + coeff_line(s, t + j, part_of) * kc[j : j + 1, part_of * n : (part_of + 1) * n]
            return jax.nn.silu(tot)

        hp = hp_ref[c]
        rate = jnp.exp(hp[1:2])
        expand_in, final_w = [], []
        b_last = None
        for s in range(steps):
            c_now = coeff(s, s, 1)
            fade = jnp.ones((cr, LANES), F32)
            scaled, weights, bs = [None] * (s + 1), [None] * (s + 1), [None] * (s + 1)
            for t in range(s, -1, -1):
                k = news.index((s, t))
                v = line_nr[k * cr : (k + 1) * cr] + hp[0:1]
                size = jnp.maximum(v, 0.0) + jnp.log1p(jnp.exp(-jnp.abs(v)))
                weights[t] = fade * size
                bs[t] = coeff(s, t, 0)
                scaled[t] = weights[t] * jnp.sum(bs[t] * c_now, axis=1, keepdims=True)
                fade = fade * jnp.exp(-rate * size)
            expand_in += [fade] + scaled
            if s == steps - 1:
                final_w, b_last = weights, bs
        expand_in += final_w
        n_exp = len(expand_in)
        expand_in.append(jnp.broadcast_to(hp[2:3], (8, LANES)))
        spread = (
            lax.broadcasted_iota(I32, (LANES, hc), 0)
            == jnp.right_shift(lax.broadcasted_iota(I32, (LANES, hc), 1), head_shift)
        ).astype(F32)
        wide = dot_exact(jnp.concatenate(expand_in, axis=0), spread)
        wides = [wide[k * cr : (k + 1) * cr] for k in range(n_exp)]
        skip = wide[n_exp * cr : n_exp * cr + 1]

        for d in range(1, chips):
            landed(1, d).wait_recv()
        line_n[...] = dot(pick_nb, t_new[...].reshape(chips * blk, hc))

        def x_line(s, tau):
            if tau < past:
                k = wins.index((s, tau))
                return line_w[k * cr : (k + 1) * cr, :]
            k = news.index((s, tau - past))
            return line_n[k * cr : (k + 1) * cr, :]

        kx_own = kx_ref[:, half_cols(c)]
        bx_own = bx_ref[:, half_cols(c)]
        for k, (s, t) in enumerate(news):
            tot = bx_own
            for j in range(taps):
                tot = tot + x_line(s, t + j) * kx_own[j : j + 1]
            xs[k] = jax.nn.silu(tot)

        last = steps - 1
        outs = [wides[n_exp - steps + t] * xs[news.index((last, t))] for t in range(steps)]
        outs.append(wides[n_exp - steps - (last + 1) - 1])
        outs += [x_line(last, steps + j) for j in range(past)]

        @pl.when(c == 0)
        def _():
            for k, v in enumerate(outs):
                x_ref[0, k] = v[:rd]
                x_away[k] = v[rd:]
            for t in range(steps):
                bo_ref[t] = b_last[t][:rd]
            for j in range(past):
                for part_of in range(2):
                    fc_own[j * rd : (j + 1) * rd, part_of * n : (part_of + 1) * n] = coeff_line(last, steps + j, part_of)[:rd]

        @pl.when(c == 1)
        def _():
            for k, v in enumerate(outs):
                x_ref[1, k] = v[rd:]
                x_away[k] = v[:rd]
            for t in range(steps):
                bo_ref[t] = b_last[t][rd:]
            for j in range(past):
                for part_of in range(2):
                    fc_own[j * rd : (j + 1) * rd, part_of * n : (part_of + 1) * n] = coeff_line(last, steps + j, part_of)[rd:]

        x_x = go(remote(x_away, x_ref.at[c], x_s, x_r, sib))
        fc_ref[mt] = fc_own[...]
        f_x = [
            go(remote(fc_own, fc_ref.at[mt], f_s.at[k - 1], f_r.at[k - 1], me, (mt + k) % tensors))
            for k in range(1, tensors)
        ]

        for x in b_x:
            x.wait_recv()
        own_base = base[z]
        for d in range(chips - 1):
            own_base = own_base + came_b[d].astype(F32)
        ys = []
        e = 0
        for s in range(steps):
            y = wides[e] * own_base[s * cr : (s + 1) * cr] + skip * xs[news.index((s, s))]
            for t in range(s + 1):
                y = y + wides[e + 1 + t] * xs[news.index((s, t))]
            e += s + 2
            ys.append(y * jax.nn.silu(gate[s * cr : (s + 1) * cr, :]))
        y = jnp.concatenate(ys, axis=0)
        first_head = mt * (2 * hh) + c * hh
        col_head = first_head + jnp.right_shift(lax.broadcasted_iota(I32, (LANES, hc), 1), head_shift)
        col_group = col_head - jnp.left_shift(jnp.right_shift(col_head, group_shift), group_shift)
        member = (lax.broadcasted_iota(I32, (LANES, hc), 0) == col_group).astype(F32)
        own_sq = lax.dot_general(
            y * y, member, (((1,), (1,)), ((), ())), preferred_element_type=F32, precision=lax.Precision.HIGHEST
        )
        squares[...] = own_sq
        q_x = [go(remote(squares, came_q.at[0], q_s.at[0], q_r.at[0], sib))]
        for i, (k, cc) in enumerate(pairs):
            slot = 1 + (k - 1) * 2 + lax.rem(cc + c, 2)
            dst = 1 + (k - 1) * 2 + lax.rem(cc + c, 2)
            q_x.append(go(remote(squares, came_q.at[dst], q_s.at[slot], q_r.at[slot], z * 2 + cc, (mt + k) % tensors)))

        phase(3)

        for x in q_x:
            x.wait_recv()
        tot = squares[...]
        for i in range(1 + len(pairs)):
            tot = tot + came_q[i]
        inverse = lax.rsqrt(tot / group_channels + 1e-05)
        normed[c, z] = (y * dot_exact(inverse, member) * gain_ref[:, half_cols(c)]).astype(BF)
        n_x = []
        for d in range(1, chips):
            rep = ((z + d) % chips) * 2 + c
            n_x.append(go(remote(normed.at[c, z], normed.at[c, z], n_s.at[d - 1], n_r.at[d - 1], rep)))

        for p in range(4, count):
            phase(p)

        for d in range(1, chips):
            src = (z + chips - d) % chips
            remote(normed.at[c, src], normed.at[c, src], n_s.at[d - 1], n_r.at[d - 1], src * 2 + c).wait_recv()
        go(remote(normed.at[c], normed.at[c], rel_s.at[1], rel_r.at[1], sib))
        remote(normed.at[1 - c], normed.at[1 - c], rel_s.at[1], rel_r.at[1], sib).wait_recv()

        w_in.wait()
        out_tile = min(512, width)
        left = normed[0].reshape(chips * blk, hc)
        right = normed[1].reshape(chips * blk, hc)

        def project(j, carry):
            at = pl.ds(pl.multiple_of(j * out_tile, out_tile), out_tile)
            got = dot(left, w_vm[:hc, at]) + dot(right, w_vm[hc:, at])
            part[:, :, :, at] = got.reshape(chips, steps, cr, out_tile)
            return carry

        lax.fori_loop(0, width // out_tile, project, 0)

        def share(t):
            first = t * rt
            return part.at[first // cr, :, pl.ds(pl.multiple_of(first % cr, 8), rt), :]

        m_x = []
        for k in range(1, tensors):
            to = (mt + k) % tensors
            m_x.append(go(remote(share(to), came_m.at[k - 1], m_s.at[k - 1], m_r.at[k - 1], me, to)))

        arrived(count - 1)
        sources = [(up_recv[e], cr + offs[e]) for e in range(count)]
        sources += [(dn_recv[e], cr + total + offs[e]) for e in range(count)]

        def final_row(i, carry):
            gather(moved_ref.at[:, c], i, tab_ref[2, z * cr + c * rd + i], sources)
            gather(away, i, tab_ref[2, z * cr + (1 - c) * rd + i], sources)
            return carry

        lax.fori_loop(0, rd, final_row, 0)
        mv_x = go(remote(away, moved_ref.at[:, c], mv_s, mv_r, sib))

        for x in m_x:
            x.wait_recv()
        first = mt * rt
        tot = part[first // cr, :, pl.ds(pl.multiple_of(first % cr, 8), rt), :]
        for k in range(tensors - 1):
            tot = tot + came_m[k]
        mixed_ref[...] = tot.astype(BF)

        remote(x_away, x_ref.at[1 - c], x_s, x_r, sib).wait_recv()
        for k in range(1, tensors):
            src = (mt + tensors - k) % tensors
            remote(fc_own, fc_ref.at[src], f_s.at[k - 1], f_r.at[k - 1], me, src).wait_recv()
        remote(away, moved_ref.at[:, 1 - c], mv_s, mv_r, sib).wait_recv()
        for x in sends:
            x.wait_send()
        for p in range(count):

            @pl.when(can_up)
            def _(p=p):
                hop(p, 1).wait_send()

            @pl.when(can_dn)
            def _(p=p):
                hop(p, -1).wait_send()

    def vm(*shape, dtype=F32):
        return pltpu.VMEM(shape, dtype)

    def sem(*shape):
        return pltpu.SemaphoreType.DMA(shape) if shape else pltpu.SemaphoreType.DMA

    slots = [vm(cap, hc, n, dtype=BF) for cap in caps]
    few = chips - 1
    scratch = [
        vm(2, sr, hc), vm(2, sr, hc), vm(sr, small.shape[2]), vm(chips, 2, blk, hc, dtype=BF),
        vm(chips, blk, small.shape[2]), vm(few, 2, blk, hc, dtype=BF), vm(few, blk, small.shape[2]),
        vm(blk, hc), vm(chips, blk, hc, dtype=BF), vm(2, chips, blk, small.shape[2]),
        vm(replicas, win_pad, hc, dtype=BF), vm(replicas, win_pad, 2 * n), vm(*w_out.shape, dtype=BF),
        vm(2, 2, hc, n), vm(cr, hc, n, dtype=BF), vm(rd, hc, n, dtype=BF),
        *slots, *slots, *slots, *slots,
        vm(n_win * cr, hc), vm(n_new * cr, hc), vm(n_new, cr, hc),
        vm(2 * sr, cr * n, dtype=BF), vm(tile, cr * n, dtype=BF),
        vm(chips, blk, hc), vm(chips, blk, hc, dtype=BF), vm(few, blk, hc, dtype=BF),
        vm(blk, LANES), vm(1 + len(pairs), blk, LANES), vm(2, chips, blk, hc, dtype=BF),
        vm(chips, steps, cr, width), vm(tensors - 1, steps, rt, width),
        vm(rd, hc, n, dtype=BF), vm(n_out, rd, hc), vm(past * rd, 2 * n),
        sem(2), sem(2), sem(2), sem(2), sem(2, replicas - 1), sem(2, replicas - 1), sem(), sem(),
        sem(2, few), sem(2, few), sem(2, few), sem(2, few), sem(2), sem(2), sem(few), sem(few),
        sem(1 + len(pairs)), sem(1 + len(pairs)), sem(tensors - 1), sem(tensors - 1), sem(few), sem(few),
        sem(tensors - 1), sem(tensors - 1), sem(), sem(), sem(), sem(),
        sem(len(caps)), sem(len(caps)), sem(len(caps)), sem(len(caps)),
    ]
    in_vm = pl.BlockSpec(memory_space=pltpu.VMEM)
    in_any = pl.BlockSpec(memory_space=pl.ANY)
    return pl.pallas_call(
        kernel,
        out_shape=(
            jax.ShapeDtypeStruct((steps, rt, width), BF),
            jax.ShapeDtypeStruct((rd, 2, hc, n), BF),
            jax.ShapeDtypeStruct((2, n_out, rd, hc), F32),
            jax.ShapeDtypeStruct((steps, rd, n), F32),
            jax.ShapeDtypeStruct((tensors, past * rd, 2 * n), F32),
        ),
        in_specs=[pl.BlockSpec(memory_space=pltpu.SMEM), in_vm, in_any, in_vm, in_vm, in_vm, in_any]
        + [in_vm] * 6
        + [in_any],
        out_specs=[in_vm] * 5,
        scratch_shapes=scratch,
        compiler_params=pltpu.CompilerParams(
            collective_id=0, has_side_effects=True, vmem_limit_bytes=60 * 1024 * 1024
        ),
        name="engine",
    )(tab, cols, proj, small, win, wc, state, kern_x, bias_x, kern_c, bias_c, head_par, gain, w_out)


def fetch(every, index):
    count = index.shape[0]

    def kernel(index_ref, every_ref, out_ref, sems):
        for i in range(count):
            pltpu.make_async_copy(every_ref.at[index_ref[i]], out_ref.at[i], sems.at[i]).start()
        for i in range(count):
            pltpu.make_async_copy(every_ref.at[0], out_ref.at[i], sems.at[i]).wait()

    return pl.pallas_call(
        kernel,
        out_shape=jax.ShapeDtypeStruct((count,) + every.shape[1:], every.dtype),
        in_specs=[pl.BlockSpec(memory_space=pltpu.SMEM), pl.BlockSpec(memory_space=pl.ANY)],
        out_specs=pl.BlockSpec(memory_space=pltpu.VMEM),
        scratch_shapes=[pltpu.SemaphoreType.DMA((count,))],
        name="fetch",
    )(index, every)


def local(
    hidden,
    parents,
    input_weight,
    coeff_weight,
    step_weight,
    kernel_x,
    kernel_bias_x,
    kernel_coeff,
    kernel_bias_coeff,
    step_bias,
    log_rate,
    skip_gain,
    norm_gain,
    output_weight,
    scan_state,
    window_x,
    window_coeff,
):
    rows_dev, heads, head_dim, n = scan_state.shape
    steps, rows, depth = hidden.shape
    taps = kernel_x.shape[0]
    past = taps - 1
    chans = heads * head_dim
    half = chans // 2
    replicas = lax.axis_size("replica")
    tensors = lax.axis_size("tensor")
    chips = replicas // 2
    chip_rows = 2 * rows_dev
    me = lax.axis_index("replica")
    mt = lax.axis_index("tensor")
    heads_all = heads * tensors
    groups = kernel_bias_coeff.shape[1] // n
    my_group = mt * heads * groups // heads_all
    coeff_at = my_group * n
    win_rows = past * rows_dev
    win_pad = -(-win_rows // 16) * 16

    def own_group(v):
        return lax.dynamic_slice_in_dim(v, coeff_at, n, axis=v.ndim - 1)

    tab, cols = plan(parents.astype(I32), replicas, past, win_pad)

    win = window_x.transpose(1, 0, 2).reshape(win_rows, chans).astype(BF)
    win = jnp.pad(win, ((0, win_pad - win_rows), (0, 0)))
    wc = own_group(window_coeff).transpose(1, 0, 2, 3).reshape(win_rows, 2 * n)
    wc = jnp.pad(wc, ((0, win_pad - win_rows), (0, 0)))

    h = hidden.reshape(steps, chips, chip_rows, depth).transpose(1, 0, 2, 3)
    h = h.reshape(steps * rows, depth)
    proj = jnp.einsum("rd,dkc->krc", h, input_weight, preferred_element_type=F32)
    cw = own_group(coeff_weight)
    pad = jnp.zeros((depth, LANES - heads // 2), BF)
    small_w = jnp.concatenate(
        [cw[:, 0], step_weight[:, : heads // 2], pad, cw[:, 1], step_weight[:, heads // 2 :], pad], axis=1
    )
    small = dot(h, small_w).reshape(steps * rows, 2, n + LANES).transpose(1, 0, 2)

    kern_c = own_group(kernel_coeff).reshape(taps, 2 * n)
    bias_c = own_group(kernel_bias_coeff).reshape(1, 2 * n)
    head_par = jnp.stack([step_bias, log_rate, skip_gain]).reshape(3, 2, heads // 2).transpose(1, 0, 2)
    head_par = jnp.pad(head_par, ((0, 0), (0, 5), (0, LANES - heads // 2)))

    mixed, moved, x_out, b_out, fc = engine(
        tab, cols, proj, small, win, wc, scan_state.reshape(rows_dev, 2, half, n), kernel_x,
        kernel_bias_x.reshape(1, chans), kern_c, bias_c, head_par, norm_gain.reshape(1, chans), output_weight,
        dict(steps=steps, past=past, groups=groups, replicas=replicas, tensors=tensors, head_dim=head_dim),
    )
    mixed = mixed.reshape(steps, rows // tensors, -1)

    def finish(rows_of):
        final = x_out[:, steps].transpose(1, 0, 2)[..., None] * rows_of.astype(F32)
        for t in range(steps):
            final = final + x_out[:, t].transpose(1, 0, 2)[..., None] * b_out[t][:, None, None, :]
        return final.reshape(rows_dev, heads, head_dim, n)

    def slow():
        every = lax.all_gather(scan_state.astype(BF).reshape(rows_dev, 2, half, n), "replica", axis=0, tiled=True)
        first = jnp.arange(rows, dtype=I32)
        for s in range(steps - 1, -1, -1):
            first = jnp.take(parents[s], first)
        return finish(fetch(every, lax.dynamic_slice_in_dim(first, me * rows_dev, rows_dev)))

    final = lax.cond(tab[3, 0] > 0, slow, lambda: finish(moved))
    final_x = x_out[:, steps + 1 :].transpose(2, 1, 0, 3).reshape(rows_dev, past, chans)
    final_c = fc.reshape(groups, tensors // groups, past, rows_dev, 2, n)[:, 0]
    final_c = final_c.transpose(2, 1, 3, 0, 4).reshape(rows_dev, past, 2, groups * n)
    return (mixed, final, final_x, final_c)


def solution(mesh):
    placed = (
        P(None, None, "replica"),
        P(),
        P("replica", None, "tensor"),
        P("replica", None, None),
        P("replica", "tensor"),
        P(None, "tensor"),
        P("tensor"),
        P(),
        P(),
        P("tensor"),
        P("tensor"),
        P("tensor"),
        P("tensor"),
        P("tensor", "replica"),
        P("replica", "tensor", None, None),
        P("replica", None, "tensor"),
        P("replica", None, None, None),
    )
    return jax.shard_map(
        local,
        mesh=mesh,
        in_specs=placed,
        out_specs=(
            P(None, "tensor", "replica"),
            P("replica", "tensor", None, None),
            P("replica", None, "tensor"),
            P("replica", None, None, None),
        ),
        check_vma=False,
    )
```

```python
import functools

import jax
import jax.numpy as jnp
from jax import lax
from jax.experimental import pallas as pl
from jax.experimental.pallas import tpu as pltpu
from jax.sharding import PartitionSpec as P

BF = jnp.bfloat16
F32 = jnp.float32
I32 = jnp.int32
MESH = pl.DeviceIdType.MESH
LANES = 128


def dot(a, b):
    return jnp.dot(a, b, preferred_element_type=F32)


def dot_exact(a, b):
    return jnp.dot(a, b, preferred_element_type=F32, precision=lax.Precision.HIGHEST)


def halves(v):
    high = v.astype(BF)
    return high, (v - high.astype(F32)).astype(BF)


def shift_of(v):
    assert v & (v - 1) == 0
    return v.bit_length() - 1


def phase_caps(chips):
    return (2, 2, 2, 2, 2, 2)


def place_lists(steps, past):
    wins = [(s, tau) for s in range(steps) for tau in range(past)]
    news = [(s, t) for s in range(steps) for t in range(s + 1)]
    return wins, news


def plan(parents, replicas, past):
    steps, rows = parents.shape
    rows_dev = rows // replicas
    chips = replicas // 2
    chip_rows = 2 * rows_dev
    chip_pad = -(-chips // 8) * 8
    width = max(rows, LANES)
    caps = phase_caps(chips)
    total = sum(caps)
    dev_shift, chip_shift = shift_of(rows_dev), shift_of(chip_rows)
    wins, news = place_lists(steps, past)

    def kernel(par_ref, tab_ref, cols_ref):
        z = lax.axis_index("replica") // 2
        lane = lax.broadcasted_iota(I32, (rows, rows), 1)
        sub = lax.broadcasted_iota(I32, (rows, rows), 0)
        eye = lane == sub
        own = lax.broadcasted_iota(I32, (rows, 1), 0)
        anc = {}
        for s in range(steps):
            anc[s, s + 1] = own
            for t in range(s, -1, -1):
                hit = jnp.where(lane == anc[s, t + 1], par_ref[t : t + 1, :], 0)
                anc[s, t] = jnp.sum(hit, axis=1, keepdims=True)
        columns = []
        for s, tau in wins:
            a = anc[s, 0]
            dev = jnp.right_shift(a, dev_shift)
            columns.append(dev * (past * rows_dev) + tau * rows_dev + (a - dev * rows_dev))
        for s, t in news:
            a = anc[s, t + 1]
            chip = jnp.right_shift(a, chip_shift)
            columns.append(chip * (steps * chip_rows) + t * chip_rows + (a - chip * chip_rows))
        columns += [anc[s, 0] for s in range(steps)]
        at = lax.broadcasted_iota(I32, (rows, LANES), 1)
        table = jnp.zeros((rows, LANES), I32)
        for k, col in enumerate(columns):
            table = jnp.where(at == k, col, table)
        cols_ref[...] = table

        last = anc[steps - 1, 0]
        hit = lane == last
        row_chip = jnp.right_shift(sub, chip_shift)
        up_to = jnp.max(jnp.where(hit, row_chip, -1), axis=0, keepdims=True)
        down_to = jnp.min(jnp.where(hit, row_chip, chips), axis=0, keepdims=True)
        q = lax.broadcasted_iota(I32, (1, rows), 1)
        q_chip = jnp.right_shift(q, chip_shift)
        q_local = q - q_chip * chip_rows
        at_chip = lax.broadcasted_iota(I32, (chip_pad, rows), 0)
        shift_down = (
            lax.broadcasted_iota(I32, (chip_pad, chip_pad), 0)
            == lax.broadcasted_iota(I32, (chip_pad, chip_pad), 1) + 1
        ).astype(F32)
        src_at = lax.broadcasted_iota(I32, (chip_pad, width), 1)

        def route(home, dest):
            have = ((home == at_chip) & (dest > at_chip)).astype(I32)
            beyond = (dest > at_chip).astype(I32)
            loc = jnp.where(home == at_chip, q_local, 0)
            key = dest * rows + (rows - 1 - q)
            key_col = jnp.sum(jnp.where(eye, key, 0), axis=1, keepdims=True)
            ahead = (key_col > key).astype(F32)
            src = jnp.zeros((chip_pad, width), I32)
            off = 0
            for cap in caps:
                rank = dot(have.astype(F32), ahead).astype(I32)
                picked = have * (rank < cap).astype(I32)
                for k in range(cap):
                    chosen = jnp.where(rank == k, picked * loc, 0)
                    v = jnp.sum(chosen, axis=1, keepdims=True)
                    src = jnp.where(src_at == off + k, v, src)
                sent = picked * (1 + chip_rows + off + rank)
                came = dot(shift_down, sent.astype(F32)).astype(I32)
                loc = jnp.where(came > 0, came - 1, loc)
                have = jnp.where(came > 0, beyond, have - picked)
                off += cap
            return src, loc, jnp.max(have)

        up_src, up_loc, up_over = route(q_chip, up_to)
        down_src, down_loc, down_over = route(chips - 1 - q_chip, chips - 1 - down_to)

        def row_of(v, chip):
            index = lax.broadcasted_iota(I32, v.shape, 0)
            return jnp.sum(jnp.where(index == chip, v, 0), axis=0, keepdims=True)

        here_up = row_of(up_loc, z)
        here_down = row_of(down_loc, chips - 1 - z) + total
        code = jnp.where(q_chip == z, q_local, jnp.where(q_chip < z, here_up, here_down))
        code_col = jnp.sum(jnp.where(hit, code, 0), axis=1, keepdims=True)
        code_row = jnp.sum(jnp.where(eye, code_col, 0), axis=0, keepdims=True)
        tab_ref[...] = jnp.zeros(tab_ref.shape, I32)
        tab_ref[0:1, :] = row_of(up_src, z)
        tab_ref[1:2, :] = row_of(down_src, chips - 1 - z)
        tab_ref[2:3, :rows] = code_row
        tab_ref[3:4, :] = jnp.zeros((1, width), I32) + jnp.maximum(up_over, down_over)

    return pl.pallas_call(
        kernel,
        out_shape=(
            jax.ShapeDtypeStruct((8, width), I32),
            jax.ShapeDtypeStruct((rows, LANES), I32),
        ),
        in_specs=[pl.BlockSpec(memory_space=pltpu.VMEM)],
        out_specs=[pl.BlockSpec(memory_space=pltpu.VMEM)] * 2,
        name="plan",
    )(parents)


def engine(tab, cols, proj, small, win, wc, state, kern_x, bias_x, kern_c, bias_c, head_par, gain, w_out, dims):
    steps, past, groups = dims["steps"], dims["past"], dims["groups"]
    replicas, tensors = dims["replicas"], dims["tensors"]
    rows = cols.shape[0]
    rd, _, hc, n = state.shape
    chips = replicas // 2
    cr = 2 * rd
    sr = steps * rows
    blk = steps * cr
    head_dim = dims["head_dim"]
    hh = hc // head_dim
    taps = past + 1
    win_pad, win_rows = win.shape[0], past * rd
    win_blk = 2 * win_rows
    caps = phase_caps(chips)
    offs = [sum(caps[:i]) for i in range(len(caps))]
    total = sum(caps)
    width = w_out.shape[1]
    rt = rows // tensors
    group_channels = tensors * 2 * hc // groups
    wins, news = place_lists(steps, past)
    n_win, n_new = len(wins), len(news)
    tile = min(256, hc)
    n_out = steps + 1 + past
    pairs = [(k, cc) for k in range(1, tensors) for cc in range(2)]
    head_shift, group_shift = shift_of(head_dim), shift_of(groups)

    def kernel(
        tab_ref, cols_ref, proj_ref, small_ref, win_ref, wc_ref, state_ref, kx_ref, bx_ref, kc_ref, bc_ref,
        hp_ref, gain_ref, wout_ref,
        mixed_ref, moved_ref, x_ref, bo_ref, fc_ref,
        p_own, p_sib, s_sib, send_p, send_s, came_p, came_s, gate, t_new, t_c, w_sib, wc_sib, t_win, t_wc,
        w_vm, stage, bank, swap, *rest,
    ):
        count = len(caps)
        slots = [[[rest[(k * count + p) * 2 + h] for h in range(2)] for p in range(count)] for k in range(4)]
        up_send, up_recv, dn_send, dn_recv = slots
        (
            line_w, line_n, xs, lhs, rhs, base, out_b, came_b, own_b, squares, came_q, normed, part, came_m,
            away, x_away, fc_own,
            loc_sem, stage_sem, sib_s, sib_r, win_s, win_r, swap_s, swap_r, rs_s, rs_r, ag_s, ag_r,
            rel_s, rel_r, b_s, b_r, q_s, q_r, f_s, f_r, n_s, n_r, m_s, m_r, x_s, x_r, mv_s, mv_r,
            up_s, up_r, dn_s, dn_r,
        ) = rest[8 * count :]
        me = lax.axis_index("replica")
        mt = lax.axis_index("tensor")
        z = me // 2
        c = me % 2
        sib = me + 1 - 2 * c

        def remote(src, dst, s, r, rep, ten=None):
            return pltpu.make_async_remote_copy(
                src_ref=src, dst_ref=dst, send_sem=s, recv_sem=r,
                device_id=(rep, mt if ten is None else ten), device_id_type=MESH,
            )

        barrier = pltpu.get_barrier_semaphore()
        for k in range(1, replicas):
            pl.semaphore_signal(barrier, inc=1, device_id=((me + k) % replicas, mt), device_id_type=MESH)
        for k, cc in pairs:
            pl.semaphore_signal(
                barrier, inc=1, device_id=(z * 2 + cc, (mt + k) % tensors), device_id_type=MESH
            )
        pl.semaphore_wait(barrier, replicas - 1 + len(pairs))

        sends = []

        def go(copy):
            copy.start()
            sends.append(copy)
            return copy

        ends = []

        class Spread:
            def __init__(self, blocks, s, r):
                self.blocks, self.s, self.r = blocks, s, r
                ends.append(self.drain)

            def copy(self, i, way, j, b):
                ref = self.blocks[i](b)
                rep = (me + (2 if way == 0 else replicas - 2)) % replicas
                return remote(ref, ref, self.s.at[i, way, j], self.r.at[i, way, j], rep)

            def each(self, j, what, sending):
                for i in range(len(self.blocks)):
                    for way in range(2):
                        if sending:
                            b = z - j if way == 0 else z + j
                            able = (b >= 0) & (z < chips - 1) if way == 0 else (b < chips) & (z > 0)
                        else:
                            b = z - 1 - j if way == 0 else z + 1 + j
                            able = b >= 0 if way == 0 else b < chips

                        @pl.when(able)
                        def _(i=i, way=way, b=b):
                            getattr(self.copy(i, way, j, b), what)()

            def step(self, j):
                if j > 0:
                    self.each(j - 1, "wait_recv", False)
                if j < chips - 1:
                    self.each(j, "start", True)

            def drain(self):
                for j in range(chips - 1):
                    self.each(j, "wait_send", True)

        def half_cols(h):
            return pl.ds(pl.multiple_of(h * hc, hc), hc)

        own_cols = pltpu.make_async_copy(proj_ref.at[:, :, half_cols(c)], p_own, loc_sem.at[0])
        own_cols.start()
        s_x = go(remote(small_ref.at[1 - c], s_sib, sib_s.at[1], sib_r.at[1], sib))
        other = pl.ds(pl.multiple_of((1 - c) * n, n), n)
        w_x = go(remote(win_ref.at[:, half_cols(1 - c)], w_sib, sib_s.at[2], sib_r.at[2], sib))
        wc_x = go(remote(wc_ref.at[:, other], wc_sib, sib_s.at[3], sib_r.at[3], sib))
        p_x = go(remote(proj_ref.at[:, :, half_cols(1 - c)], p_sib, sib_s.at[0], sib_r.at[0], sib))
        w_in = pltpu.make_async_copy(wout_ref, w_vm, loc_sem.at[1])

        def stage_in(i, slot):
            return pltpu.make_async_copy(state_ref.at[i], stage.at[slot], stage_sem.at[slot])

        stage_in(0, 0).start()

        s_x.wait_recv()
        send_s[...] = (small_ref[c] + s_sib[...]).reshape(send_s.shape)

        def around(d):
            return (z + d) % chips

        rs_x, p_sent = [], ([], [])
        for d in range(1, chips):
            rep = around(d) * 2 + c
            rs_x.append(go(remote(send_s.at[around(d)], came_s.at[d - 1], rs_s.at[2, d - 1], rs_r.at[2, d - 1], rep)))

        w_x.wait_recv()
        wc_x.wait_recv()

        def in_order(own, sibling):
            return jnp.where(c == 0, jnp.concatenate([own, sibling]), jnp.concatenate([sibling, own]))

        t_win[z] = in_order(win_ref[:win_rows, half_cols(c)].astype(F32), w_sib[:win_rows].astype(F32)).astype(BF)
        t_wc[c, z] = in_order(wc_ref[:, pl.ds(pl.multiple_of(c * n, n), n)], wc_sib[...])
        windows = Spread([lambda b: t_win.at[b], lambda b: t_wc.at[c, b]], win_s, win_r)
        windows.step(0)

        step_rows = min(hc, 256)

        def convert(i, carry):
            slot = lax.rem(i, 2)

            @pl.when(i + 1 < rd)
            def _():
                stage_in(i + 1, 1 - slot).start()

            stage_in(i, slot).wait()

            def chunk(j, carry):
                at = pl.ds(pl.multiple_of(j * step_rows, step_rows), step_rows)
                bank[c * rd + i, at, :] = stage[slot, c, at, :].astype(BF)
                swap[i, at, :] = stage[slot, 1 - c, at, :].astype(BF)
                return carry

            return lax.fori_loop(0, hc // step_rows, chunk, carry)

        lax.fori_loop(0, rd, convert, 0)
        swap_x = go(remote(swap, bank.at[pl.ds(c * rd, rd)], swap_s, swap_r, sib))
        w_in.start()

        part_rows = hc // 2
        gather_rows = min(part_rows, 128)

        def gather(dst, index, first, code, sources, h):
            def chunk(j, carry):
                at = pl.ds(pl.multiple_of(j * gather_rows, gather_rows), gather_rows)
                v = bank[jnp.minimum(code, cr - 1), pl.ds(pl.multiple_of(h * part_rows + j * gather_rows, gather_rows), gather_rows), :]
                for ref, off in sources:
                    i = jnp.clip(code - off, 0, ref.shape[0] - 1)
                    v = jnp.where(code >= off, ref[i, at, :], v)
                dst[index, pl.ds(pl.multiple_of(first + j * gather_rows, gather_rows), gather_rows), :] = v
                return carry

            lax.fori_loop(0, part_rows // gather_rows, chunk, 0)

        can_up, can_dn = z < chips - 1, z > 0

        def hop(p, h, sign):
            send, recv, s, r = (up_send, up_recv, up_s, up_r) if sign > 0 else (dn_send, dn_recv, dn_s, dn_r)
            return remote(send[p][h], recv[p][h], s.at[p, h], r.at[p, h], (me + 2 * sign + replicas) % replicas)

        def arrived(p, h):
            @pl.when(can_dn)
            def _():
                hop(p, h, 1).wait_recv()

            @pl.when(can_up)
            def _():
                hop(p, h, -1).wait_recv()

        def move(steps_from, steps_to):
            for step in range(steps_from, steps_to):
                p, h = step // 2, step % 2
                if p > 0:
                    arrived(p - 1, h)
                elif h == 0:
                    swap_x.wait_recv()
                for row, sign, send, recv, able in ((0, 1, up_send, up_recv, can_up), (1, -1, dn_send, dn_recv, can_dn)):

                    @pl.when(able)
                    def _(p=p, h=h, row=row, sign=sign, send=send, recv=recv):
                        sources = [(recv[e][h], cr + offs[e]) for e in range(p)]
                        for k in range(caps[p]):
                            gather(send[p][h], k, 0, tab_ref[row, offs[p] + k], sources, h)
                        hop(p, h, sign).start()

        windows.step(1)
        for x in rs_x:
            x.wait_recv()
        v = send_s[z]
        for d in range(chips - 1):
            v = v + came_s[d]
        t_c[c, z] = v
        for d in range(1, chips):
            go(remote(t_c.at[c, z], t_c.at[c, z], ag_s.at[0, d - 1], ag_r.at[0, d - 1], around(d) * 2 + c))
        for j in range(2, chips - 1):
            windows.step(j)
        move(0, 1)

        own_cols.wait()
        p_x.wait_recv()

        def chip_p(k, b):
            at = pl.ds(pl.multiple_of(b * blk, blk), blk)
            return p_own[k, at, :] + p_sib[k, at, :]

        def scatter(k):
            for d in range(1, chips):
                send_p[k, d - 1] = chip_p(k, around(d)).astype(BF)
                p_sent[k].append(
                    go(remote(send_p.at[k, d - 1], came_p.at[k, d - 1], rs_s.at[k, d - 1], rs_r.at[k, d - 1], around(d) * 2 + c))
                )

        def gathered(k):
            v = chip_p(k, z)
            for x in p_sent[k]:
                x.wait_recv()
            for d in range(chips - 1):
                v = v + came_p[k, d].astype(F32)
            return v

        scatter(1)


        for d in range(1, chips):
            src = (z + chips - d) % chips
            remote(t_c.at[c, src], t_c.at[c, src], ag_s.at[0, d - 1], ag_r.at[0, d - 1], src * 2 + c).wait_recv()
        go(remote(t_c.at[c], t_c.at[c], rel_s.at[0], rel_r.at[0], sib))
        remote(t_c.at[1 - c], t_c.at[1 - c], rel_s.at[0], rel_r.at[0], sib).wait_recv()

        windows.step(chips - 1)
        go(remote(t_wc.at[c], t_wc.at[c], rel_s.at[2], rel_r.at[2], sib))
        mine = cols_ref[pl.ds(pl.multiple_of(z * cr, cr), cr), :]

        def pick(columns, entries):
            index = jnp.concatenate(columns, axis=0)
            lane = lax.broadcasted_iota(I32, (index.shape[0], entries), 1)
            return jnp.where(index == lane, 1.0, 0.0).astype(F32)

        pick_w = pick([mine[:, k : k + 1] for k in range(n_win)], chips * win_blk)
        pick_n = pick([mine[:, n_win + k : n_win + k + 1] for k in range(n_new)], chips * blk)
        pick_wb, pick_nb = pick_w.astype(BF), pick_n.astype(BF)
        line_w[...] = dot(pick_wb, t_win[...].reshape(chips * win_blk, hc))
        remote(t_wc.at[1 - c], t_wc.at[1 - c], rel_s.at[2], rel_r.at[2], sib).wait_recv()
        wc_all = jnp.concatenate([t_wc[part_of].reshape(chips * win_blk, n) for part_of in range(2)], axis=1)
        line_wc = dot_exact(pick_w, wc_all)
        all_cols = cols_ref[...]
        far_w = [(s, tau) for s in range(steps) for tau in range(s, past)]
        pick_fw = pick([all_cols[:, s * past + tau : s * past + tau + 1] for s, tau in far_w], chips * win_blk)
        far_wc = dot_exact(pick_fw, wc_all[:, n:])

        kc = kc_ref[...]
        bc = bc_ref[...]
        b_new = t_c[0].reshape(chips * blk, -1)
        c_new = t_c[1].reshape(chips * blk, -1)
        raw_new = t_c[c].reshape(chips * blk, -1)
        far_n = [(s, t) for s in range(steps) for t in range(max(0, s - past), s + 1)]
        pick_fn = pick([all_cols[:, n_win + news.index(st) : n_win + news.index(st) + 1] for st in far_n], chips * blk)
        far_nc = dot_exact(pick_fn, c_new[:, :n])
        out_c = []
        for s in range(steps):
            tot = bc[:, n:]
            for j in range(taps):
                tau = s + j
                if tau < past:
                    k = far_w.index((s, tau))
                    v = far_wc[k * rows : (k + 1) * rows]
                else:
                    k = far_n.index((s, tau - past))
                    v = far_nc[k * rows : (k + 1) * rows]
                tot = tot + v * kc[j : j + 1, n:]
            out_c.append(jax.nn.silu(tot))
        c_all = jnp.concatenate(out_c, axis=0)
        c_hi, c_lo = halves(c_all)
        home = jnp.concatenate([all_cols[:, n_win + n_new + s : n_win + n_new + s + 1] for s in range(steps)], axis=0)
        zero = jnp.zeros_like(c_hi)
        for q in range(cr):
            here = home == z * cr + q
            lhs[:sr, q * n : (q + 1) * n] = jnp.where(here, c_hi, zero)
            lhs[sr:, q * n : (q + 1) * n] = jnp.where(here, c_lo, zero)

        def base_tile(j, carry):
            at = pl.ds(pl.multiple_of(j * tile, tile), tile)
            for q in range(cr):
                rhs[:, q * n : (q + 1) * n] = bank[q, at, :]
            got = lax.dot_general(lhs[...], rhs[...], (((1,), (1,)), ((), ())), preferred_element_type=F32)
            got = got[:sr] + got[sr:]
            for s in range(steps):
                for b in range(chips):
                    base[b, s * cr : (s + 1) * cr, at] = got[s * rows + b * cr : s * rows + (b + 1) * cr]
            return carry

        lax.fori_loop(0, hc // tile, base_tile, 0)
        for d in range(1, chips):
            out_b[d - 1] = base[around(d)].astype(BF)
        own_b[...] = base[z]
        b_x = [
            go(remote(out_b.at[d - 1], came_b.at[d - 1], b_s.at[d - 1], b_r.at[d - 1], around(d) * 2 + c))
            for d in range(1, chips)
        ]
        t_new[z] = gathered(1).astype(BF)
        for d in range(1, chips):
            go(remote(t_new.at[z], t_new.at[z], ag_s.at[1, d - 1], ag_r.at[1, d - 1], around(d) * 2 + c))
        scatter(0)

        move(1, 3)

        line_nb = dot_exact(pick_n, b_new[:, :n])
        line_nc = dot_exact(pick_n, c_new[:, :n])
        line_nr = dot_exact(pick_n, raw_new[:, n:])

        def coeff_line(s, tau, part_of):
            if tau < past:
                k = wins.index((s, tau))
                return line_wc[k * cr : (k + 1) * cr, part_of * n : (part_of + 1) * n]
            k = news.index((s, tau - past))
            return (line_nb, line_nc)[part_of][k * cr : (k + 1) * cr]

        def coeff(s, t, part_of):
            tot = bc[:, part_of * n : (part_of + 1) * n]
            for j in range(taps):
                tot = tot + coeff_line(s, t + j, part_of) * kc[j : j + 1, part_of * n : (part_of + 1) * n]
            return jax.nn.silu(tot)

        hp = hp_ref[c]
        rate = jnp.exp(hp[1:2])
        expand_in, final_w = [], []
        b_last = None
        for s in range(steps):
            c_now = coeff(s, s, 1)
            fade = jnp.ones((cr, LANES), F32)
            scaled, weights, bs = [None] * (s + 1), [None] * (s + 1), [None] * (s + 1)
            for t in range(s, -1, -1):
                k = news.index((s, t))
                v = line_nr[k * cr : (k + 1) * cr] + hp[0:1]
                size = jnp.maximum(v, 0.0) + jnp.log1p(jnp.exp(-jnp.abs(v)))
                weights[t] = fade * size
                bs[t] = coeff(s, t, 0)
                scaled[t] = weights[t] * jnp.sum(bs[t] * c_now, axis=1, keepdims=True)
                fade = fade * jnp.exp(-rate * size)
            expand_in += [fade] + scaled
            if s == steps - 1:
                final_w, b_last = weights, bs
        expand_in += final_w
        n_exp = len(expand_in)
        expand_in.append(jnp.broadcast_to(hp[2:3], (8, LANES)))
        spread = (
            lax.broadcasted_iota(I32, (LANES, hc), 0)
            == jnp.right_shift(lax.broadcasted_iota(I32, (LANES, hc), 1), head_shift)
        ).astype(F32)
        wide = dot_exact(jnp.concatenate(expand_in, axis=0), spread)
        wides = [wide[k * cr : (k + 1) * cr] for k in range(n_exp)]
        skip = wide[n_exp * cr : n_exp * cr + 1]

        for d in range(1, chips):
            src = (z + chips - d) % chips
            remote(t_new.at[src], t_new.at[src], ag_s.at[1, d - 1], ag_r.at[1, d - 1], src * 2 + c).wait_recv()
        line_n[...] = dot(pick_nb, t_new[...].reshape(chips * blk, hc))

        def x_line(s, tau):
            if tau < past:
                k = wins.index((s, tau))
                return line_w[k * cr : (k + 1) * cr, :]
            k = news.index((s, tau - past))
            return line_n[k * cr : (k + 1) * cr, :]

        kx_own = kx_ref[:, half_cols(c)]
        bx_own = bx_ref[:, half_cols(c)]
        for k, (s, t) in enumerate(news):
            tot = bx_own
            for j in range(taps):
                tot = tot + x_line(s, t + j) * kx_own[j : j + 1]
            xs[k] = jax.nn.silu(tot)

        last = steps - 1
        outs = [wides[n_exp - steps + t] * xs[news.index((last, t))] for t in range(steps)]
        outs.append(wides[n_exp - steps - (last + 1) - 1])
        outs += [x_line(last, steps + j) for j in range(past)]

        @pl.when(c == 0)
        def _():
            for k, v in enumerate(outs):
                x_ref[0, k] = v[:rd]
                x_away[k] = v[rd:]
            for t in range(steps):
                bo_ref[t] = b_last[t][:rd]
            for j in range(past):
                for part_of in range(2):
                    fc_own[j * rd : (j + 1) * rd, part_of * n : (part_of + 1) * n] = coeff_line(last, steps + j, part_of)[:rd]

        @pl.when(c == 1)
        def _():
            for k, v in enumerate(outs):
                x_ref[1, k] = v[rd:]
                x_away[k] = v[:rd]
            for t in range(steps):
                bo_ref[t] = b_last[t][rd:]
            for j in range(past):
                for part_of in range(2):
                    fc_own[j * rd : (j + 1) * rd, part_of * n : (part_of + 1) * n] = coeff_line(last, steps + j, part_of)[rd:]

        x_x = go(remote(x_away, x_ref.at[c], x_s, x_r, sib))
        fc_ref[mt] = fc_own[...]
        f_x = [
            go(remote(fc_own, fc_ref.at[mt], f_s.at[k - 1], f_r.at[k - 1], me, (mt + k) % tensors))
            for k in range(1, tensors)
        ]

        for x in b_x:
            x.wait_recv()
        gate[...] = gathered(0)
        own_base = own_b[...]
        for d in range(chips - 1):
            own_base = own_base + came_b[d].astype(F32)
        ys = []
        e = 0
        for s in range(steps):
            y = wides[e] * own_base[s * cr : (s + 1) * cr] + skip * xs[news.index((s, s))]
            for t in range(s + 1):
                y = y + wides[e + 1 + t] * xs[news.index((s, t))]
            e += s + 2
            ys.append(y * jax.nn.silu(gate[s * cr : (s + 1) * cr, :]))
        y = jnp.concatenate(ys, axis=0)
        first_head = mt * (2 * hh) + c * hh
        col_head = first_head + jnp.right_shift(lax.broadcasted_iota(I32, (LANES, hc), 1), head_shift)
        col_group = col_head - jnp.left_shift(jnp.right_shift(col_head, group_shift), group_shift)
        member = (lax.broadcasted_iota(I32, (LANES, hc), 0) == col_group).astype(F32)
        own_sq = lax.dot_general(
            y * y, member, (((1,), (1,)), ((), ())), preferred_element_type=F32, precision=lax.Precision.HIGHEST
        )
        squares[...] = own_sq
        q_x = [go(remote(squares, came_q.at[0], q_s.at[0], q_r.at[0], sib))]
        for i, (k, cc) in enumerate(pairs):
            slot = 1 + (k - 1) * 2 + lax.rem(cc + c, 2)
            dst = 1 + (k - 1) * 2 + lax.rem(cc + c, 2)
            q_x.append(go(remote(squares, came_q.at[dst], q_s.at[slot], q_r.at[slot], z * 2 + cc, (mt + k) % tensors)))

        move(3, 4)

        for x in q_x:
            x.wait_recv()
        tot = squares[...]
        for i in range(1 + len(pairs)):
            tot = tot + came_q[i]
        inverse = lax.rsqrt(tot / group_channels + 1e-05)
        normed[c, z] = (y * dot_exact(inverse, member) * gain_ref[:, half_cols(c)]).astype(BF)
        for d in range(1, chips):
            go(remote(normed.at[c, z], normed.at[c, z], n_s.at[d - 1], n_r.at[d - 1], around(d) * 2 + c))

        move(4, 6)

        for d in range(1, chips):
            src = (z + chips - d) % chips
            remote(normed.at[c, src], normed.at[c, src], n_s.at[d - 1], n_r.at[d - 1], src * 2 + c).wait_recv()
        go(remote(normed.at[c], normed.at[c], rel_s.at[1], rel_r.at[1], sib))
        remote(normed.at[1 - c], normed.at[1 - c], rel_s.at[1], rel_r.at[1], sib).wait_recv()

        move(6, 7)
        w_in.wait()
        out_tile = min(512, width)
        left = normed[0].reshape(chips * blk, hc)
        right = normed[1].reshape(chips * blk, hc)

        def project(j, carry):
            at = pl.ds(pl.multiple_of(j * out_tile, out_tile), out_tile)
            got = dot(left, w_vm[:hc, at]) + dot(right, w_vm[hc:, at])
            part[:, :, :, at] = got.reshape(chips, steps, cr, out_tile)
            return carry

        lax.fori_loop(0, width // out_tile, project, 0)

        def share(t):
            first = t * rt
            return part.at[first // cr, :, pl.ds(pl.multiple_of(first % cr, 8), rt), :]

        m_x = []
        for k in range(1, tensors):
            to = (mt + k) % tensors
            m_x.append(go(remote(share(to), came_m.at[k - 1], m_s.at[k - 1], m_r.at[k - 1], me, to)))

        move(7, 2 * count)
        mv_x = []
        for h in range(2):
            arrived(count - 1, h)
            sources = [(up_recv[e][h], cr + offs[e]) for e in range(count)]
            sources += [(dn_recv[e][h], cr + total + offs[e]) for e in range(count)]

            def final_row(i, carry, sources=sources, h=h):
                first = h * part_rows
                gather(away.at[h], i, 0, tab_ref[2, z * cr + (1 - c) * rd + i], sources, h)
                gather(moved_ref.at[:, c], i, first, tab_ref[2, z * cr + c * rd + i], sources, h)
                return carry

            lax.fori_loop(0, rd, final_row, 0)
            mv_x.append(go(remote(away.at[h], moved_ref.at[:, c, pl.ds(h * part_rows, part_rows)], mv_s.at[h], mv_r.at[h], sib)))

        for x in m_x:
            x.wait_recv()
        first = mt * rt
        tot = part[first // cr, :, pl.ds(pl.multiple_of(first % cr, 8), rt), :]
        for k in range(tensors - 1):
            tot = tot + came_m[k]
        mixed_ref[...] = tot.astype(BF)

        remote(x_away, x_ref.at[1 - c], x_s, x_r, sib).wait_recv()
        for k in range(1, tensors):
            src = (mt + tensors - k) % tensors
            remote(fc_own, fc_ref.at[src], f_s.at[k - 1], f_r.at[k - 1], me, src).wait_recv()
        for h in range(2):
            remote(away.at[h], moved_ref.at[:, 1 - c, pl.ds(h * part_rows, part_rows)], mv_s.at[h], mv_r.at[h], sib).wait_recv()
        for x in sends:
            x.wait_send()
        for drain in ends:
            drain()
        for p in range(count):
            for h in range(2):

                @pl.when(can_up)
                def _(p=p, h=h):
                    hop(p, h, 1).wait_send()

                @pl.when(can_dn)
                def _(p=p, h=h):
                    hop(p, h, -1).wait_send()

    def vm(*shape, dtype=F32):
        return pltpu.VMEM(shape, dtype)

    def sem(*shape):
        return pltpu.SemaphoreType.DMA(shape) if shape else pltpu.SemaphoreType.DMA

    slots = [vm(cap, hc // 2, n, dtype=BF) for cap in caps for h in range(2)]
    few = chips - 1
    scratch = [
        vm(2, sr, hc), vm(2, sr, hc), vm(sr, small.shape[2]),
        vm(2, few, blk, hc, dtype=BF), vm(chips, blk, small.shape[2]),
        vm(2, few, blk, hc, dtype=BF), vm(few, blk, small.shape[2]),
        vm(blk, hc),
        vm(chips, blk, hc, dtype=BF), vm(2, chips, blk, small.shape[2]),
        vm(win_pad, hc, dtype=BF), vm(win_rows, n), vm(chips, win_blk, hc, dtype=BF), vm(2, chips, win_blk, n),
        vm(*w_out.shape, dtype=BF),
        vm(2, 2, hc, n), vm(cr, hc, n, dtype=BF), vm(rd, hc, n, dtype=BF),
        *slots, *slots, *slots, *slots,
        vm(n_win * cr, hc), vm(n_new * cr, hc), vm(n_new, cr, hc),
        vm(2 * sr, cr * n, dtype=BF), vm(tile, cr * n, dtype=BF),
        vm(chips, blk, hc), vm(few, blk, hc, dtype=BF), vm(few, blk, hc, dtype=BF), vm(blk, hc),
        vm(blk, LANES), vm(1 + len(pairs), blk, LANES), vm(2, chips, blk, hc, dtype=BF),
        vm(chips, steps, cr, width), vm(tensors - 1, steps, rt, width),
        vm(2, rd, hc // 2, n, dtype=BF), vm(n_out, rd, hc), vm(past * rd, 2 * n),
        sem(2), sem(2), sem(4), sem(4), sem(2, 2, few), sem(2, 2, few), sem(), sem(),
        sem(3, few), sem(3, few), sem(2, few), sem(2, few), sem(3), sem(3), sem(few), sem(few),
        sem(1 + len(pairs)), sem(1 + len(pairs)), sem(tensors - 1), sem(tensors - 1), sem(few), sem(few),
        sem(tensors - 1), sem(tensors - 1), sem(), sem(), sem(2), sem(2),
        sem(len(caps), 2), sem(len(caps), 2), sem(len(caps), 2), sem(len(caps), 2),
    ]
    in_vm = pl.BlockSpec(memory_space=pltpu.VMEM)
    in_any = pl.BlockSpec(memory_space=pl.ANY)
    return pl.pallas_call(
        kernel,
        out_shape=(
            jax.ShapeDtypeStruct((steps, rt, width), BF),
            jax.ShapeDtypeStruct((rd, 2, hc, n), BF),
            jax.ShapeDtypeStruct((2, n_out, rd, hc), F32),
            jax.ShapeDtypeStruct((steps, rd, n), F32),
            jax.ShapeDtypeStruct((tensors, past * rd, 2 * n), F32),
        ),
        in_specs=[pl.BlockSpec(memory_space=pltpu.SMEM), in_vm, in_any, in_vm, in_vm, in_vm, in_any]
        + [in_vm] * 6
        + [in_any],
        out_specs=[in_vm] * 5,
        scratch_shapes=scratch,
        compiler_params=pltpu.CompilerParams(
            collective_id=0, has_side_effects=True, vmem_limit_bytes=60 * 1024 * 1024
        ),
        name="engine",
    )(tab, cols, proj, small, win, wc, state, kern_x, bias_x, kern_c, bias_c, head_par, gain, w_out)


def finish(moved, x_out, b_out):
    rd, _, hc, n = moved.shape
    steps = b_out.shape[0]

    def kernel(moved_ref, x_ref, b_ref, out_ref):
        r = pl.program_id(0)
        b_hi, b_lo = halves(jnp.concatenate([b_ref[t, pl.ds(r, 1), :] for t in range(steps)], axis=0))
        ones = jnp.ones((2, n), BF)
        right = jnp.concatenate(
            [
                jnp.concatenate([b_hi, b_hi, b_lo, jnp.zeros_like(ones)], axis=0),
                jnp.concatenate([jnp.zeros((3 * steps, n), BF), ones], axis=0),
            ],
            axis=1,
        )
        for j in range(2):
            hi, lo = halves(jnp.concatenate([x_ref[j, t, pl.ds(r, 1), :] for t in range(steps)], axis=0))
            fade_hi, fade_lo = halves(x_ref[j, steps, pl.ds(r, 1), :])
            left = jnp.concatenate([hi, lo, hi, fade_hi, fade_lo], axis=0)
            both = lax.dot_general(left, right, (((0,), (0,)), ((), ())), preferred_element_type=F32)
            out_ref[0, j] = both[:, n:] * moved_ref[0, j].astype(F32) + both[:, :n]

    return pl.pallas_call(
        kernel,
        grid=(rd,),
        out_shape=jax.ShapeDtypeStruct(moved.shape, F32),
        in_specs=[
            pl.BlockSpec((1, 2, hc, n), lambda r: (r, 0, 0, 0)),
            pl.BlockSpec((2, steps + 1, rd, hc), lambda r: (0, 0, 0, 0)),
            pl.BlockSpec((steps, rd, n), lambda r: (0, 0, 0)),
        ],
        out_specs=pl.BlockSpec((1, 2, hc, n), lambda r: (r, 0, 0, 0)),
        name="finish",
    )(moved, x_out, b_out)


def fetch(every, index):
    count = index.shape[0]

    def kernel(index_ref, every_ref, out_ref, sems):
        for i in range(count):
            pltpu.make_async_copy(every_ref.at[index_ref[i]], out_ref.at[i], sems.at[i]).start()
        for i in range(count):
            pltpu.make_async_copy(every_ref.at[0], out_ref.at[i], sems.at[i]).wait()

    return pl.pallas_call(
        kernel,
        out_shape=jax.ShapeDtypeStruct((count,) + every.shape[1:], every.dtype),
        in_specs=[pl.BlockSpec(memory_space=pltpu.SMEM), pl.BlockSpec(memory_space=pl.ANY)],
        out_specs=pl.BlockSpec(memory_space=pltpu.VMEM),
        scratch_shapes=[pltpu.SemaphoreType.DMA((count,))],
        name="fetch",
    )(index, every)


def local(
    hidden,
    parents,
    input_weight,
    coeff_weight,
    step_weight,
    kernel_x,
    kernel_bias_x,
    kernel_coeff,
    kernel_bias_coeff,
    step_bias,
    log_rate,
    skip_gain,
    norm_gain,
    output_weight,
    scan_state,
    window_x,
    window_coeff,
):
    rows_dev, heads, head_dim, n = scan_state.shape
    steps, rows, depth = hidden.shape
    taps = kernel_x.shape[0]
    past = taps - 1
    chans = heads * head_dim
    half = chans // 2
    replicas = lax.axis_size("replica")
    tensors = lax.axis_size("tensor")
    chips = replicas // 2
    chip_rows = 2 * rows_dev
    me = lax.axis_index("replica")
    mt = lax.axis_index("tensor")
    heads_all = heads * tensors
    groups = kernel_bias_coeff.shape[1] // n
    my_group = mt * heads * groups // heads_all
    coeff_at = my_group * n
    win_rows = past * rows_dev
    win_pad = -(-win_rows // 16) * 16

    def own_group(v):
        return lax.dynamic_slice_in_dim(v, coeff_at, n, axis=v.ndim - 1)

    tab, cols = plan(parents.astype(I32), replicas, past)

    win = window_x.transpose(1, 0, 2).reshape(win_rows, chans).astype(BF)
    win = jnp.pad(win, ((0, win_pad - win_rows), (0, 0)))
    wc = own_group(window_coeff).transpose(1, 0, 2, 3).reshape(win_rows, 2 * n)

    h = hidden.reshape(steps, chips, chip_rows, depth).transpose(1, 0, 2, 3)
    h = h.reshape(steps * rows, depth)
    proj = jnp.einsum("rd,dkc->krc", h, input_weight, preferred_element_type=F32)
    coef = jnp.einsum("rd,dkc->krc", h, own_group(coeff_weight), preferred_element_type=F32)
    raw = dot(h, step_weight).reshape(steps * rows, 2, heads // 2).transpose(1, 0, 2)
    small = jnp.concatenate([coef, jnp.pad(raw, ((0, 0), (0, 0), (0, LANES - heads // 2)))], axis=2)

    kern_c = own_group(kernel_coeff).reshape(taps, 2 * n)
    bias_c = own_group(kernel_bias_coeff).reshape(1, 2 * n)
    head_par = jnp.stack([step_bias, log_rate, skip_gain]).reshape(3, 2, heads // 2).transpose(1, 0, 2)
    head_par = jnp.pad(head_par, ((0, 0), (0, 5), (0, LANES - heads // 2)))

    mixed, moved, x_out, b_out, fc = engine(
        tab, cols, proj, small, win, wc, scan_state.reshape(rows_dev, 2, half, n), kernel_x,
        kernel_bias_x.reshape(1, chans), kern_c, bias_c, head_par, norm_gain.reshape(1, chans), output_weight,
        dict(steps=steps, past=past, groups=groups, replicas=replicas, tensors=tensors, head_dim=head_dim),
    )
    mixed = mixed.reshape(steps, rows // tensors, -1)

    def slow():
        every = lax.all_gather(scan_state.astype(BF).reshape(rows_dev, 2, half, n), "replica", axis=0, tiled=True)
        first = jnp.arange(rows, dtype=I32)
        for s in range(steps - 1, -1, -1):
            first = jnp.take(parents[s], first)
        return finish(fetch(every, lax.dynamic_slice_in_dim(first, me * rows_dev, rows_dev)), x_out, b_out)

    final = lax.cond(tab[3, 0] > 0, slow, lambda: finish(moved, x_out, b_out))
    final = final.reshape(rows_dev, heads, head_dim, n)
    final_x = x_out[:, steps + 1 :].transpose(2, 1, 0, 3).reshape(rows_dev, past, chans)
    final_c = fc.reshape(groups, tensors // groups, past, rows_dev, 2, n)[:, 0]
    final_c = final_c.transpose(2, 1, 3, 0, 4).reshape(rows_dev, past, 2, groups * n)
    return (mixed, final, final_x, final_c)


def solution(mesh):
    placed = (
        P(None, None, "replica"),
        P(),
        P("replica", None, "tensor"),
        P("replica", None, None),
        P("replica", "tensor"),
        P(None, "tensor"),
        P("tensor"),
        P(),
        P(),
        P("tensor"),
        P("tensor"),
        P("tensor"),
        P("tensor"),
        P("tensor", "replica"),
        P("replica", "tensor", None, None),
        P("replica", None, "tensor"),
        P("replica", None, None, None),
    )
    return jax.shard_map(
        local,
        mesh=mesh,
        in_specs=placed,
        out_specs=(
            P(None, "tensor", "replica"),
            P("replica", "tensor", None, None),
            P("replica", None, "tensor"),
            P("replica", None, None, None),
        ),
        check_vma=False,
    )
```

```python
import functools

import jax
import jax.numpy as jnp
from jax import lax
from jax.experimental import pallas as pl
from jax.experimental.pallas import tpu as pltpu
from jax.sharding import PartitionSpec as P

BF = jnp.bfloat16
F32 = jnp.float32
I32 = jnp.int32
MESH = pl.DeviceIdType.MESH
LANES = 128


def dot(a, b):
    return jnp.dot(a, b, preferred_element_type=F32)


def dot_exact(a, b):
    return jnp.dot(a, b, preferred_element_type=F32, precision=lax.Precision.HIGHEST)


def halves(v):
    high = v.astype(BF)
    return high, (v - high.astype(F32)).astype(BF)


def shift_of(v):
    assert v & (v - 1) == 0
    return v.bit_length() - 1


def phase_caps(chips):
    return (2,) * (2 * chips - 1)


def place_lists(steps, past):
    wins = [(s, tau) for s in range(steps) for tau in range(past)]
    news = [(s, t) for s in range(steps) for t in range(s + 1)]
    return wins, news


def plan(parents, replicas, past):
    steps, rows = parents.shape
    rows_dev = rows // replicas
    chips = replicas // 2
    chip_rows = 2 * rows_dev
    chip_pad = -(-chips // 8) * 8
    width = max(rows, LANES)
    caps = phase_caps(chips)
    total = sum(caps)
    dev_shift, chip_shift = shift_of(rows_dev), shift_of(chip_rows)
    wins, news = place_lists(steps, past)

    def kernel(par_ref, tab_ref, cols_ref):
        z = lax.axis_index("replica") // 2
        lane = lax.broadcasted_iota(I32, (rows, rows), 1)
        sub = lax.broadcasted_iota(I32, (rows, rows), 0)
        eye = lane == sub
        own = lax.broadcasted_iota(I32, (rows, 1), 0)
        anc = {}
        for s in range(steps):
            anc[s, s + 1] = own
            for t in range(s, -1, -1):
                hit = jnp.where(lane == anc[s, t + 1], par_ref[t : t + 1, :], 0)
                anc[s, t] = jnp.sum(hit, axis=1, keepdims=True)
        columns = []
        for s, tau in wins:
            a = anc[s, 0]
            dev = jnp.right_shift(a, dev_shift)
            columns.append(dev * (past * rows_dev) + tau * rows_dev + (a - dev * rows_dev))
        for s, t in news:
            a = anc[s, t + 1]
            chip = jnp.right_shift(a, chip_shift)
            columns.append(chip * (steps * chip_rows) + t * chip_rows + (a - chip * chip_rows))
        columns += [anc[s, 0] for s in range(steps)]
        at = lax.broadcasted_iota(I32, (rows, LANES), 1)
        table = jnp.zeros((rows, LANES), I32)
        for k, col in enumerate(columns):
            table = jnp.where(at == k, col, table)
        cols_ref[...] = table

        last = anc[steps - 1, 0]
        hit = lane == last
        row_chip = jnp.right_shift(sub, chip_shift)
        up_to = jnp.max(jnp.where(hit, row_chip, -1), axis=0, keepdims=True)
        down_to = jnp.min(jnp.where(hit, row_chip, chips), axis=0, keepdims=True)
        q = lax.broadcasted_iota(I32, (1, rows), 1)
        q_chip = jnp.right_shift(q, chip_shift)
        q_local = q - q_chip * chip_rows
        at_chip = lax.broadcasted_iota(I32, (chip_pad, rows), 0)
        shift_down = (
            lax.broadcasted_iota(I32, (chip_pad, chip_pad), 0)
            == lax.broadcasted_iota(I32, (chip_pad, chip_pad), 1) + 1
        ).astype(F32)
        src_at = lax.broadcasted_iota(I32, (chip_pad, width), 1)

        def route(home, dest):
            have = ((home == at_chip) & (dest > at_chip)).astype(I32)
            beyond = (dest > at_chip).astype(I32)
            loc = jnp.where(home == at_chip, q_local, 0)
            key = dest * rows + (rows - 1 - q)
            key_col = jnp.sum(jnp.where(eye, key, 0), axis=1, keepdims=True)
            ahead = (key_col > key).astype(F32)
            src = jnp.zeros((chip_pad, width), I32)
            off, needed = 0, jnp.zeros((1, 1), I32)
            for p, cap in enumerate(caps):
                rank = dot(have.astype(F32), ahead).astype(I32)
                picked = have * (rank < cap).astype(I32)
                for k in range(cap):
                    chosen = jnp.where(rank == k, picked * loc, 0)
                    v = jnp.sum(chosen, axis=1, keepdims=True)
                    src = jnp.where(src_at == off + k, v, src)
                sent = picked * (1 + chip_rows + off + rank)
                came = dot(shift_down, sent.astype(F32)).astype(I32)
                loc = jnp.where(came > 0, came - 1, loc)
                have = jnp.where(came > 0, beyond, have - picked)
                off += cap
                used = jnp.max(jnp.max(picked, axis=1, keepdims=True), axis=0, keepdims=True)
                needed = jnp.where(used > 0, p + 1, needed)
            left = jnp.max(jnp.max(have, axis=1, keepdims=True), axis=0, keepdims=True)
            return src, loc, jnp.where(left > 0, len(caps) + 1, needed)

        up_src, up_loc, up_needed = route(q_chip, up_to)
        down_src, down_loc, down_needed = route(chips - 1 - q_chip, chips - 1 - down_to)

        def row_of(v, chip):
            index = lax.broadcasted_iota(I32, v.shape, 0)
            return jnp.sum(jnp.where(index == chip, v, 0), axis=0, keepdims=True)

        here_up = row_of(up_loc, z)
        here_down = row_of(down_loc, chips - 1 - z) + total
        code = jnp.where(q_chip == z, q_local, jnp.where(q_chip < z, here_up, here_down))
        code_col = jnp.sum(jnp.where(hit, code, 0), axis=1, keepdims=True)
        code_row = jnp.sum(jnp.where(eye, code_col, 0), axis=0, keepdims=True)
        tab_ref[...] = jnp.zeros(tab_ref.shape, I32)
        tab_ref[0:1, :] = row_of(up_src, z)
        tab_ref[1:2, :] = row_of(down_src, chips - 1 - z)
        tab_ref[2:3, :rows] = code_row
        tab_ref[3:4, :] = jnp.zeros((1, width), I32) + jnp.maximum(up_needed, down_needed)

    return pl.pallas_call(
        kernel,
        out_shape=(
            jax.ShapeDtypeStruct((8, width), I32),
            jax.ShapeDtypeStruct((rows, LANES), I32),
        ),
        in_specs=[pl.BlockSpec(memory_space=pltpu.VMEM)],
        out_specs=[pl.BlockSpec(memory_space=pltpu.VMEM)] * 2,
        name="plan",
    )(parents)


def engine(tab, cols, proj, small, win, wc, state, kern_x, bias_x, kern_c, bias_c, head_par, gain, w_out, dims, count, ident):
    steps, past, groups = dims["steps"], dims["past"], dims["groups"]
    replicas, tensors = dims["replicas"], dims["tensors"]
    rows = cols.shape[0]
    rd, _, hc, n = state.shape
    chips = replicas // 2
    cr = 2 * rd
    sr = steps * rows
    blk = steps * cr
    head_dim = dims["head_dim"]
    hh = hc // head_dim
    taps = past + 1
    win_pad, win_rows = win.shape[0], past * rd
    win_blk = 2 * win_rows
    total = sum(phase_caps(chips))
    caps = phase_caps(chips)[:count]
    offs = [sum(caps[:i]) for i in range(len(caps))]
    width = w_out.shape[1]
    rt = rows // tensors
    group_channels = tensors * 2 * hc // groups
    wins, news = place_lists(steps, past)
    n_win, n_new = len(wins), len(news)
    tile = min(256, hc)
    n_out = steps + 1 + past
    pairs = [(k, cc) for k in range(1, tensors) for cc in range(2)]
    head_shift, group_shift = shift_of(head_dim), shift_of(groups)

    def kernel(
        tab_ref, cols_ref, proj_ref, small_ref, win_ref, wc_ref, state_ref, kx_ref, bx_ref, kc_ref, bc_ref,
        hp_ref, gain_ref, wout_ref,
        mixed_ref, moved_ref, x_ref, bo_ref, fc_ref,
        p_own, p_sib, s_sib, send_p, send_s, came_p, came_s, gate, t_new, t_c, w_sib, wc_sib, t_win, t_wc,
        w_vm, stage, bank, swap, *rest,
    ):
        slots = [[[rest[(k * count + p) * 2 + h] for h in range(2)] for p in range(count)] for k in range(4)]
        up_send, up_recv, dn_send, dn_recv = slots
        (
            line_w, line_n, xs, lhs, rhs, base, out_b, came_b, own_b, squares, came_q, normed, part, came_m,
            away, x_away, fc_own,
            loc_sem, stage_sem, sib_s, sib_r, win_s, win_r, swap_s, swap_r, rs_s, rs_r, ag_s, ag_r,
            rel_s, rel_r, b_s, b_r, q_s, q_r, f_s, f_r, n_s, n_r, m_s, m_r, x_s, x_r, mv_s, mv_r,
            up_s, up_r, dn_s, dn_r, x_ag_s, x_ag_r,
        ) = rest[8 * count :]
        me = lax.axis_index("replica")
        mt = lax.axis_index("tensor")
        z = me // 2
        c = me % 2
        sib = me + 1 - 2 * c

        def remote(src, dst, s, r, rep, ten=None):
            return pltpu.make_async_remote_copy(
                src_ref=src, dst_ref=dst, send_sem=s, recv_sem=r,
                device_id=(rep, mt if ten is None else ten), device_id_type=MESH,
            )

        barrier = pltpu.get_barrier_semaphore()
        for k in range(1, replicas):
            pl.semaphore_signal(barrier, inc=1, device_id=((me + k) % replicas, mt), device_id_type=MESH)
        for k, cc in pairs:
            pl.semaphore_signal(
                barrier, inc=1, device_id=(z * 2 + cc, (mt + k) % tensors), device_id_type=MESH
            )
        pl.semaphore_wait(barrier, replicas - 1 + len(pairs))

        sends = []

        def go(copy):
            copy.start()
            sends.append(copy)
            return copy

        ends = []

        class Spread:
            def __init__(self, blocks, s, r):
                self.blocks, self.s, self.r = blocks, s, r
                ends.append(self.drain)

            def copy(self, i, way, j, b):
                ref = self.blocks[i](b)
                rep = (me + (2 if way == 0 else replicas - 2)) % replicas
                return remote(ref, ref, self.s.at[i, way, j], self.r.at[i, way, j], rep)

            def each(self, j, what, sending):
                for i in range(len(self.blocks)):
                    for way in range(2):
                        if sending:
                            b = z - j if way == 0 else z + j
                            able = (b >= 0) & (z < chips - 1) if way == 0 else (b < chips) & (z > 0)
                        else:
                            b = z - 1 - j if way == 0 else z + 1 + j
                            able = b >= 0 if way == 0 else b < chips

                        @pl.when(able)
                        def _(i=i, way=way, b=b):
                            getattr(self.copy(i, way, j, b), what)()

            def step(self, j):
                if j > 0:
                    self.each(j - 1, "wait_recv", False)
                if j < chips - 1:
                    self.each(j, "start", True)

            def drain(self):
                for j in range(chips - 1):
                    self.each(j, "wait_send", True)

        def half_cols(h):
            return pl.ds(pl.multiple_of(h * hc, hc), hc)

        own_cols = pltpu.make_async_copy(proj_ref.at[:, :, half_cols(c)], p_own, loc_sem.at[0])
        own_cols.start()
        s_x = go(remote(small_ref.at[1 - c], s_sib, sib_s.at[1], sib_r.at[1], sib))
        other = pl.ds(pl.multiple_of((1 - c) * n, n), n)
        w_x = go(remote(win_ref.at[:, half_cols(1 - c)], w_sib, sib_s.at[2], sib_r.at[2], sib))
        wc_x = go(remote(wc_ref.at[:, other], wc_sib, sib_s.at[3], sib_r.at[3], sib))
        p_x = go(remote(proj_ref.at[:, :, half_cols(1 - c)], p_sib, sib_s.at[0], sib_r.at[0], sib))
        w_in = pltpu.make_async_copy(wout_ref, w_vm, loc_sem.at[1])

        def stage_in(i, slot):
            return pltpu.make_async_copy(state_ref.at[i], stage.at[slot], stage_sem.at[slot])

        stage_in(0, 0).start()

        s_x.wait_recv()
        send_s[...] = (small_ref[c] + s_sib[...]).reshape(send_s.shape)

        def around(d):
            return (z + d) % chips

        rs_x, p_sent = [], ([], [])
        for d in range(1, chips):
            rep = around(d) * 2 + c
            rs_x.append(go(remote(send_s.at[around(d)], came_s.at[d - 1], rs_s.at[2, d - 1], rs_r.at[2, d - 1], rep)))

        w_x.wait_recv()
        wc_x.wait_recv()

        def in_order(own, sibling):
            return jnp.where(c == 0, jnp.concatenate([own, sibling]), jnp.concatenate([sibling, own]))

        t_win[z] = in_order(win_ref[:win_rows, half_cols(c)].astype(F32), w_sib[:win_rows].astype(F32)).astype(BF)
        t_wc[c, z] = in_order(wc_ref[:, pl.ds(pl.multiple_of(c * n, n), n)], wc_sib[...])
        windows = Spread([lambda b: t_win.at[b], lambda b: t_wc.at[c, b]], win_s, win_r)
        windows.step(0)

        step_rows = min(hc, 256)

        def convert(i, carry):
            slot = lax.rem(i, 2)

            @pl.when(i + 1 < rd)
            def _():
                stage_in(i + 1, 1 - slot).start()

            stage_in(i, slot).wait()

            def chunk(j, carry):
                at = pl.ds(pl.multiple_of(j * step_rows, step_rows), step_rows)
                bank[c * rd + i, at, :] = stage[slot, c, at, :].astype(BF)
                swap[i, at, :] = stage[slot, 1 - c, at, :].astype(BF)
                return carry

            return lax.fori_loop(0, hc // step_rows, chunk, carry)

        lax.fori_loop(0, rd, convert, 0)
        swap_x = go(remote(swap, bank.at[pl.ds(c * rd, rd)], swap_s, swap_r, sib))
        w_in.start()

        part_rows = hc // 2
        gather_rows = min(part_rows, 128)

        def gather(dst, index, first, code, sources, h):
            def chunk(j, carry):
                at = pl.ds(pl.multiple_of(j * gather_rows, gather_rows), gather_rows)
                v = bank[jnp.minimum(code, cr - 1), pl.ds(pl.multiple_of(h * part_rows + j * gather_rows, gather_rows), gather_rows), :]
                for ref, off in sources:
                    i = jnp.clip(code - off, 0, ref.shape[0] - 1)
                    v = jnp.where(code >= off, ref[i, at, :], v)
                dst[index, pl.ds(pl.multiple_of(first + j * gather_rows, gather_rows), gather_rows), :] = v
                return carry

            lax.fori_loop(0, part_rows // gather_rows, chunk, 0)

        can_up, can_dn = z < chips - 1, z > 0

        def hop(p, h, sign):
            send, recv, s, r = (up_send, up_recv, up_s, up_r) if sign > 0 else (dn_send, dn_recv, dn_s, dn_r)
            return remote(send[p][h], recv[p][h], s.at[p, h], r.at[p, h], (me + 2 * sign + replicas) % replicas)

        def arrived(p, h):
            @pl.when(can_dn)
            def _():
                hop(p, h, 1).wait_recv()

            @pl.when(can_up)
            def _():
                hop(p, h, -1).wait_recv()

        def move(steps_from, steps_to):
            for step in range(steps_from, steps_to):
                p, h = step // 2, step % 2
                if p > 0:
                    arrived(p - 1, h)
                elif h == 0:
                    swap_x.wait_recv()
                for row, sign, send, recv, able in ((0, 1, up_send, up_recv, can_up), (1, -1, dn_send, dn_recv, can_dn)):

                    @pl.when(able)
                    def _(p=p, h=h, row=row, sign=sign, send=send, recv=recv):
                        sources = [(recv[e][h], cr + offs[e]) for e in range(p)]
                        for k in range(caps[p]):
                            gather(send[p][h], k, 0, tab_ref[row, offs[p] + k], sources, h)
                        hop(p, h, sign).start()

        windows.step(1)
        for x in rs_x:
            x.wait_recv()
        v = send_s[z]
        for d in range(chips - 1):
            v = v + came_s[d]
        t_c[c, z] = v
        for d in range(1, chips):
            go(remote(t_c.at[c, z], t_c.at[c, z], ag_s.at[0, d - 1], ag_r.at[0, d - 1], around(d) * 2 + c))
        for j in range(2, chips - 1):
            windows.step(j)
        move(0, 2)

        own_cols.wait()
        p_x.wait_recv()

        def chip_p(k, b):
            at = pl.ds(pl.multiple_of(b * blk, blk), blk)
            return p_own[k, at, :] + p_sib[k, at, :]

        def scatter(k):
            for d in range(1, chips):
                send_p[k, d - 1] = chip_p(k, around(d)).astype(BF)
                p_sent[k].append(
                    go(remote(send_p.at[k, d - 1], came_p.at[k, d - 1], rs_s.at[k, d - 1], rs_r.at[k, d - 1], around(d) * 2 + c))
                )

        def gathered(k):
            v = chip_p(k, z)
            for x in p_sent[k]:
                x.wait_recv()
            for d in range(chips - 1):
                v = v + came_p[k, d].astype(F32)
            return v

        scatter(1)


        for d in range(1, chips):
            src = (z + chips - d) % chips
            remote(t_c.at[c, src], t_c.at[c, src], ag_s.at[0, d - 1], ag_r.at[0, d - 1], src * 2 + c).wait_recv()
        go(remote(t_c.at[c], t_c.at[c], rel_s.at[0], rel_r.at[0], sib))
        remote(t_c.at[1 - c], t_c.at[1 - c], rel_s.at[0], rel_r.at[0], sib).wait_recv()

        windows.step(chips - 1)
        go(remote(t_wc.at[c], t_wc.at[c], rel_s.at[2], rel_r.at[2], sib))
        mine = cols_ref[pl.ds(pl.multiple_of(z * cr, cr), cr), :]

        def pick(columns, entries):
            index = jnp.concatenate(columns, axis=0)
            lane = lax.broadcasted_iota(I32, (index.shape[0], entries), 1)
            return jnp.where(index == lane, 1.0, 0.0).astype(F32)

        pick_w = pick([mine[:, k : k + 1] for k in range(n_win)], chips * win_blk)
        pick_n = pick([mine[:, n_win + k : n_win + k + 1] for k in range(n_new)], chips * blk)
        pick_wb, pick_nb = pick_w.astype(BF), pick_n.astype(BF)
        line_w[...] = dot(pick_wb, t_win[...].reshape(chips * win_blk, hc))
        remote(t_wc.at[1 - c], t_wc.at[1 - c], rel_s.at[2], rel_r.at[2], sib).wait_recv()
        wc_all = jnp.concatenate([t_wc[part_of].reshape(chips * win_blk, n) for part_of in range(2)], axis=1)
        line_wc = dot_exact(pick_w, wc_all)
        all_cols = cols_ref[...]
        far_w = [(s, tau) for s in range(steps) for tau in range(s, past)]
        pick_fw = pick([all_cols[:, s * past + tau : s * past + tau + 1] for s, tau in far_w], chips * win_blk)
        far_wc = dot_exact(pick_fw, wc_all[:, n:])

        kc = kc_ref[...]
        bc = bc_ref[...]
        b_new = t_c[0].reshape(chips * blk, -1)
        c_new = t_c[1].reshape(chips * blk, -1)
        raw_new = t_c[c].reshape(chips * blk, -1)
        far_n = [(s, t) for s in range(steps) for t in range(max(0, s - past), s + 1)]
        pick_fn = pick([all_cols[:, n_win + news.index(st) : n_win + news.index(st) + 1] for st in far_n], chips * blk)
        far_nc = dot_exact(pick_fn, c_new[:, :n])
        out_c = []
        for s in range(steps):
            tot = bc[:, n:]
            for j in range(taps):
                tau = s + j
                if tau < past:
                    k = far_w.index((s, tau))
                    v = far_wc[k * rows : (k + 1) * rows]
                else:
                    k = far_n.index((s, tau - past))
                    v = far_nc[k * rows : (k + 1) * rows]
                tot = tot + v * kc[j : j + 1, n:]
            out_c.append(jax.nn.silu(tot))
        c_all = jnp.concatenate(out_c, axis=0)
        c_hi, c_lo = halves(c_all)
        home = jnp.concatenate([all_cols[:, n_win + n_new + s : n_win + n_new + s + 1] for s in range(steps)], axis=0)
        zero = jnp.zeros_like(c_hi)
        for q in range(cr):
            here = home == z * cr + q
            lhs[:sr, q * n : (q + 1) * n] = jnp.where(here, c_hi, zero)
            lhs[sr:, q * n : (q + 1) * n] = jnp.where(here, c_lo, zero)

        def base_tile(j, carry):
            at = pl.ds(pl.multiple_of(j * tile, tile), tile)
            for q in range(cr):
                rhs[:, q * n : (q + 1) * n] = bank[q, at, :]
            got = lax.dot_general(lhs[...], rhs[...], (((1,), (1,)), ((), ())), preferred_element_type=F32)
            got = got[:sr] + got[sr:]
            for s in range(steps):
                for b in range(chips):
                    base[b, s * cr : (s + 1) * cr, at] = got[s * rows + b * cr : s * rows + (b + 1) * cr]
            return carry

        lax.fori_loop(0, hc // tile, base_tile, 0)
        for d in range(1, chips):
            out_b[d - 1] = base[around(d)].astype(BF)
        own_b[...] = base[z]
        b_x = [
            go(remote(out_b.at[d - 1], came_b.at[d - 1], b_s.at[d - 1], b_r.at[d - 1], around(d) * 2 + c))
            for d in range(1, chips)
        ]
        t_new[z] = gathered(1).astype(BF)
        channels = Spread([lambda b: t_new.at[b]], x_ag_s, x_ag_r)
        channels.step(0)
        scatter(0)

        move(2, 3)

        line_nb = dot_exact(pick_n, b_new[:, :n])
        line_nc = dot_exact(pick_n, c_new[:, :n])
        line_nr = dot_exact(pick_n, raw_new[:, n:])

        def coeff_line(s, tau, part_of):
            if tau < past:
                k = wins.index((s, tau))
                return line_wc[k * cr : (k + 1) * cr, part_of * n : (part_of + 1) * n]
            k = news.index((s, tau - past))
            return (line_nb, line_nc)[part_of][k * cr : (k + 1) * cr]

        def coeff(s, t, part_of):
            tot = bc[:, part_of * n : (part_of + 1) * n]
            for j in range(taps):
                tot = tot + coeff_line(s, t + j, part_of) * kc[j : j + 1, part_of * n : (part_of + 1) * n]
            return jax.nn.silu(tot)

        hp = hp_ref[c]
        rate = jnp.exp(hp[1:2])
        expand_in, final_w = [], []
        b_last = None
        for s in range(steps):
            c_now = coeff(s, s, 1)
            fade = jnp.ones((cr, LANES), F32)
            scaled, weights, bs = [None] * (s + 1), [None] * (s + 1), [None] * (s + 1)
            for t in range(s, -1, -1):
                k = news.index((s, t))
                v = line_nr[k * cr : (k + 1) * cr] + hp[0:1]
                size = jnp.maximum(v, 0.0) + jnp.log1p(jnp.exp(-jnp.abs(v)))
                weights[t] = fade * size
                bs[t] = coeff(s, t, 0)
                scaled[t] = weights[t] * jnp.sum(bs[t] * c_now, axis=1, keepdims=True)
                fade = fade * jnp.exp(-rate * size)
            expand_in += [fade] + scaled
            if s == steps - 1:
                final_w, b_last = weights, bs
        expand_in += final_w
        n_exp = len(expand_in)
        expand_in.append(jnp.broadcast_to(hp[2:3], (8, LANES)))
        spread = (
            lax.broadcasted_iota(I32, (LANES, hc), 0)
            == jnp.right_shift(lax.broadcasted_iota(I32, (LANES, hc), 1), head_shift)
        ).astype(F32)
        wide = dot_exact(jnp.concatenate(expand_in, axis=0), spread)
        wides = [wide[k * cr : (k + 1) * cr] for k in range(n_exp)]
        skip = wide[n_exp * cr : n_exp * cr + 1]

        for j in range(1, chips):
            channels.step(j)
            move(3 + (j - 1) * 1, 3 + j * 1)
        line_n[...] = dot(pick_nb, t_new[...].reshape(chips * blk, hc))

        def x_line(s, tau):
            if tau < past:
                k = wins.index((s, tau))
                return line_w[k * cr : (k + 1) * cr, :]
            k = news.index((s, tau - past))
            return line_n[k * cr : (k + 1) * cr, :]

        kx_own = kx_ref[:, half_cols(c)]
        bx_own = bx_ref[:, half_cols(c)]
        for k, (s, t) in enumerate(news):
            tot = bx_own
            for j in range(taps):
                tot = tot + x_line(s, t + j) * kx_own[j : j + 1]
            xs[k] = jax.nn.silu(tot)

        last = steps - 1
        outs = [wides[n_exp - steps + t] * xs[news.index((last, t))] for t in range(steps)]
        outs.append(jnp.concatenate([fade] + [jnp.zeros_like(fade)] * (hc // LANES - 1), axis=1))
        outs += [x_line(last, steps + j) for j in range(past)]

        @pl.when(c == 0)
        def _():
            for k, v in enumerate(outs):
                x_ref[0, k] = v[:rd]
                x_away[k] = v[rd:]
            for t in range(steps):
                bo_ref[t] = b_last[t][:rd]
            for j in range(past):
                for part_of in range(2):
                    fc_own[j * rd : (j + 1) * rd, part_of * n : (part_of + 1) * n] = coeff_line(last, steps + j, part_of)[:rd]

        @pl.when(c == 1)
        def _():
            for k, v in enumerate(outs):
                x_ref[1, k] = v[rd:]
                x_away[k] = v[:rd]
            for t in range(steps):
                bo_ref[t] = b_last[t][rd:]
            for j in range(past):
                for part_of in range(2):
                    fc_own[j * rd : (j + 1) * rd, part_of * n : (part_of + 1) * n] = coeff_line(last, steps + j, part_of)[rd:]

        x_x = go(remote(x_away, x_ref.at[c], x_s, x_r, sib))
        fc_ref[mt] = fc_own[...]
        f_x = [
            go(remote(fc_own, fc_ref.at[mt], f_s.at[k - 1], f_r.at[k - 1], me, (mt + k) % tensors))
            for k in range(1, tensors)
        ]

        for x in b_x:
            x.wait_recv()
        gate[...] = gathered(0)
        own_base = own_b[...]
        for d in range(chips - 1):
            own_base = own_base + came_b[d].astype(F32)
        ys = []
        e = 0
        for s in range(steps):
            y = wides[e] * own_base[s * cr : (s + 1) * cr] + skip * xs[news.index((s, s))]
            for t in range(s + 1):
                y = y + wides[e + 1 + t] * xs[news.index((s, t))]
            e += s + 2
            ys.append(y * jax.nn.silu(gate[s * cr : (s + 1) * cr, :]))
        y = jnp.concatenate(ys, axis=0)
        first_head = mt * (2 * hh) + c * hh
        col_head = first_head + jnp.right_shift(lax.broadcasted_iota(I32, (LANES, hc), 1), head_shift)
        col_group = col_head - jnp.left_shift(jnp.right_shift(col_head, group_shift), group_shift)
        member = (lax.broadcasted_iota(I32, (LANES, hc), 0) == col_group).astype(F32)
        own_sq = lax.dot_general(
            y * y, member, (((1,), (1,)), ((), ())), preferred_element_type=F32, precision=lax.Precision.HIGHEST
        )
        squares[...] = own_sq
        q_x = [go(remote(squares, came_q.at[0], q_s.at[0], q_r.at[0], sib))]
        for i, (k, cc) in enumerate(pairs):
            slot = 1 + (k - 1) * 2 + lax.rem(cc + c, 2)
            dst = 1 + (k - 1) * 2 + lax.rem(cc + c, 2)
            q_x.append(go(remote(squares, came_q.at[dst], q_s.at[slot], q_r.at[slot], z * 2 + cc, (mt + k) % tensors)))


        for x in q_x:
            x.wait_recv()
        tot = squares[...]
        for i in range(1 + len(pairs)):
            tot = tot + came_q[i]
        inverse = lax.rsqrt(tot / group_channels + 1e-05)
        normed[c, z] = (y * dot_exact(inverse, member) * gain_ref[:, half_cols(c)]).astype(BF)
        outputs = Spread([lambda b: normed.at[c, b]], n_s, n_r)
        outputs.step(0)

        move(6, 7)

        for j in range(1, chips):
            outputs.step(j)
            move(7 + (j - 1) * 1, 7 + j * 1)
        go(remote(normed.at[c], normed.at[c], rel_s.at[1], rel_r.at[1], sib))
        remote(normed.at[1 - c], normed.at[1 - c], rel_s.at[1], rel_r.at[1], sib).wait_recv()

        w_in.wait()
        out_tile = min(512, width)
        left = normed[0].reshape(chips * blk, hc)
        right = normed[1].reshape(chips * blk, hc)

        def project(j, carry):
            at = pl.ds(pl.multiple_of(j * out_tile, out_tile), out_tile)
            got = dot(left, w_vm[:hc, at]) + dot(right, w_vm[hc:, at])
            part[:, :, :, at] = got.reshape(chips, steps, cr, out_tile)
            return carry

        lax.fori_loop(0, width // out_tile, project, 0)

        def share(t):
            first = t * rt
            return part.at[first // cr, :, pl.ds(pl.multiple_of(first % cr, 8), rt), :]

        m_x = []
        for k in range(1, tensors):
            to = (mt + k) % tensors
            m_x.append(go(remote(share(to), came_m.at[k - 1], m_s.at[k - 1], m_r.at[k - 1], me, to)))

        move(10, 2 * count)
        mv_x = []
        for h in range(2):
            arrived(count - 1, h)
            sources = [(up_recv[e][h], cr + offs[e]) for e in range(count)]
            sources += [(dn_recv[e][h], cr + total + offs[e]) for e in range(count)]

            def final_row(i, carry, sources=sources, h=h):
                first = h * part_rows
                gather(away.at[h], i, 0, tab_ref[2, z * cr + (1 - c) * rd + i], sources, h)
                gather(moved_ref.at[:, c], i, first, tab_ref[2, z * cr + c * rd + i], sources, h)
                return carry

            lax.fori_loop(0, rd, final_row, 0)
            mv_x.append(go(remote(away.at[h], moved_ref.at[:, c, pl.ds(h * part_rows, part_rows)], mv_s.at[h], mv_r.at[h], sib)))

        for x in m_x:
            x.wait_recv()
        first = mt * rt
        tot = part[first // cr, :, pl.ds(pl.multiple_of(first % cr, 8), rt), :]
        for k in range(tensors - 1):
            tot = tot + came_m[k]
        mixed_ref[...] = tot.astype(BF)

        remote(x_away, x_ref.at[1 - c], x_s, x_r, sib).wait_recv()
        for k in range(1, tensors):
            src = (mt + tensors - k) % tensors
            remote(fc_own, fc_ref.at[src], f_s.at[k - 1], f_r.at[k - 1], me, src).wait_recv()
        for h in range(2):
            remote(away.at[h], moved_ref.at[:, 1 - c, pl.ds(h * part_rows, part_rows)], mv_s.at[h], mv_r.at[h], sib).wait_recv()
        for x in sends:
            x.wait_send()
        for drain in ends:
            drain()
        for p in range(count):
            for h in range(2):

                @pl.when(can_up)
                def _(p=p, h=h):
                    hop(p, h, 1).wait_send()

                @pl.when(can_dn)
                def _(p=p, h=h):
                    hop(p, h, -1).wait_send()

    def vm(*shape, dtype=F32):
        return pltpu.VMEM(shape, dtype)

    def sem(*shape):
        return pltpu.SemaphoreType.DMA(shape) if shape else pltpu.SemaphoreType.DMA

    slots = [vm(cap, hc // 2, n, dtype=BF) for cap in caps for h in range(2)]
    few = chips - 1
    scratch = [
        vm(2, sr, hc), vm(2, sr, hc), vm(sr, small.shape[2]),
        vm(2, few, blk, hc, dtype=BF), vm(chips, blk, small.shape[2]),
        vm(2, few, blk, hc, dtype=BF), vm(few, blk, small.shape[2]),
        vm(blk, hc),
        vm(chips, blk, hc, dtype=BF), vm(2, chips, blk, small.shape[2]),
        vm(win_pad, hc, dtype=BF), vm(win_rows, n), vm(chips, win_blk, hc, dtype=BF), vm(2, chips, win_blk, n),
        vm(*w_out.shape, dtype=BF),
        vm(2, 2, hc, n), vm(cr, hc, n, dtype=BF), vm(rd, hc, n, dtype=BF),
        *slots, *slots, *slots, *slots,
        vm(n_win * cr, hc), vm(n_new * cr, hc), vm(n_new, cr, hc),
        vm(2 * sr, cr * n, dtype=BF), vm(tile, cr * n, dtype=BF),
        vm(chips, blk, hc), vm(few, blk, hc, dtype=BF), vm(few, blk, hc, dtype=BF), vm(blk, hc),
        vm(blk, LANES), vm(1 + len(pairs), blk, LANES), vm(2, chips, blk, hc, dtype=BF),
        vm(chips, steps, cr, width), vm(tensors - 1, steps, rt, width),
        vm(2, rd, hc // 2, n, dtype=BF), vm(n_out, rd, hc), vm(past * rd, 2 * n),
        sem(2), sem(2), sem(4), sem(4), sem(2, 2, few), sem(2, 2, few), sem(), sem(),
        sem(3, few), sem(3, few), sem(2, few), sem(2, few), sem(3), sem(3), sem(few), sem(few),
        sem(1 + len(pairs)), sem(1 + len(pairs)), sem(tensors - 1), sem(tensors - 1), sem(1, 2, few), sem(1, 2, few),
        sem(tensors - 1), sem(tensors - 1), sem(), sem(), sem(2), sem(2),
        sem(len(caps), 2), sem(len(caps), 2), sem(len(caps), 2), sem(len(caps), 2),
        sem(1, 2, few), sem(1, 2, few),
    ]
    in_vm = pl.BlockSpec(memory_space=pltpu.VMEM)
    in_any = pl.BlockSpec(memory_space=pl.ANY)
    return pl.pallas_call(
        kernel,
        out_shape=(
            jax.ShapeDtypeStruct((steps, rt, width), BF),
            jax.ShapeDtypeStruct((rd, 2, hc, n), BF),
            jax.ShapeDtypeStruct((2, n_out, rd, hc), F32),
            jax.ShapeDtypeStruct((steps, rd, n), F32),
            jax.ShapeDtypeStruct((tensors, past * rd, 2 * n), F32),
        ),
        in_specs=[pl.BlockSpec(memory_space=pltpu.SMEM), in_vm, in_any, in_vm, in_vm, in_vm, in_any]
        + [in_vm] * 6
        + [in_any],
        out_specs=[in_vm] * 5,
        scratch_shapes=scratch,
        compiler_params=pltpu.CompilerParams(
            collective_id=ident, has_side_effects=True, vmem_limit_bytes=60 * 1024 * 1024
        ),
        name=f"engine{count}",
    )(tab, cols, proj, small, win, wc, state, kern_x, bias_x, kern_c, bias_c, head_par, gain, w_out)


def finish(moved, x_out, b_out, fade):
    rd, _, hc, n = moved.shape
    steps = b_out.shape[0]

    per = hc // fade.shape[2]

    def kernel(fade_ref, moved_ref, x_ref, b_ref, out_ref):
        r = pl.program_id(0)
        b_hi, b_lo = halves(jnp.concatenate([b_ref[t, pl.ds(r, 1), :] for t in range(steps)], axis=0))
        right = jnp.concatenate([b_hi, b_hi, b_lo], axis=0)
        for j in range(2):
            hi, lo = halves(jnp.concatenate([x_ref[j, t, pl.ds(r, 1), :] for t in range(steps)], axis=0))
            left = jnp.concatenate([hi, lo, hi], axis=0)
            more = lax.dot_general(left, right, (((0,), (0,)), ((), ())), preferred_element_type=F32)
            for k in range(hc // per):
                at = slice(k * per, (k + 1) * per)
                out_ref[0, j, at] = fade_ref[j, r, k] * moved_ref[0, j, at].astype(F32) + more[at]

    return pl.pallas_call(
        kernel,
        grid=(rd,),
        out_shape=jax.ShapeDtypeStruct(moved.shape, F32),
        in_specs=[
            pl.BlockSpec(memory_space=pltpu.SMEM),
            pl.BlockSpec((1, 2, hc, n), lambda r: (r, 0, 0, 0)),
            pl.BlockSpec((2, steps, rd, hc), lambda r: (0, 0, 0, 0)),
            pl.BlockSpec((steps, rd, n), lambda r: (0, 0, 0)),
        ],
        out_specs=pl.BlockSpec((1, 2, hc, n), lambda r: (r, 0, 0, 0)),
        name="finish",
    )(fade, moved, x_out, b_out)


def fetch(every, index):
    count = index.shape[0]

    def kernel(index_ref, every_ref, out_ref, sems):
        for i in range(count):
            pltpu.make_async_copy(every_ref.at[index_ref[i]], out_ref.at[i], sems.at[i]).start()
        for i in range(count):
            pltpu.make_async_copy(every_ref.at[0], out_ref.at[i], sems.at[i]).wait()

    return pl.pallas_call(
        kernel,
        out_shape=jax.ShapeDtypeStruct((count,) + every.shape[1:], every.dtype),
        in_specs=[pl.BlockSpec(memory_space=pltpu.SMEM), pl.BlockSpec(memory_space=pl.ANY)],
        out_specs=pl.BlockSpec(memory_space=pltpu.VMEM),
        scratch_shapes=[pltpu.SemaphoreType.DMA((count,))],
        name="fetch",
    )(index, every)


def local(
    hidden,
    parents,
    input_weight,
    coeff_weight,
    step_weight,
    kernel_x,
    kernel_bias_x,
    kernel_coeff,
    kernel_bias_coeff,
    step_bias,
    log_rate,
    skip_gain,
    norm_gain,
    output_weight,
    scan_state,
    window_x,
    window_coeff,
):
    rows_dev, heads, head_dim, n = scan_state.shape
    steps, rows, depth = hidden.shape
    taps = kernel_x.shape[0]
    past = taps - 1
    chans = heads * head_dim
    half = chans // 2
    replicas = lax.axis_size("replica")
    tensors = lax.axis_size("tensor")
    chips = replicas // 2
    chip_rows = 2 * rows_dev
    me = lax.axis_index("replica")
    mt = lax.axis_index("tensor")
    heads_all = heads * tensors
    groups = kernel_bias_coeff.shape[1] // n
    my_group = mt * heads * groups // heads_all
    coeff_at = my_group * n
    win_rows = past * rows_dev
    win_pad = -(-win_rows // 16) * 16

    def own_group(v):
        return lax.dynamic_slice_in_dim(v, coeff_at, n, axis=v.ndim - 1)

    tab, cols = plan(parents.astype(I32), replicas, past)

    win = window_x.transpose(1, 0, 2).reshape(win_rows, chans).astype(BF)
    win = jnp.pad(win, ((0, win_pad - win_rows), (0, 0)))
    wc = own_group(window_coeff).transpose(1, 0, 2, 3).reshape(win_rows, 2 * n)

    h = hidden.reshape(steps, chips, chip_rows, depth).transpose(1, 0, 2, 3)
    h = h.reshape(steps * rows, depth)
    proj = jnp.einsum("rd,dkc->krc", h, input_weight, preferred_element_type=F32)
    coef = jnp.einsum("rd,dkc->krc", h, own_group(coeff_weight), preferred_element_type=F32)
    raw = dot(h, step_weight).reshape(steps * rows, 2, heads // 2).transpose(1, 0, 2)
    small = jnp.concatenate([coef, jnp.pad(raw, ((0, 0), (0, 0), (0, LANES - heads // 2)))], axis=2)

    kern_c = own_group(kernel_coeff).reshape(taps, 2 * n)
    bias_c = own_group(kernel_bias_coeff).reshape(1, 2 * n)
    head_par = jnp.stack([step_bias, log_rate, skip_gain]).reshape(3, 2, heads // 2).transpose(1, 0, 2)
    head_par = jnp.pad(head_par, ((0, 0), (0, 5), (0, LANES - heads // 2)))

    operands = (
        tab, cols, proj, small, win, wc, scan_state.reshape(rows_dev, 2, half, n), kernel_x,
        kernel_bias_x.reshape(1, chans), kern_c, bias_c, head_par, norm_gain.reshape(1, chans), output_weight,
    )
    dims = dict(steps=steps, past=past, groups=groups, replicas=replicas, tensors=tensors, head_dim=head_dim)
    most = len(phase_caps(chips))
    needed = tab[3, 0]

    def slow(x_out, b_out, fade):
        every = lax.all_gather(scan_state.astype(BF).reshape(rows_dev, 2, half, n), "replica", axis=0, tiled=True)
        first = jnp.arange(rows, dtype=I32)
        for s in range(steps - 1, -1, -1):
            first = jnp.take(parents[s], first)
        return finish(fetch(every, lax.dynamic_slice_in_dim(first, me * rows_dev, rows_dev)), x_out, b_out, fade)

    def run(count, ident):
        mixed, moved, x_out, b_out, fc = engine(*operands, dims, count, ident)
        fade = x_out[:, steps, :, : heads // 2]
        if count < most:
            final = finish(moved, x_out, b_out, fade)
        else:
            final = lax.cond(
                needed > most, lambda: slow(x_out, b_out, fade), lambda: finish(moved, x_out, b_out, fade)
            )
        return mixed, final, x_out, fc

    counts = (most - 2, most - 1, most)
    mixed, final, x_out, fc = lax.switch(
        jnp.clip(needed - counts[0], 0, 2), [functools.partial(run, k, i) for i, k in enumerate(counts)]
    )
    mixed = mixed.reshape(steps, rows // tensors, -1)
    final = final.reshape(rows_dev, heads, head_dim, n)
    final_x = x_out[:, steps + 1 :].transpose(2, 1, 0, 3).reshape(rows_dev, past, chans)
    final_c = fc.reshape(groups, tensors // groups, past, rows_dev, 2, n)[:, 0]
    final_c = final_c.transpose(2, 1, 3, 0, 4).reshape(rows_dev, past, 2, groups * n)
    return (mixed, final, final_x, final_c)


def solution(mesh):
    placed = (
        P(None, None, "replica"),
        P(),
        P("replica", None, "tensor"),
        P("replica", None, None),
        P("replica", "tensor"),
        P(None, "tensor"),
        P("tensor"),
        P(),
        P(),
        P("tensor"),
        P("tensor"),
        P("tensor"),
        P("tensor"),
        P("tensor", "replica"),
        P("replica", "tensor", None, None),
        P("replica", None, "tensor"),
        P("replica", None, None, None),
    )
    return jax.shard_map(
        local,
        mesh=mesh,
        in_specs=placed,
        out_specs=(
            P(None, "tensor", "replica"),
            P("replica", "tensor", None, None),
            P("replica", None, "tensor"),
            P("replica", None, None, None),
        ),
        check_vma=False,
    )
```

```python
import functools

import jax
import jax.numpy as jnp
from jax import lax
from jax.experimental import pallas as pl
from jax.experimental.pallas import tpu as pltpu
from jax.sharding import PartitionSpec as P

BF = jnp.bfloat16
F32 = jnp.float32
I32 = jnp.int32
MESH = pl.DeviceIdType.MESH
LANES = 128


def dot(a, b):
    return jnp.dot(a, b, preferred_element_type=F32)


def dot_exact(a, b):
    return jnp.dot(a, b, preferred_element_type=F32, precision=lax.Precision.HIGHEST)


def halves(v):
    high = v.astype(BF)
    return high, (v - high.astype(F32)).astype(BF)


def shift_of(v):
    assert v & (v - 1) == 0
    return v.bit_length() - 1


def phase_caps(chips):
    return (2,) * (2 * chips - 1)


def place_lists(steps, past):
    wins = [(s, tau) for s in range(steps) for tau in range(past)]
    news = [(s, t) for s in range(steps) for t in range(s + 1)]
    return wins, news


def plan(parents, replicas, past):
    steps, rows = parents.shape
    rows_dev = rows // replicas
    chips = replicas // 2
    chip_rows = 2 * rows_dev
    chip_pad = -(-chips // 8) * 8
    width = max(rows, LANES)
    caps = phase_caps(chips)
    total = sum(caps)
    dev_shift, chip_shift = shift_of(rows_dev), shift_of(chip_rows)
    wins, news = place_lists(steps, past)

    def kernel(par_ref, tab_ref, cols_ref):
        z = lax.axis_index("replica") // 2
        lane = lax.broadcasted_iota(I32, (rows, rows), 1)
        sub = lax.broadcasted_iota(I32, (rows, rows), 0)
        eye = lane == sub
        own = lax.broadcasted_iota(I32, (rows, 1), 0)
        anc = {}
        for s in range(steps):
            anc[s, s + 1] = own
            for t in range(s, -1, -1):
                hit = jnp.where(lane == anc[s, t + 1], par_ref[t : t + 1, :], 0)
                anc[s, t] = jnp.sum(hit, axis=1, keepdims=True)
        columns = []
        for s, tau in wins:
            a = anc[s, 0]
            dev = jnp.right_shift(a, dev_shift)
            columns.append(dev * (past * rows_dev) + tau * rows_dev + (a - dev * rows_dev))
        for s, t in news:
            a = anc[s, t + 1]
            chip = jnp.right_shift(a, chip_shift)
            columns.append(chip * (steps * chip_rows) + t * chip_rows + (a - chip * chip_rows))
        columns += [anc[s, 0] for s in range(steps)]
        at = lax.broadcasted_iota(I32, (rows, LANES), 1)
        table = jnp.zeros((rows, LANES), I32)
        for k, col in enumerate(columns):
            table = jnp.where(at == k, col, table)
        cols_ref[...] = table

        last = anc[steps - 1, 0]
        hit = lane == last
        row_chip = jnp.right_shift(sub, chip_shift)
        up_to = jnp.max(jnp.where(hit, row_chip, -1), axis=0, keepdims=True)
        down_to = jnp.min(jnp.where(hit, row_chip, chips), axis=0, keepdims=True)
        q = lax.broadcasted_iota(I32, (1, rows), 1)
        q_chip = jnp.right_shift(q, chip_shift)
        q_local = q - q_chip * chip_rows
        at_chip = lax.broadcasted_iota(I32, (chip_pad, rows), 0)
        shift_down = (
            lax.broadcasted_iota(I32, (chip_pad, chip_pad), 0)
            == lax.broadcasted_iota(I32, (chip_pad, chip_pad), 1) + 1
        ).astype(F32)
        src_at = lax.broadcasted_iota(I32, (chip_pad, width), 1)

        def route(home, dest):
            have = ((home == at_chip) & (dest > at_chip)).astype(I32)
            beyond = (dest > at_chip).astype(I32)
            loc = jnp.where(home == at_chip, q_local, 0)
            key = dest * rows + (rows - 1 - q)
            key_col = jnp.sum(jnp.where(eye, key, 0), axis=1, keepdims=True)
            ahead = (key_col > key).astype(F32)
            src = jnp.zeros((chip_pad, width), I32)
            off, needed = 0, jnp.zeros((1, 1), I32)
            for p, cap in enumerate(caps):
                rank = dot(have.astype(F32), ahead).astype(I32)
                picked = have * (rank < cap).astype(I32)
                for k in range(cap):
                    chosen = jnp.where(rank == k, picked * loc, 0)
                    v = jnp.sum(chosen, axis=1, keepdims=True)
                    src = jnp.where(src_at == off + k, v, src)
                sent = picked * (1 + chip_rows + off + rank)
                came = dot(shift_down, sent.astype(F32)).astype(I32)
                loc = jnp.where(came > 0, came - 1, loc)
                have = jnp.where(came > 0, beyond, have - picked)
                off += cap
                used = jnp.max(jnp.max(picked, axis=1, keepdims=True), axis=0, keepdims=True)
                needed = jnp.where(used > 0, p + 1, needed)
            left = jnp.max(jnp.max(have, axis=1, keepdims=True), axis=0, keepdims=True)
            return src, loc, jnp.where(left > 0, len(caps) + 1, needed)

        up_src, up_loc, up_needed = route(q_chip, up_to)
        down_src, down_loc, down_needed = route(chips - 1 - q_chip, chips - 1 - down_to)

        def row_of(v, chip):
            index = lax.broadcasted_iota(I32, v.shape, 0)
            return jnp.sum(jnp.where(index == chip, v, 0), axis=0, keepdims=True)

        here_up = row_of(up_loc, z)
        here_down = row_of(down_loc, chips - 1 - z) + total
        code = jnp.where(q_chip == z, q_local, jnp.where(q_chip < z, here_up, here_down))
        code_col = jnp.sum(jnp.where(hit, code, 0), axis=1, keepdims=True)
        code_row = jnp.sum(jnp.where(eye, code_col, 0), axis=0, keepdims=True)
        tab_ref[...] = jnp.zeros(tab_ref.shape, I32)
        tab_ref[0:1, :] = row_of(up_src, z)
        tab_ref[1:2, :] = row_of(down_src, chips - 1 - z)
        tab_ref[2:3, :rows] = code_row
        tab_ref[3:4, :] = jnp.zeros((1, width), I32) + jnp.maximum(up_needed, down_needed)

    return pl.pallas_call(
        kernel,
        out_shape=(
            jax.ShapeDtypeStruct((8, width), I32),
            jax.ShapeDtypeStruct((rows, LANES), I32),
        ),
        in_specs=[pl.BlockSpec(memory_space=pltpu.VMEM)],
        out_specs=[pl.BlockSpec(memory_space=pltpu.VMEM)] * 2,
        name="plan",
    )(parents)


def engine(tab, cols, proj, small, win, wc, state, kern_x, bias_x, kern_c, bias_c, step_b, log_r, skip_g, gain, w_out, dims, count, ident):
    steps, past, groups = dims["steps"], dims["past"], dims["groups"]
    replicas, tensors = dims["replicas"], dims["tensors"]
    rows = cols.shape[0]
    rd, _, hc, n = state.shape
    chips = replicas // 2
    cr = 2 * rd
    sr = steps * rows
    blk = steps * cr
    head_dim = dims["head_dim"]
    hh = hc // head_dim
    taps = past + 1
    win_pad, win_rows = win.shape[0], past * rd
    win_blk = 2 * win_rows
    total = sum(phase_caps(chips))
    caps = phase_caps(chips)[:count]
    offs = [sum(caps[:i]) for i in range(len(caps))]
    width = w_out.shape[1]
    rt = rows // tensors
    group_channels = tensors * 2 * hc // groups
    wins, news = place_lists(steps, past)
    n_win, n_new = len(wins), len(news)
    tile = min(256, hc)
    n_out = steps + 1 + past
    pairs = [(k, cc) for k in range(1, tensors) for cc in range(2)]
    head_shift, group_shift = shift_of(head_dim), shift_of(groups)

    def kernel(
        tab_ref, cols_ref, proj_ref, small_ref, win_ref, wc_ref, state_ref, kx_ref, bx_ref, kc_ref, bc_ref,
        sb_ref, lr_ref, sg_ref, gain_ref, wout_ref,
        mixed_ref, moved_ref, x_ref, bo_ref, fc_ref,
        p_own, p_sib, s_sib, send_p, send_s, came_p, came_s, gate, t_new, t_c, w_sib, wc_sib, t_win, t_wc,
        w_vm, stage, bank, swap, *rest,
    ):
        slots = [[[rest[(k * count + p) * 2 + h] for h in range(2)] for p in range(count)] for k in range(4)]
        up_send, up_recv, dn_send, dn_recv = slots
        (
            line_w, line_n, xs, lhs, rhs, base, out_b, came_b, own_b, squares, came_q, normed, part, came_m,
            away, x_away, fc_own,
            loc_sem, stage_sem, sib_s, sib_r, win_s, win_r, swap_s, swap_r, rs_s, rs_r, ag_s, ag_r,
            rel_s, rel_r, b_s, b_r, q_s, q_r, f_s, f_r, n_s, n_r, m_s, m_r, x_s, x_r, mv_s, mv_r,
            up_s, up_r, dn_s, dn_r, x_ag_s, x_ag_r,
        ) = rest[8 * count :]
        me = lax.axis_index("replica")
        mt = lax.axis_index("tensor")
        z = me // 2
        c = me % 2
        sib = me + 1 - 2 * c

        def remote(src, dst, s, r, rep, ten=None):
            return pltpu.make_async_remote_copy(
                src_ref=src, dst_ref=dst, send_sem=s, recv_sem=r,
                device_id=(rep, mt if ten is None else ten), device_id_type=MESH,
            )

        barrier = pltpu.get_barrier_semaphore()
        for k in range(1, replicas):
            pl.semaphore_signal(barrier, inc=1, device_id=((me + k) % replicas, mt), device_id_type=MESH)
        for k, cc in pairs:
            pl.semaphore_signal(
                barrier, inc=1, device_id=(z * 2 + cc, (mt + k) % tensors), device_id_type=MESH
            )
        pl.semaphore_wait(barrier, replicas - 1 + len(pairs))

        sends = []

        def go(copy):
            copy.start()
            sends.append(copy)
            return copy

        ends = []

        class Spread:
            def __init__(self, blocks, s, r):
                self.blocks, self.s, self.r = blocks, s, r
                ends.append(self.drain)

            def copy(self, i, way, j, b):
                ref = self.blocks[i](b)
                rep = (me + (2 if way == 0 else replicas - 2)) % replicas
                return remote(ref, ref, self.s.at[i, way, j], self.r.at[i, way, j], rep)

            def each(self, j, what, sending):
                for i in range(len(self.blocks)):
                    for way in range(2):
                        if sending:
                            b = z - j if way == 0 else z + j
                            able = (b >= 0) & (z < chips - 1) if way == 0 else (b < chips) & (z > 0)
                        else:
                            b = z - 1 - j if way == 0 else z + 1 + j
                            able = b >= 0 if way == 0 else b < chips

                        @pl.when(able)
                        def _(i=i, way=way, b=b):
                            getattr(self.copy(i, way, j, b), what)()

            def step(self, j):
                if j > 0:
                    self.each(j - 1, "wait_recv", False)
                if j < chips - 1:
                    self.each(j, "start", True)

            def drain(self):
                for j in range(chips - 1):
                    self.each(j, "wait_send", True)

        def half_cols(h):
            return pl.ds(pl.multiple_of(h * hc, hc), hc)

        own_cols = pltpu.make_async_copy(proj_ref.at[:, :, half_cols(c)], p_own, loc_sem.at[0])
        own_cols.start()
        s_x = go(remote(small_ref.at[1 - c], s_sib, sib_s.at[1], sib_r.at[1], sib))
        other = pl.ds(pl.multiple_of((1 - c) * n, n), n)
        w_x = go(remote(win_ref.at[:, half_cols(1 - c)], w_sib, sib_s.at[2], sib_r.at[2], sib))
        wc_x = go(remote(wc_ref.at[:, other], wc_sib, sib_s.at[3], sib_r.at[3], sib))
        p_x = go(remote(proj_ref.at[:, :, half_cols(1 - c)], p_sib, sib_s.at[0], sib_r.at[0], sib))
        w_in = pltpu.make_async_copy(wout_ref, w_vm, loc_sem.at[1])

        def stage_in(i, slot):
            return pltpu.make_async_copy(state_ref.at[i], stage.at[slot], stage_sem.at[slot])

        stage_in(0, 0).start()

        s_x.wait_recv()
        send_s[...] = (small_ref[c] + s_sib[...]).reshape(send_s.shape)

        def around(d):
            return (z + d) % chips

        rs_x, p_sent = [], ([], [])
        for d in range(1, chips):
            rep = around(d) * 2 + c
            rs_x.append(go(remote(send_s.at[around(d)], came_s.at[d - 1], rs_s.at[2, d - 1], rs_r.at[2, d - 1], rep)))

        w_x.wait_recv()
        wc_x.wait_recv()

        def in_order(own, sibling):
            return jnp.where(c == 0, jnp.concatenate([own, sibling]), jnp.concatenate([sibling, own]))

        t_win[z] = in_order(win_ref[:win_rows, half_cols(c)].astype(F32), w_sib[:win_rows].astype(F32)).astype(BF)
        t_wc[c, z] = in_order(wc_ref[:, pl.ds(pl.multiple_of(c * n, n), n)], wc_sib[...])
        windows = Spread([lambda b: t_win.at[b], lambda b: t_wc.at[c, b]], win_s, win_r)
        windows.step(0)

        step_rows = min(hc, 256)

        def convert(i, carry):
            slot = lax.rem(i, 2)

            @pl.when(i + 1 < rd)
            def _():
                stage_in(i + 1, 1 - slot).start()

            stage_in(i, slot).wait()

            def chunk(j, carry):
                at = pl.ds(pl.multiple_of(j * step_rows, step_rows), step_rows)
                bank[c * rd + i, at, :] = stage[slot, c, at, :].astype(BF)
                swap[i, at, :] = stage[slot, 1 - c, at, :].astype(BF)
                return carry

            return lax.fori_loop(0, hc // step_rows, chunk, carry)

        lax.fori_loop(0, rd, convert, 0)
        swap_x = go(remote(swap, bank.at[pl.ds(c * rd, rd)], swap_s, swap_r, sib))
        w_in.start()

        part_rows = hc // 2
        gather_rows = min(part_rows, 128)

        def gather(dst, index, first, code, sources, h, again=False):
            def chunk(j, carry):
                at = pl.ds(pl.multiple_of(j * gather_rows, gather_rows), gather_rows)
                to = pl.ds(pl.multiple_of(first + j * gather_rows, gather_rows), gather_rows)
                if again:
                    v = dst[index, to, :]
                else:
                    whole = pl.ds(pl.multiple_of(h * part_rows + j * gather_rows, gather_rows), gather_rows)
                    v = bank[jnp.minimum(code, cr - 1), whole, :]
                for ref, off, cap in sources:
                    i = jnp.clip(code - off, 0, cap - 1)
                    v = jnp.where((code >= off) & (code < off + cap), ref[i, at, :], v)
                dst[index, to, :] = v
                return carry

            lax.fori_loop(0, part_rows // gather_rows, chunk, 0)

        can_up, can_dn = z < chips - 1, z > 0

        def hop(p, h, sign):
            send, recv, s, r = (up_send, up_recv, up_s, up_r) if sign > 0 else (dn_send, dn_recv, dn_s, dn_r)
            return remote(send[p][h], recv[p][h], s.at[p, h], r.at[p, h], (me + 2 * sign + replicas) % replicas)

        def arrived(p, h):
            @pl.when(can_dn)
            def _():
                hop(p, h, 1).wait_recv()

            @pl.when(can_up)
            def _():
                hop(p, h, -1).wait_recv()

        def move(steps_from, steps_to):
            for step in range(steps_from, steps_to):
                p, h = step // 2, step % 2
                if p > 0:
                    arrived(p - 1, h)
                elif h == 0:
                    swap_x.wait_recv()
                for row, sign, send, recv, able in ((0, 1, up_send, up_recv, can_up), (1, -1, dn_send, dn_recv, can_dn)):

                    @pl.when(able)
                    def _(p=p, h=h, row=row, sign=sign, send=send, recv=recv):
                        sources = [(recv[e][h], cr + offs[e], caps[e]) for e in range(p)]
                        for k in range(caps[p]):
                            gather(send[p][h], k, 0, tab_ref[row, offs[p] + k], sources, h)
                        hop(p, h, sign).start()

        windows.step(1)
        for x in rs_x:
            x.wait_recv()
        v = send_s[z]
        for d in range(chips - 1):
            v = v + came_s[d]
        t_c[c, z] = v
        for d in range(1, chips):
            go(remote(t_c.at[c, z], t_c.at[c, z], ag_s.at[0, d - 1], ag_r.at[0, d - 1], around(d) * 2 + c))
        for j in range(2, chips - 1):
            windows.step(j)
        move(0, 1)

        own_cols.wait()
        p_x.wait_recv()

        def chip_p(k, b):
            at = pl.ds(pl.multiple_of(b * blk, blk), blk)
            return p_own[k, at, :] + p_sib[k, at, :]

        def scatter(k):
            for d in range(1, chips):
                send_p[k, d - 1] = chip_p(k, around(d)).astype(BF)
                p_sent[k].append(
                    go(remote(send_p.at[k, d - 1], came_p.at[k, d - 1], rs_s.at[k, d - 1], rs_r.at[k, d - 1], around(d) * 2 + c))
                )

        def gathered(k):
            v = chip_p(k, z)
            for x in p_sent[k]:
                x.wait_recv()
            for d in range(chips - 1):
                v = v + came_p[k, d].astype(F32)
            return v

        scatter(1)


        for d in range(1, chips):
            src = (z + chips - d) % chips
            remote(t_c.at[c, src], t_c.at[c, src], ag_s.at[0, d - 1], ag_r.at[0, d - 1], src * 2 + c).wait_recv()
        go(remote(t_c.at[c], t_c.at[c], rel_s.at[0], rel_r.at[0], sib))
        remote(t_c.at[1 - c], t_c.at[1 - c], rel_s.at[0], rel_r.at[0], sib).wait_recv()

        windows.step(chips - 1)
        go(remote(t_wc.at[c], t_wc.at[c], rel_s.at[2], rel_r.at[2], sib))
        mine = cols_ref[pl.ds(pl.multiple_of(z * cr, cr), cr), :]

        def pick(columns, entries):
            index = jnp.concatenate(columns, axis=0)
            lane = lax.broadcasted_iota(I32, (index.shape[0], entries), 1)
            return jnp.where(index == lane, 1.0, 0.0).astype(F32)

        pick_w = pick([mine[:, k : k + 1] for k in range(n_win)], chips * win_blk)
        pick_n = pick([mine[:, n_win + k : n_win + k + 1] for k in range(n_new)], chips * blk)
        pick_wb, pick_nb = pick_w.astype(BF), pick_n.astype(BF)
        line_w[...] = dot(pick_wb, t_win[...].reshape(chips * win_blk, hc))
        remote(t_wc.at[1 - c], t_wc.at[1 - c], rel_s.at[2], rel_r.at[2], sib).wait_recv()
        wc_all = jnp.concatenate([t_wc[part_of].reshape(chips * win_blk, n) for part_of in range(2)], axis=1)
        line_wc = dot_exact(pick_w, wc_all)
        all_cols = cols_ref[...]
        far_w = [(s, tau) for s in range(steps) for tau in range(s, past)]
        pick_fw = pick([all_cols[:, s * past + tau : s * past + tau + 1] for s, tau in far_w], chips * win_blk)
        far_wc = dot_exact(pick_fw, wc_all[:, n:])

        group_at = pl.ds(pl.multiple_of((mt * groups // tensors) * n, n), n)
        kc = jnp.concatenate([kc_ref[:, part_of, group_at] for part_of in range(2)], axis=1)
        bc = jnp.concatenate([bc_ref[part_of : part_of + 1, group_at] for part_of in range(2)], axis=1)
        b_new = t_c[0].reshape(chips * blk, -1)
        c_new = t_c[1].reshape(chips * blk, -1)
        raw_new = t_c[c].reshape(chips * blk, -1)
        far_n = [(s, t) for s in range(steps) for t in range(max(0, s - past), s + 1)]
        pick_fn = pick([all_cols[:, n_win + news.index(st) : n_win + news.index(st) + 1] for st in far_n], chips * blk)
        far_nc = dot_exact(pick_fn, c_new[:, :n])
        out_c = []
        for s in range(steps):
            tot = bc[:, n:]
            for j in range(taps):
                tau = s + j
                if tau < past:
                    k = far_w.index((s, tau))
                    v = far_wc[k * rows : (k + 1) * rows]
                else:
                    k = far_n.index((s, tau - past))
                    v = far_nc[k * rows : (k + 1) * rows]
                tot = tot + v * kc[j : j + 1, n:]
            out_c.append(jax.nn.silu(tot))
        c_all = jnp.concatenate(out_c, axis=0)
        c_hi, c_lo = halves(c_all)
        home = jnp.concatenate([all_cols[:, n_win + n_new + s : n_win + n_new + s + 1] for s in range(steps)], axis=0)
        zero = jnp.zeros_like(c_hi)
        for q in range(cr):
            here = home == z * cr + q
            lhs[:sr, q * n : (q + 1) * n] = jnp.where(here, c_hi, zero)
            lhs[sr:, q * n : (q + 1) * n] = jnp.where(here, c_lo, zero)

        def base_tile(j, carry):
            at = pl.ds(pl.multiple_of(j * tile, tile), tile)
            for q in range(cr):
                rhs[:, q * n : (q + 1) * n] = bank[q, at, :]
            got = lax.dot_general(lhs[...], rhs[...], (((1,), (1,)), ((), ())), preferred_element_type=F32)
            got = got[:sr] + got[sr:]
            for s in range(steps):
                for b in range(chips):
                    base[b, s * cr : (s + 1) * cr, at] = got[s * rows + b * cr : s * rows + (b + 1) * cr]
            return carry

        lax.fori_loop(0, hc // tile, base_tile, 0)
        for d in range(1, chips):
            out_b[d - 1] = base[around(d)].astype(BF)
        own_b[...] = base[z]
        b_x = [
            go(remote(out_b.at[d - 1], came_b.at[d - 1], b_s.at[d - 1], b_r.at[d - 1], around(d) * 2 + c))
            for d in range(1, chips)
        ]
        t_new[z] = gathered(1).astype(BF)
        channels = Spread([lambda b: t_new.at[b]], x_ag_s, x_ag_r)
        channels.step(0)
        scatter(0)

        move(1, 3)

        line_nb = dot_exact(pick_n, b_new[:, :n])
        line_nc = dot_exact(pick_n, c_new[:, :n])
        line_nr = dot_exact(pick_n, raw_new[:, n:])

        def coeff_line(s, tau, part_of):
            if tau < past:
                k = wins.index((s, tau))
                return line_wc[k * cr : (k + 1) * cr, part_of * n : (part_of + 1) * n]
            k = news.index((s, tau - past))
            return (line_nb, line_nc)[part_of][k * cr : (k + 1) * cr]

        def coeff(s, t, part_of):
            tot = bc[:, part_of * n : (part_of + 1) * n]
            for j in range(taps):
                tot = tot + coeff_line(s, t + j, part_of) * kc[j : j + 1, part_of * n : (part_of + 1) * n]
            return jax.nn.silu(tot)

        every_head = jnp.concatenate([sb_ref[...], lr_ref[...], sg_ref[...]], axis=0)

        def heads_of(core):
            source = lax.broadcasted_iota(I32, (2 * hh, LANES), 0) - core * hh
            lane = lax.broadcasted_iota(I32, (2 * hh, LANES), 1)
            return dot_exact(every_head, ((source == lane) & (lane < hh)).astype(F32))

        hp = heads_of(c)
        rate = jnp.exp(hp[1:2])
        expand_in, final_w = [], []
        b_last = None
        for s in range(steps):
            c_now = coeff(s, s, 1)
            fade = jnp.ones((cr, LANES), F32)
            scaled, weights, bs = [None] * (s + 1), [None] * (s + 1), [None] * (s + 1)
            for t in range(s, -1, -1):
                k = news.index((s, t))
                v = line_nr[k * cr : (k + 1) * cr] + hp[0:1]
                size = jnp.maximum(v, 0.0) + jnp.log1p(jnp.exp(-jnp.abs(v)))
                weights[t] = fade * size
                bs[t] = coeff(s, t, 0)
                scaled[t] = weights[t] * jnp.sum(bs[t] * c_now, axis=1, keepdims=True)
                fade = fade * jnp.exp(-rate * size)
            expand_in += [fade] + scaled
            if s == steps - 1:
                final_w, b_last = weights, bs
        expand_in += final_w
        n_exp = len(expand_in)
        expand_in.append(jnp.broadcast_to(hp[2:3], (8, LANES)))
        spread = (
            lax.broadcasted_iota(I32, (LANES, hc), 0)
            == jnp.right_shift(lax.broadcasted_iota(I32, (LANES, hc), 1), head_shift)
        ).astype(F32)
        wide = dot_exact(jnp.concatenate(expand_in, axis=0), spread)
        wides = [wide[k * cr : (k + 1) * cr] for k in range(n_exp)]
        skip = wide[n_exp * cr : n_exp * cr + 1]

        for j in range(1, chips):
            channels.step(j)
            move(3 + (j - 1) * 1, 3 + j * 1)
        line_n[...] = dot(pick_nb, t_new[...].reshape(chips * blk, hc))

        def x_line(s, tau):
            if tau < past:
                k = wins.index((s, tau))
                return line_w[k * cr : (k + 1) * cr, :]
            k = news.index((s, tau - past))
            return line_n[k * cr : (k + 1) * cr, :]

        kx_own = kx_ref[:, half_cols(c)]
        bx_own = bx_ref[:, half_cols(c)]
        for k, (s, t) in enumerate(news):
            tot = bx_own
            for j in range(taps):
                tot = tot + x_line(s, t + j) * kx_own[j : j + 1]
            xs[k] = jax.nn.silu(tot)

        last = steps - 1
        outs = [wides[n_exp - steps + t] * xs[news.index((last, t))] for t in range(steps)]
        outs.append(jnp.concatenate([fade] + [jnp.zeros_like(fade)] * (hc // LANES - 1), axis=1))
        outs += [x_line(last, steps + j) for j in range(past)]

        @pl.when(c == 0)
        def _():
            for k, v in enumerate(outs):
                x_ref[0, k] = v[:rd]
                x_away[k] = v[rd:]
            for t in range(steps):
                bo_ref[t] = b_last[t][:rd]
            for j in range(past):
                for part_of in range(2):
                    fc_own[j * rd : (j + 1) * rd, part_of * n : (part_of + 1) * n] = coeff_line(last, steps + j, part_of)[:rd]

        @pl.when(c == 1)
        def _():
            for k, v in enumerate(outs):
                x_ref[1, k] = v[rd:]
                x_away[k] = v[:rd]
            for t in range(steps):
                bo_ref[t] = b_last[t][rd:]
            for j in range(past):
                for part_of in range(2):
                    fc_own[j * rd : (j + 1) * rd, part_of * n : (part_of + 1) * n] = coeff_line(last, steps + j, part_of)[rd:]

        x_x = go(remote(x_away, x_ref.at[c], x_s, x_r, sib))
        fc_ref[mt] = fc_own[...]
        f_x = [
            go(remote(fc_own, fc_ref.at[mt], f_s.at[k - 1], f_r.at[k - 1], me, (mt + k) % tensors))
            for k in range(1, tensors)
        ]

        for x in b_x:
            x.wait_recv()
        gate[...] = gathered(0)
        own_base = own_b[...]
        for d in range(chips - 1):
            own_base = own_base + came_b[d].astype(F32)
        ys = []
        e = 0
        for s in range(steps):
            y = wides[e] * own_base[s * cr : (s + 1) * cr] + skip * xs[news.index((s, s))]
            for t in range(s + 1):
                y = y + wides[e + 1 + t] * xs[news.index((s, t))]
            e += s + 2
            ys.append(y * jax.nn.silu(gate[s * cr : (s + 1) * cr, :]))
        y = jnp.concatenate(ys, axis=0)
        first_head = mt * (2 * hh) + c * hh
        col_head = first_head + jnp.right_shift(lax.broadcasted_iota(I32, (LANES, hc), 1), head_shift)
        col_group = col_head - jnp.left_shift(jnp.right_shift(col_head, group_shift), group_shift)
        member = (lax.broadcasted_iota(I32, (LANES, hc), 0) == col_group).astype(F32)
        own_sq = lax.dot_general(
            y * y, member, (((1,), (1,)), ((), ())), preferred_element_type=F32, precision=lax.Precision.HIGHEST
        )
        squares[...] = own_sq
        q_x = [go(remote(squares, came_q.at[0], q_s.at[0], q_r.at[0], sib))]
        for i, (k, cc) in enumerate(pairs):
            slot = 1 + (k - 1) * 2 + lax.rem(cc + c, 2)
            dst = 1 + (k - 1) * 2 + lax.rem(cc + c, 2)
            q_x.append(go(remote(squares, came_q.at[dst], q_s.at[slot], q_r.at[slot], z * 2 + cc, (mt + k) % tensors)))


        for x in q_x:
            x.wait_recv()
        tot = squares[...]
        for i in range(1 + len(pairs)):
            tot = tot + came_q[i]
        inverse = lax.rsqrt(tot / group_channels + 1e-05)
        normed[c, z] = (y * dot_exact(inverse, member) * gain_ref[:, half_cols(c)]).astype(BF)
        outputs = Spread([lambda b: normed.at[c, b]], n_s, n_r)
        outputs.step(0)

        move(6, 7)

        for j in range(1, chips):
            outputs.step(j)
            move(7 + (j - 1) * 1, 7 + j * 1)
        go(remote(normed.at[c], normed.at[c], rel_s.at[1], rel_r.at[1], sib))
        remote(normed.at[1 - c], normed.at[1 - c], rel_s.at[1], rel_r.at[1], sib).wait_recv()

        w_in.wait()
        out_tile = min(512, width)
        left = normed[0].reshape(chips * blk, hc)
        right = normed[1].reshape(chips * blk, hc)

        def project(j, carry):
            at = pl.ds(pl.multiple_of(j * out_tile, out_tile), out_tile)
            got = dot(left, w_vm[:hc, at]) + dot(right, w_vm[hc:, at])
            part[:, :, :, at] = got.reshape(chips, steps, cr, out_tile)
            return carry

        lax.fori_loop(0, width // out_tile, project, 0)

        def share(t):
            first = t * rt
            return part.at[first // cr, :, pl.ds(pl.multiple_of(first % cr, 8), rt), :]

        m_x = []
        for k in range(1, tensors):
            to = (mt + k) % tensors
            m_x.append(go(remote(share(to), came_m.at[k - 1], m_s.at[k - 1], m_r.at[k - 1], me, to)))

        move(10, 2 * count)
        mv_x = []

        def final_rows(h, sources, again):
            def final_row(i, carry):
                first = h * part_rows
                ours, theirs = z * cr + c * rd + i, z * cr + (1 - c) * rd + i
                gather(away.at[h], i, 0, tab_ref[2, theirs], sources, h, again)
                gather(moved_ref.at[:, c], i, first, tab_ref[2, ours], sources, h, again)
                return carry

            lax.fori_loop(0, rd, final_row, 0)

        def final_sources(h, phases):
            ups = [(up_recv[e][h], cr + offs[e], caps[e]) for e in phases]
            return ups + [(dn_recv[e][h], cr + total + offs[e], caps[e]) for e in phases]

        for h in range(2):
            final_rows(h, final_sources(h, range(count - 1)), False)
            arrived(count - 1, h)
            final_rows(h, final_sources(h, range(count - 1, count)), True)
            mv_x.append(go(remote(away.at[h], moved_ref.at[:, c, pl.ds(h * part_rows, part_rows)], mv_s.at[h], mv_r.at[h], sib)))

        for x in m_x:
            x.wait_recv()
        first = mt * rt
        tot = part[first // cr, :, pl.ds(pl.multiple_of(first % cr, 8), rt), :]
        for k in range(tensors - 1):
            tot = tot + came_m[k]
        mixed_ref[...] = tot.astype(BF)

        remote(x_away, x_ref.at[1 - c], x_s, x_r, sib).wait_recv()
        for k in range(1, tensors):
            src = (mt + tensors - k) % tensors
            remote(fc_own, fc_ref.at[src], f_s.at[k - 1], f_r.at[k - 1], me, src).wait_recv()
        for h in range(2):
            remote(away.at[h], moved_ref.at[:, 1 - c, pl.ds(h * part_rows, part_rows)], mv_s.at[h], mv_r.at[h], sib).wait_recv()
        for x in sends:
            x.wait_send()
        for drain in ends:
            drain()
        for p in range(count):
            for h in range(2):

                @pl.when(can_up)
                def _(p=p, h=h):
                    hop(p, h, 1).wait_send()

                @pl.when(can_dn)
                def _(p=p, h=h):
                    hop(p, h, -1).wait_send()

    def vm(*shape, dtype=F32):
        return pltpu.VMEM(shape, dtype)

    def sem(*shape):
        return pltpu.SemaphoreType.DMA(shape) if shape else pltpu.SemaphoreType.DMA

    slots = [vm(cap, hc // 2, n, dtype=BF) for cap in caps for h in range(2)]
    few = chips - 1
    scratch = [
        vm(2, sr, hc), vm(2, sr, hc), vm(sr, small.shape[2]),
        vm(2, few, blk, hc, dtype=BF), vm(chips, blk, small.shape[2]),
        vm(2, few, blk, hc, dtype=BF), vm(few, blk, small.shape[2]),
        vm(blk, hc),
        vm(chips, blk, hc, dtype=BF), vm(2, chips, blk, small.shape[2]),
        vm(win_pad, hc, dtype=BF), vm(win_rows, n), vm(chips, win_blk, hc, dtype=BF), vm(2, chips, win_blk, n),
        vm(*w_out.shape, dtype=BF),
        vm(2, 2, hc, n), vm(cr, hc, n, dtype=BF), vm(rd, hc, n, dtype=BF),
        *slots, *slots, *slots, *slots,
        vm(n_win * cr, hc), vm(n_new * cr, hc), vm(n_new, cr, hc),
        vm(2 * sr, cr * n, dtype=BF), vm(tile, cr * n, dtype=BF),
        vm(chips, blk, hc), vm(few, blk, hc, dtype=BF), vm(few, blk, hc, dtype=BF), vm(blk, hc),
        vm(blk, LANES), vm(1 + len(pairs), blk, LANES), vm(2, chips, blk, hc, dtype=BF),
        vm(chips, steps, cr, width), vm(tensors - 1, steps, rt, width),
        vm(2, rd, hc // 2, n, dtype=BF), vm(n_out, rd, hc), vm(past * rd, 2 * n),
        sem(2), sem(2), sem(4), sem(4), sem(2, 2, few), sem(2, 2, few), sem(), sem(),
        sem(3, few), sem(3, few), sem(2, few), sem(2, few), sem(3), sem(3), sem(few), sem(few),
        sem(1 + len(pairs)), sem(1 + len(pairs)), sem(tensors - 1), sem(tensors - 1), sem(1, 2, few), sem(1, 2, few),
        sem(tensors - 1), sem(tensors - 1), sem(), sem(), sem(2), sem(2),
        sem(len(caps), 2), sem(len(caps), 2), sem(len(caps), 2), sem(len(caps), 2),
        sem(1, 2, few), sem(1, 2, few),
    ]
    in_vm = pl.BlockSpec(memory_space=pltpu.VMEM)
    in_any = pl.BlockSpec(memory_space=pl.ANY)
    return pl.pallas_call(
        kernel,
        out_shape=(
            jax.ShapeDtypeStruct((steps, rt, width), BF),
            jax.ShapeDtypeStruct((rd, 2, hc, n), BF),
            jax.ShapeDtypeStruct((2, n_out, rd, hc), F32),
            jax.ShapeDtypeStruct((steps, rd, n), F32),
            jax.ShapeDtypeStruct((tensors, past * rd, 2 * n), F32),
        ),
        in_specs=[pl.BlockSpec(memory_space=pltpu.SMEM), in_vm, in_any, in_vm, in_vm, in_vm, in_any]
        + [in_vm] * 8
        + [in_any],
        out_specs=[in_vm] * 5,
        scratch_shapes=scratch,
        compiler_params=pltpu.CompilerParams(
            collective_id=ident, has_side_effects=True, vmem_limit_bytes=60 * 1024 * 1024
        ),
        name=f"engine{count}",
    )(tab, cols, proj, small, win, wc, state, kern_x, bias_x, kern_c, bias_c, step_b, log_r, skip_g, gain, w_out)


def finish(moved, x_out, b_out, fade):
    rd, _, hc, n = moved.shape
    steps = b_out.shape[0]

    per = hc // fade.shape[2]

    def kernel(fade_ref, moved_ref, x_ref, b_ref, out_ref):
        r = pl.program_id(0)
        b_hi, b_lo = halves(jnp.concatenate([b_ref[t, pl.ds(r, 1), :] for t in range(steps)], axis=0))
        right = jnp.concatenate([b_hi, b_hi, b_lo], axis=0)
        for j in range(2):
            hi, lo = halves(jnp.concatenate([x_ref[j, t, pl.ds(r, 1), :] for t in range(steps)], axis=0))
            left = jnp.concatenate([hi, lo, hi], axis=0)
            more = lax.dot_general(left, right, (((0,), (0,)), ((), ())), preferred_element_type=F32)
            for k in range(hc // per):
                at = slice(k * per, (k + 1) * per)
                out_ref[0, j, at] = fade_ref[j, r, k] * moved_ref[0, j, at].astype(F32) + more[at]

    return pl.pallas_call(
        kernel,
        grid=(rd,),
        out_shape=jax.ShapeDtypeStruct(moved.shape, F32),
        in_specs=[
            pl.BlockSpec(memory_space=pltpu.SMEM),
            pl.BlockSpec((1, 2, hc, n), lambda r: (r, 0, 0, 0)),
            pl.BlockSpec((2, steps, rd, hc), lambda r: (0, 0, 0, 0)),
            pl.BlockSpec((steps, rd, n), lambda r: (0, 0, 0)),
        ],
        out_specs=pl.BlockSpec((1, 2, hc, n), lambda r: (r, 0, 0, 0)),
        name="finish",
    )(fade, moved, x_out, b_out)


def fetch(every, index):
    count = index.shape[0]

    def kernel(index_ref, every_ref, out_ref, sems):
        for i in range(count):
            pltpu.make_async_copy(every_ref.at[index_ref[i]], out_ref.at[i], sems.at[i]).start()
        for i in range(count):
            pltpu.make_async_copy(every_ref.at[0], out_ref.at[i], sems.at[i]).wait()

    return pl.pallas_call(
        kernel,
        out_shape=jax.ShapeDtypeStruct((count,) + every.shape[1:], every.dtype),
        in_specs=[pl.BlockSpec(memory_space=pltpu.SMEM), pl.BlockSpec(memory_space=pl.ANY)],
        out_specs=pl.BlockSpec(memory_space=pltpu.VMEM),
        scratch_shapes=[pltpu.SemaphoreType.DMA((count,))],
        name="fetch",
    )(index, every)


def local(
    hidden,
    parents,
    input_weight,
    coeff_weight,
    step_weight,
    kernel_x,
    kernel_bias_x,
    kernel_coeff,
    kernel_bias_coeff,
    step_bias,
    log_rate,
    skip_gain,
    norm_gain,
    output_weight,
    scan_state,
    window_x,
    window_coeff,
):
    rows_dev, heads, head_dim, n = scan_state.shape
    steps, rows, depth = hidden.shape
    taps = kernel_x.shape[0]
    past = taps - 1
    chans = heads * head_dim
    half = chans // 2
    replicas = lax.axis_size("replica")
    tensors = lax.axis_size("tensor")
    chips = replicas // 2
    chip_rows = 2 * rows_dev
    me = lax.axis_index("replica")
    mt = lax.axis_index("tensor")
    heads_all = heads * tensors
    groups = kernel_bias_coeff.shape[1] // n
    my_group = mt * heads * groups // heads_all
    coeff_at = my_group * n
    win_rows = past * rows_dev
    win_pad = -(-win_rows // 16) * 16

    def own_group(v):
        return lax.dynamic_slice_in_dim(v, coeff_at, n, axis=v.ndim - 1)

    tab, cols = plan(parents.astype(I32), replicas, past)

    win = window_x.transpose(1, 0, 2).reshape(win_rows, chans).astype(BF)
    win = jnp.pad(win, ((0, win_pad - win_rows), (0, 0)))
    wc = own_group(window_coeff).transpose(1, 0, 2, 3).reshape(win_rows, 2 * n)

    h = hidden.reshape(steps, chips, chip_rows, depth).transpose(1, 0, 2, 3)
    h = h.reshape(steps * rows, depth)
    proj = jnp.einsum("rd,dkc->krc", h, input_weight, preferred_element_type=F32)
    coef = jnp.einsum("rd,dkc->krc", h, own_group(coeff_weight), preferred_element_type=F32)
    raw = dot(h, step_weight).reshape(steps * rows, 2, heads // 2).transpose(1, 0, 2)
    small = jnp.concatenate([coef, jnp.pad(raw, ((0, 0), (0, 0), (0, LANES - heads // 2)))], axis=2)

    operands = (
        tab, cols, proj, small, win, wc, scan_state.reshape(rows_dev, 2, half, n), kernel_x,
        kernel_bias_x.reshape(1, chans), kernel_coeff, kernel_bias_coeff, step_bias.reshape(1, heads),
        log_rate.reshape(1, heads), skip_gain.reshape(1, heads), norm_gain.reshape(1, chans), output_weight,
    )
    dims = dict(steps=steps, past=past, groups=groups, replicas=replicas, tensors=tensors, head_dim=head_dim)
    most = len(phase_caps(chips))
    needed = tab[3, 0]

    def slow(x_out, b_out, fade):
        every = lax.all_gather(scan_state.astype(BF).reshape(rows_dev, 2, half, n), "replica", axis=0, tiled=True)
        first = jnp.arange(rows, dtype=I32)
        for s in range(steps - 1, -1, -1):
            first = jnp.take(parents[s], first)
        return finish(fetch(every, lax.dynamic_slice_in_dim(first, me * rows_dev, rows_dev)), x_out, b_out, fade)

    def run(count, ident):
        mixed, moved, x_out, b_out, fc = engine(*operands, dims, count, ident)
        fade = x_out[:, steps, :, : heads // 2]
        if count < most:
            final = finish(moved, x_out, b_out, fade)
        else:
            final = lax.cond(
                needed > most, lambda: slow(x_out, b_out, fade), lambda: finish(moved, x_out, b_out, fade)
            )
        return mixed, final, x_out, fc

    counts = (most - 2, most - 1, most)
    mixed, final, x_out, fc = lax.switch(
        jnp.clip(needed - counts[0], 0, 2), [functools.partial(run, k, i) for i, k in enumerate(counts)]
    )
    mixed = mixed.reshape(steps, rows // tensors, -1)
    final = final.reshape(rows_dev, heads, head_dim, n)
    final_x = x_out[:, steps + 1 :].transpose(2, 1, 0, 3).reshape(rows_dev, past, chans)
    final_c = fc.reshape(groups, tensors // groups, past, rows_dev, 2, n)[:, 0]
    final_c = final_c.transpose(2, 1, 3, 0, 4).reshape(rows_dev, past, 2, groups * n)
    return (mixed, final, final_x, final_c)


def solution(mesh):
    placed = (
        P(None, None, "replica"),
        P(),
        P("replica", None, "tensor"),
        P("replica", None, None),
        P("replica", "tensor"),
        P(None, "tensor"),
        P("tensor"),
        P(),
        P(),
        P("tensor"),
        P("tensor"),
        P("tensor"),
        P("tensor"),
        P("tensor", "replica"),
        P("replica", "tensor", None, None),
        P("replica", None, "tensor"),
        P("replica", None, None, None),
    )
    return jax.shard_map(
        local,
        mesh=mesh,
        in_specs=placed,
        out_specs=(
            P(None, "tensor", "replica"),
            P("replica", "tensor", None, None),
            P("replica", None, "tensor"),
            P("replica", None, None, None),
        ),
        check_vma=False,
    )
```

```python
import functools

import jax
import jax.numpy as jnp
from jax import lax
from jax.experimental import pallas as pl
from jax.experimental.pallas import tpu as pltpu
from jax.sharding import PartitionSpec as P

BF = jnp.bfloat16
F32 = jnp.float32
I32 = jnp.int32
MESH = pl.DeviceIdType.MESH
LANES = 128


def dot(a, b):
    return jnp.dot(a, b, preferred_element_type=F32)


def dot_exact(a, b):
    return jnp.dot(a, b, preferred_element_type=F32, precision=lax.Precision.HIGHEST)


def halves(v):
    high = v.astype(BF)
    return high, (v - high.astype(F32)).astype(BF)


def shift_of(v):
    assert v & (v - 1) == 0
    return v.bit_length() - 1


def phase_caps(chips):
    return (2,) * (2 * chips - 1)


def place_lists(steps, past):
    wins = [(s, tau) for s in range(steps) for tau in range(past)]
    news = [(s, t) for s in range(steps) for t in range(s + 1)]
    return wins, news


def plan(parents, replicas, past):
    steps, rows = parents.shape
    rows_dev = rows // replicas
    chips = replicas // 2
    chip_rows = 2 * rows_dev
    chip_pad = -(-chips // 8) * 8
    width = max(rows, LANES)
    caps = phase_caps(chips)
    total = sum(caps)
    dev_shift, chip_shift = shift_of(rows_dev), shift_of(chip_rows)
    wins, news = place_lists(steps, past)

    def kernel(par_ref, tab_ref, cols_ref):
        z = lax.axis_index("replica") // 2
        lane = lax.broadcasted_iota(I32, (rows, rows), 1)
        sub = lax.broadcasted_iota(I32, (rows, rows), 0)
        eye = lane == sub
        own = lax.broadcasted_iota(I32, (rows, 1), 0)
        anc = {}
        for s in range(steps):
            anc[s, s + 1] = own
            for t in range(s, -1, -1):
                hit = jnp.where(lane == anc[s, t + 1], par_ref[t : t + 1, :], 0)
                anc[s, t] = jnp.sum(hit, axis=1, keepdims=True)
        columns = []
        for s, tau in wins:
            a = anc[s, 0]
            dev = jnp.right_shift(a, dev_shift)
            columns.append(dev * (past * rows_dev) + tau * rows_dev + (a - dev * rows_dev))
        for s, t in news:
            a = anc[s, t + 1]
            chip = jnp.right_shift(a, chip_shift)
            columns.append(chip * (steps * chip_rows) + t * chip_rows + (a - chip * chip_rows))
        columns += [anc[s, 0] for s in range(steps)]
        at = lax.broadcasted_iota(I32, (rows, LANES), 1)
        table = jnp.zeros((rows, LANES), I32)
        for k, col in enumerate(columns):
            table = jnp.where(at == k, col, table)
        cols_ref[...] = table

        last = anc[steps - 1, 0]
        hit = lane == last
        row_chip = jnp.right_shift(sub, chip_shift)
        up_to = jnp.max(jnp.where(hit, row_chip, -1), axis=0, keepdims=True)
        down_to = jnp.min(jnp.where(hit, row_chip, chips), axis=0, keepdims=True)
        q = lax.broadcasted_iota(I32, (1, rows), 1)
        q_chip = jnp.right_shift(q, chip_shift)
        q_local = q - q_chip * chip_rows
        at_chip = lax.broadcasted_iota(I32, (chip_pad, rows), 0)
        shift_down = (
            lax.broadcasted_iota(I32, (chip_pad, chip_pad), 0)
            == lax.broadcasted_iota(I32, (chip_pad, chip_pad), 1) + 1
        ).astype(F32)
        src_at = lax.broadcasted_iota(I32, (chip_pad, width), 1)

        def route(home, dest):
            have = ((home == at_chip) & (dest > at_chip)).astype(I32)
            beyond = (dest > at_chip).astype(I32)
            loc = jnp.where(home == at_chip, q_local, 0)
            key = dest * rows + (rows - 1 - q)
            key_col = jnp.sum(jnp.where(eye, key, 0), axis=1, keepdims=True)
            ahead = (key_col > key).astype(F32)
            src = jnp.zeros((chip_pad, width), I32)
            off, needed = 0, jnp.zeros((1, 1), I32)
            for p, cap in enumerate(caps):
                rank = dot(have.astype(F32), ahead).astype(I32)
                picked = have * (rank < cap).astype(I32)
                for k in range(cap):
                    chosen = jnp.where(rank == k, picked * loc, 0)
                    v = jnp.sum(chosen, axis=1, keepdims=True)
                    src = jnp.where(src_at == off + k, v, src)
                sent = picked * (1 + chip_rows + off + rank)
                came = dot(shift_down, sent.astype(F32)).astype(I32)
                loc = jnp.where(came > 0, came - 1, loc)
                have = jnp.where(came > 0, beyond, have - picked)
                off += cap
                used = jnp.max(jnp.max(picked, axis=1, keepdims=True), axis=0, keepdims=True)
                needed = jnp.where(used > 0, p + 1, needed)
                yield None
            left = jnp.max(jnp.max(have, axis=1, keepdims=True), axis=0, keepdims=True)
            yield src, loc, jnp.where(left > 0, len(caps) + 1, needed)

        both = [route(q_chip, up_to), route(chips - 1 - q_chip, chips - 1 - down_to)]
        for _ in caps:
            for one in both:
                next(one)
        (up_src, up_loc, up_needed), (down_src, down_loc, down_needed) = [next(one) for one in both]

        def row_of(v, chip):
            index = lax.broadcasted_iota(I32, v.shape, 0)
            return jnp.sum(jnp.where(index == chip, v, 0), axis=0, keepdims=True)

        here_up = row_of(up_loc, z)
        here_down = row_of(down_loc, chips - 1 - z) + total
        code = jnp.where(q_chip == z, q_local, jnp.where(q_chip < z, here_up, here_down))
        code_col = jnp.sum(jnp.where(hit, code, 0), axis=1, keepdims=True)
        code_row = jnp.sum(jnp.where(eye, code_col, 0), axis=0, keepdims=True)
        tab_ref[...] = jnp.zeros(tab_ref.shape, I32)
        tab_ref[0:1, :] = row_of(up_src, z)
        tab_ref[1:2, :] = row_of(down_src, chips - 1 - z)
        tab_ref[2:3, :rows] = code_row
        tab_ref[3:4, :] = jnp.zeros((1, width), I32) + jnp.maximum(up_needed, down_needed)

    return pl.pallas_call(
        kernel,
        out_shape=(
            jax.ShapeDtypeStruct((8, width), I32),
            jax.ShapeDtypeStruct((rows, LANES), I32),
        ),
        in_specs=[pl.BlockSpec(memory_space=pltpu.VMEM)],
        out_specs=[pl.BlockSpec(memory_space=pltpu.VMEM)] * 2,
        name="plan",
    )(parents)


def engine(tab, cols, proj, small, win, wc, state, kern_x, bias_x, kern_c, bias_c, step_b, log_r, skip_g, gain, w_out, dims, count, ident):
    steps, past, groups = dims["steps"], dims["past"], dims["groups"]
    replicas, tensors = dims["replicas"], dims["tensors"]
    rows = cols.shape[0]
    rd, _, hc, n = state.shape
    chips = replicas // 2
    cr = 2 * rd
    sr = steps * rows
    blk = steps * cr
    head_dim = dims["head_dim"]
    hh = hc // head_dim
    taps = past + 1
    win_pad, win_rows = win.shape[0], past * rd
    win_blk = 2 * win_rows
    total = sum(phase_caps(chips))
    caps = phase_caps(chips)[:count]
    offs = [sum(caps[:i]) for i in range(len(caps))]
    width = w_out.shape[1]
    rt = rows // tensors
    group_channels = tensors * 2 * hc // groups
    wins, news = place_lists(steps, past)
    n_win, n_new = len(wins), len(news)
    tile = min(256, hc)
    n_out = steps + 1 + past
    pairs = [(k, cc) for k in range(1, tensors) for cc in range(2)]
    head_shift, group_shift = shift_of(head_dim), shift_of(groups)

    def kernel(
        tab_ref, cols_ref, proj_ref, small_ref, win_ref, wc_ref, state_ref, kx_ref, bx_ref, kc_ref, bc_ref,
        sb_ref, lr_ref, sg_ref, gain_ref, wout_ref,
        mixed_ref, moved_ref, x_ref, bo_ref, fc_ref,
        p_own, p_sib, s_sib, send_p, send_s, came_p, came_s, gate, t_new, t_c, w_sib, wc_sib, t_win, t_wc,
        w_vm, stage, bank, swap, *rest,
    ):
        slots = [[[rest[(k * count + p) * 2 + h] for h in range(2)] for p in range(count)] for k in range(4)]
        up_send, up_recv, dn_send, dn_recv = slots
        (
            line_w, line_n, xs, lhs, rhs, base, out_b, came_b, own_b, squares, came_q, normed, part, came_m,
            away, x_away, fc_own,
            loc_sem, stage_sem, sib_s, sib_r, win_s, win_r, swap_s, swap_r, rs_s, rs_r, ag_s, ag_r,
            rel_s, rel_r, b_s, b_r, q_s, q_r, f_s, f_r, n_s, n_r, m_s, m_r, x_s, x_r, mv_s, mv_r,
            up_s, up_r, dn_s, dn_r, x_ag_s, x_ag_r,
        ) = rest[8 * count :]
        me = lax.axis_index("replica")
        mt = lax.axis_index("tensor")
        z = me // 2
        c = me % 2
        sib = me + 1 - 2 * c

        def remote(src, dst, s, r, rep, ten=None):
            return pltpu.make_async_remote_copy(
                src_ref=src, dst_ref=dst, send_sem=s, recv_sem=r,
                device_id=(rep, mt if ten is None else ten), device_id_type=MESH,
            )

        barrier = pltpu.get_barrier_semaphore()
        for k in range(1, replicas):
            pl.semaphore_signal(barrier, inc=1, device_id=((me + k) % replicas, mt), device_id_type=MESH)
        for k, cc in pairs:
            pl.semaphore_signal(
                barrier, inc=1, device_id=(z * 2 + cc, (mt + k) % tensors), device_id_type=MESH
            )
        pl.semaphore_wait(barrier, replicas - 1 + len(pairs))

        sends = []

        def go(copy):
            copy.start()
            sends.append(copy)
            return copy

        ends = []

        class Spread:
            def __init__(self, blocks, s, r):
                self.blocks, self.s, self.r = blocks, s, r
                ends.append(self.drain)

            def copy(self, i, way, j, b):
                ref = self.blocks[i](b)
                rep = (me + (2 if way == 0 else replicas - 2)) % replicas
                return remote(ref, ref, self.s.at[i, way, j], self.r.at[i, way, j], rep)

            def each(self, j, what, sending):
                for i in range(len(self.blocks)):
                    for way in range(2):
                        if sending:
                            b = z - j if way == 0 else z + j
                            able = (b >= 0) & (z < chips - 1) if way == 0 else (b < chips) & (z > 0)
                        else:
                            b = z - 1 - j if way == 0 else z + 1 + j
                            able = b >= 0 if way == 0 else b < chips

                        @pl.when(able)
                        def _(i=i, way=way, b=b):
                            getattr(self.copy(i, way, j, b), what)()

            def step(self, j):
                if j > 0:
                    self.each(j - 1, "wait_recv", False)
                if j < chips - 1:
                    self.each(j, "start", True)

            def drain(self):
                for j in range(chips - 1):
                    self.each(j, "wait_send", True)

        def half_cols(h):
            return pl.ds(pl.multiple_of(h * hc, hc), hc)

        own_cols = pltpu.make_async_copy(proj_ref.at[:, :, half_cols(c)], p_own, loc_sem.at[0])
        own_cols.start()
        s_x = go(remote(small_ref.at[1 - c], s_sib, sib_s.at[1], sib_r.at[1], sib))
        other = pl.ds(pl.multiple_of((1 - c) * n, n), n)
        w_x = go(remote(win_ref.at[:, half_cols(1 - c)], w_sib, sib_s.at[2], sib_r.at[2], sib))
        wc_x = go(remote(wc_ref.at[:, other], wc_sib, sib_s.at[3], sib_r.at[3], sib))
        p_x = go(remote(proj_ref.at[:, :, half_cols(1 - c)], p_sib, sib_s.at[0], sib_r.at[0], sib))
        w_in = pltpu.make_async_copy(wout_ref, w_vm, loc_sem.at[1])

        def stage_in(i, slot):
            return pltpu.make_async_copy(state_ref.at[i], stage.at[slot], stage_sem.at[slot])

        stage_in(0, 0).start()

        s_x.wait_recv()
        send_s[...] = (small_ref[c] + s_sib[...]).reshape(send_s.shape)

        def around(d):
            return (z + d) % chips

        rs_x, p_sent = [], ([], [])
        for d in range(1, chips):
            rep = around(d) * 2 + c
            rs_x.append(go(remote(send_s.at[around(d)], came_s.at[d - 1], rs_s.at[2, d - 1], rs_r.at[2, d - 1], rep)))

        w_x.wait_recv()
        wc_x.wait_recv()

        def in_order(own, sibling):
            return jnp.where(c == 0, jnp.concatenate([own, sibling]), jnp.concatenate([sibling, own]))

        t_win[z] = in_order(win_ref[:win_rows, half_cols(c)].astype(F32), w_sib[:win_rows].astype(F32)).astype(BF)
        t_wc[c, z] = in_order(wc_ref[:, pl.ds(pl.multiple_of(c * n, n), n)], wc_sib[...])
        windows = Spread([lambda b: t_win.at[b], lambda b: t_wc.at[c, b]], win_s, win_r)
        windows.step(0)

        step_rows = min(hc, 256)

        def convert(i, carry):
            slot = lax.rem(i, 2)

            @pl.when(i + 1 < rd)
            def _():
                stage_in(i + 1, 1 - slot).start()

            stage_in(i, slot).wait()

            def chunk(j, carry):
                at = pl.ds(pl.multiple_of(j * step_rows, step_rows), step_rows)
                bank[c * rd + i, at, :] = stage[slot, c, at, :].astype(BF)
                swap[i, at, :] = stage[slot, 1 - c, at, :].astype(BF)
                return carry

            return lax.fori_loop(0, hc // step_rows, chunk, carry)

        lax.fori_loop(0, rd, convert, 0)
        swap_x = go(remote(swap, bank.at[pl.ds(c * rd, rd)], swap_s, swap_r, sib))
        w_in.start()

        part_rows = hc // 2
        gather_rows = min(part_rows, 128)

        def gather(dst, index, first, code, sources, h, again=False):
            def chunk(j, carry):
                at = pl.ds(pl.multiple_of(j * gather_rows, gather_rows), gather_rows)
                to = pl.ds(pl.multiple_of(first + j * gather_rows, gather_rows), gather_rows)
                if again:
                    v = dst[index, to, :]
                else:
                    whole = pl.ds(pl.multiple_of(h * part_rows + j * gather_rows, gather_rows), gather_rows)
                    v = bank[jnp.minimum(code, cr - 1), whole, :]
                for ref, off, cap in sources:
                    i = jnp.clip(code - off, 0, cap - 1)
                    v = jnp.where((code >= off) & (code < off + cap), ref[i, at, :], v)
                dst[index, to, :] = v
                return carry

            lax.fori_loop(0, part_rows // gather_rows, chunk, 0)

        can_up, can_dn = z < chips - 1, z > 0

        def hop(p, h, sign):
            send, recv, s, r = (up_send, up_recv, up_s, up_r) if sign > 0 else (dn_send, dn_recv, dn_s, dn_r)
            return remote(send[p][h], recv[p][h], s.at[p, h], r.at[p, h], (me + 2 * sign + replicas) % replicas)

        def arrived(p, h):
            @pl.when(can_dn)
            def _():
                hop(p, h, 1).wait_recv()

            @pl.when(can_up)
            def _():
                hop(p, h, -1).wait_recv()

        def move(steps_from, steps_to):
            for step in range(steps_from, steps_to):
                p, h = step // 2, step % 2
                if p > 0:
                    arrived(p - 1, h)
                elif h == 0:
                    swap_x.wait_recv()
                for row, sign, send, recv, able in ((0, 1, up_send, up_recv, can_up), (1, -1, dn_send, dn_recv, can_dn)):

                    @pl.when(able)
                    def _(p=p, h=h, row=row, sign=sign, send=send, recv=recv):
                        sources = [(recv[e][h], cr + offs[e], caps[e]) for e in range(p)]
                        for k in range(caps[p]):
                            gather(send[p][h], k, 0, tab_ref[row, offs[p] + k], sources, h)
                        hop(p, h, sign).start()

        windows.step(1)
        for x in rs_x:
            x.wait_recv()
        v = send_s[z]
        for d in range(chips - 1):
            v = v + came_s[d]
        t_c[c, z] = v
        for d in range(1, chips):
            go(remote(t_c.at[c, z], t_c.at[c, z], ag_s.at[0, d - 1], ag_r.at[0, d - 1], around(d) * 2 + c))
        for j in range(2, chips - 1):
            windows.step(j)
        move(0, 1)

        own_cols.wait()
        p_x.wait_recv()

        def chip_p(k, b):
            at = pl.ds(pl.multiple_of(b * blk, blk), blk)
            return p_own[k, at, :] + p_sib[k, at, :]

        def scatter(k):
            for d in range(1, chips):
                send_p[k, d - 1] = chip_p(k, around(d)).astype(BF)
                p_sent[k].append(
                    go(remote(send_p.at[k, d - 1], came_p.at[k, d - 1], rs_s.at[k, d - 1], rs_r.at[k, d - 1], around(d) * 2 + c))
                )

        def gathered(k):
            v = chip_p(k, z)
            for x in p_sent[k]:
                x.wait_recv()
            for d in range(chips - 1):
                v = v + came_p[k, d].astype(F32)
            return v

        scatter(1)


        for d in range(1, chips):
            src = (z + chips - d) % chips
            remote(t_c.at[c, src], t_c.at[c, src], ag_s.at[0, d - 1], ag_r.at[0, d - 1], src * 2 + c).wait_recv()
        go(remote(t_c.at[c], t_c.at[c], rel_s.at[0], rel_r.at[0], sib))
        remote(t_c.at[1 - c], t_c.at[1 - c], rel_s.at[0], rel_r.at[0], sib).wait_recv()

        windows.step(chips - 1)
        go(remote(t_wc.at[c], t_wc.at[c], rel_s.at[2], rel_r.at[2], sib))
        mine = cols_ref[pl.ds(pl.multiple_of(z * cr, cr), cr), :]

        def pick(columns, entries):
            index = jnp.concatenate(columns, axis=0)
            lane = lax.broadcasted_iota(I32, (index.shape[0], entries), 1)
            return jnp.where(index == lane, 1.0, 0.0).astype(F32)

        pick_w = pick([mine[:, k : k + 1] for k in range(n_win)], chips * win_blk)
        pick_n = pick([mine[:, n_win + k : n_win + k + 1] for k in range(n_new)], chips * blk)
        pick_wb, pick_nb = pick_w.astype(BF), pick_n.astype(BF)
        line_w[...] = dot(pick_wb, t_win[...].reshape(chips * win_blk, hc))
        remote(t_wc.at[1 - c], t_wc.at[1 - c], rel_s.at[2], rel_r.at[2], sib).wait_recv()
        wc_all = jnp.concatenate([t_wc[part_of].reshape(chips * win_blk, n) for part_of in range(2)], axis=1)
        line_wc = dot_exact(pick_w, wc_all)
        all_cols = cols_ref[...]
        far_w = [(s, tau) for s in range(steps) for tau in range(s, past)]
        pick_fw = pick([all_cols[:, s * past + tau : s * past + tau + 1] for s, tau in far_w], chips * win_blk)
        far_wc = dot_exact(pick_fw, wc_all[:, n:])

        group_at = pl.ds(pl.multiple_of((mt * groups // tensors) * n, n), n)
        kc = jnp.concatenate([kc_ref[:, part_of, group_at] for part_of in range(2)], axis=1)
        bc = jnp.concatenate([bc_ref[part_of : part_of + 1, group_at] for part_of in range(2)], axis=1)
        b_new = t_c[0].reshape(chips * blk, -1)
        c_new = t_c[1].reshape(chips * blk, -1)
        raw_new = t_c[c].reshape(chips * blk, -1)
        far_n = [(s, t) for s in range(steps) for t in range(max(0, s - past), s + 1)]
        pick_fn = pick([all_cols[:, n_win + news.index(st) : n_win + news.index(st) + 1] for st in far_n], chips * blk)
        far_nc = dot_exact(pick_fn, c_new[:, :n])
        out_c = []
        for s in range(steps):
            tot = bc[:, n:]
            for j in range(taps):
                tau = s + j
                if tau < past:
                    k = far_w.index((s, tau))
                    v = far_wc[k * rows : (k + 1) * rows]
                else:
                    k = far_n.index((s, tau - past))
                    v = far_nc[k * rows : (k + 1) * rows]
                tot = tot + v * kc[j : j + 1, n:]
            out_c.append(jax.nn.silu(tot))
        c_all = jnp.concatenate(out_c, axis=0)
        c_hi, c_lo = halves(c_all)
        home = jnp.concatenate([all_cols[:, n_win + n_new + s : n_win + n_new + s + 1] for s in range(steps)], axis=0)
        zero = jnp.zeros_like(c_hi)
        for q in range(cr):
            here = home == z * cr + q
            lhs[:sr, q * n : (q + 1) * n] = jnp.where(here, c_hi, zero)
            lhs[sr:, q * n : (q + 1) * n] = jnp.where(here, c_lo, zero)

        def base_tile(j, carry):
            at = pl.ds(pl.multiple_of(j * tile, tile), tile)
            for q in range(cr):
                rhs[:, q * n : (q + 1) * n] = bank[q, at, :]
            got = lax.dot_general(lhs[...], rhs[...], (((1,), (1,)), ((), ())), preferred_element_type=F32)
            got = got[:sr] + got[sr:]
            for s in range(steps):
                for b in range(chips):
                    base[b, s * cr : (s + 1) * cr, at] = got[s * rows + b * cr : s * rows + (b + 1) * cr]
            return carry

        lax.fori_loop(0, hc // tile, base_tile, 0)
        for d in range(1, chips):
            out_b[d - 1] = base[around(d)].astype(BF)
        own_b[...] = base[z]
        b_x = [
            go(remote(out_b.at[d - 1], came_b.at[d - 1], b_s.at[d - 1], b_r.at[d - 1], around(d) * 2 + c))
            for d in range(1, chips)
        ]
        t_new[z] = gathered(1).astype(BF)
        channels = Spread([lambda b: t_new.at[b]], x_ag_s, x_ag_r)
        channels.step(0)
        scatter(0)

        move(1, 3)

        line_nb = dot_exact(pick_n, b_new[:, :n])
        line_nc = dot_exact(pick_n, c_new[:, :n])
        line_nr = dot_exact(pick_n, raw_new[:, n:])

        def coeff_line(s, tau, part_of):
            if tau < past:
                k = wins.index((s, tau))
                return line_wc[k * cr : (k + 1) * cr, part_of * n : (part_of + 1) * n]
            k = news.index((s, tau - past))
            return (line_nb, line_nc)[part_of][k * cr : (k + 1) * cr]

        def coeff(s, t, part_of):
            tot = bc[:, part_of * n : (part_of + 1) * n]
            for j in range(taps):
                tot = tot + coeff_line(s, t + j, part_of) * kc[j : j + 1, part_of * n : (part_of + 1) * n]
            return jax.nn.silu(tot)

        every_head = jnp.concatenate([sb_ref[...], lr_ref[...], sg_ref[...]], axis=0)

        def heads_of(core):
            source = lax.broadcasted_iota(I32, (2 * hh, LANES), 0) - core * hh
            lane = lax.broadcasted_iota(I32, (2 * hh, LANES), 1)
            return dot_exact(every_head, ((source == lane) & (lane < hh)).astype(F32))

        hp = heads_of(c)
        rate = jnp.exp(hp[1:2])
        expand_in, final_w = [], []
        b_last = None
        for s in range(steps):
            c_now = coeff(s, s, 1)
            fade = jnp.ones((cr, LANES), F32)
            scaled, weights, bs = [None] * (s + 1), [None] * (s + 1), [None] * (s + 1)
            for t in range(s, -1, -1):
                k = news.index((s, t))
                v = line_nr[k * cr : (k + 1) * cr] + hp[0:1]
                size = jnp.maximum(v, 0.0) + jnp.log1p(jnp.exp(-jnp.abs(v)))
                weights[t] = fade * size
                bs[t] = coeff(s, t, 0)
                scaled[t] = weights[t] * jnp.sum(bs[t] * c_now, axis=1, keepdims=True)
                fade = fade * jnp.exp(-rate * size)
            expand_in += [fade] + scaled
            if s == steps - 1:
                final_w, b_last = weights, bs
        expand_in += final_w
        n_exp = len(expand_in)
        expand_in.append(jnp.broadcast_to(hp[2:3], (8, LANES)))
        spread = (
            lax.broadcasted_iota(I32, (LANES, hc), 0)
            == jnp.right_shift(lax.broadcasted_iota(I32, (LANES, hc), 1), head_shift)
        ).astype(F32)
        wide = dot_exact(jnp.concatenate(expand_in, axis=0), spread)
        wides = [wide[k * cr : (k + 1) * cr] for k in range(n_exp)]
        skip = wide[n_exp * cr : n_exp * cr + 1]

        for j in range(1, chips):
            channels.step(j)
            move(3 + (j - 1) * 1, 3 + j * 1)
        line_n[...] = dot(pick_nb, t_new[...].reshape(chips * blk, hc))

        def x_line(s, tau):
            if tau < past:
                k = wins.index((s, tau))
                return line_w[k * cr : (k + 1) * cr, :]
            k = news.index((s, tau - past))
            return line_n[k * cr : (k + 1) * cr, :]

        kx_own = kx_ref[:, half_cols(c)]
        bx_own = bx_ref[:, half_cols(c)]
        for k, (s, t) in enumerate(news):
            tot = bx_own
            for j in range(taps):
                tot = tot + x_line(s, t + j) * kx_own[j : j + 1]
            xs[k] = jax.nn.silu(tot)

        last = steps - 1
        outs = [wides[n_exp - steps + t] * xs[news.index((last, t))] for t in range(steps)]
        outs.append(jnp.concatenate([fade] + [jnp.zeros_like(fade)] * (hc // LANES - 1), axis=1))
        outs += [x_line(last, steps + j) for j in range(past)]

        @pl.when(c == 0)
        def _():
            for k, v in enumerate(outs):
                x_ref[0, k] = v[:rd]
                x_away[k] = v[rd:]
            for t in range(steps):
                bo_ref[t] = b_last[t][:rd]
            for j in range(past):
                for part_of in range(2):
                    fc_own[j * rd : (j + 1) * rd, part_of * n : (part_of + 1) * n] = coeff_line(last, steps + j, part_of)[:rd]

        @pl.when(c == 1)
        def _():
            for k, v in enumerate(outs):
                x_ref[1, k] = v[rd:]
                x_away[k] = v[:rd]
            for t in range(steps):
                bo_ref[t] = b_last[t][rd:]
            for j in range(past):
                for part_of in range(2):
                    fc_own[j * rd : (j + 1) * rd, part_of * n : (part_of + 1) * n] = coeff_line(last, steps + j, part_of)[rd:]

        x_x = go(remote(x_away, x_ref.at[c], x_s, x_r, sib))
        fc_ref[mt] = fc_own[...]
        f_x = [
            go(remote(fc_own, fc_ref.at[mt], f_s.at[k - 1], f_r.at[k - 1], me, (mt + k) % tensors))
            for k in range(1, tensors)
        ]

        for x in b_x:
            x.wait_recv()
        gate[...] = gathered(0)
        own_base = own_b[...]
        for d in range(chips - 1):
            own_base = own_base + came_b[d].astype(F32)
        ys = []
        e = 0
        for s in range(steps):
            y = wides[e] * own_base[s * cr : (s + 1) * cr] + skip * xs[news.index((s, s))]
            for t in range(s + 1):
                y = y + wides[e + 1 + t] * xs[news.index((s, t))]
            e += s + 2
            ys.append(y * jax.nn.silu(gate[s * cr : (s + 1) * cr, :]))
        y = jnp.concatenate(ys, axis=0)
        first_head = mt * (2 * hh) + c * hh
        col_head = first_head + jnp.right_shift(lax.broadcasted_iota(I32, (LANES, hc), 1), head_shift)
        col_group = col_head - jnp.left_shift(jnp.right_shift(col_head, group_shift), group_shift)
        member = (lax.broadcasted_iota(I32, (LANES, hc), 0) == col_group).astype(F32)
        own_sq = lax.dot_general(
            y * y, member, (((1,), (1,)), ((), ())), preferred_element_type=F32, precision=lax.Precision.HIGHEST
        )
        squares[...] = own_sq
        q_x = [go(remote(squares, came_q.at[0], q_s.at[0], q_r.at[0], sib))]
        for i, (k, cc) in enumerate(pairs):
            slot = 1 + (k - 1) * 2 + lax.rem(cc + c, 2)
            dst = 1 + (k - 1) * 2 + lax.rem(cc + c, 2)
            q_x.append(go(remote(squares, came_q.at[dst], q_s.at[slot], q_r.at[slot], z * 2 + cc, (mt + k) % tensors)))


        for x in q_x:
            x.wait_recv()
        tot = squares[...]
        for i in range(1 + len(pairs)):
            tot = tot + came_q[i]
        inverse = lax.rsqrt(tot / group_channels + 1e-05)
        normed[c, z] = (y * dot_exact(inverse, member) * gain_ref[:, half_cols(c)]).astype(BF)
        outputs = Spread([lambda b: normed.at[c, b]], n_s, n_r)
        outputs.step(0)

        move(6, 7)

        for j in range(1, chips):
            outputs.step(j)
            move(7 + (j - 1) * 1, 7 + j * 1)
        go(remote(normed.at[c], normed.at[c], rel_s.at[1], rel_r.at[1], sib))
        remote(normed.at[1 - c], normed.at[1 - c], rel_s.at[1], rel_r.at[1], sib).wait_recv()

        w_in.wait()
        out_tile = min(512, width)
        left = normed[0].reshape(chips * blk, hc)
        right = normed[1].reshape(chips * blk, hc)

        def project(j, carry):
            at = pl.ds(pl.multiple_of(j * out_tile, out_tile), out_tile)
            got = dot(left, w_vm[:hc, at]) + dot(right, w_vm[hc:, at])
            part[:, :, :, at] = got.reshape(chips, steps, cr, out_tile)
            return carry

        lax.fori_loop(0, width // out_tile, project, 0)

        def share(t):
            first = t * rt
            return part.at[first // cr, :, pl.ds(pl.multiple_of(first % cr, 8), rt), :]

        m_x = []
        for k in range(1, tensors):
            to = (mt + k) % tensors
            m_x.append(go(remote(share(to), came_m.at[k - 1], m_s.at[k - 1], m_r.at[k - 1], me, to)))

        move(10, 2 * count)
        mv_x = []

        def final_rows(h, sources, again):
            def final_row(i, carry):
                first = h * part_rows
                ours, theirs = z * cr + c * rd + i, z * cr + (1 - c) * rd + i
                gather(away.at[h], i, 0, tab_ref[2, theirs], sources, h, again)
                gather(moved_ref.at[:, c], i, first, tab_ref[2, ours], sources, h, again)
                return carry

            lax.fori_loop(0, rd, final_row, 0)

        def final_sources(h, phases):
            ups = [(up_recv[e][h], cr + offs[e], caps[e]) for e in phases]
            return ups + [(dn_recv[e][h], cr + total + offs[e], caps[e]) for e in phases]

        for h in range(2):
            final_rows(h, final_sources(h, range(count - 1)), False)
            arrived(count - 1, h)
            final_rows(h, final_sources(h, range(count - 1, count)), True)
            mv_x.append(go(remote(away.at[h], moved_ref.at[:, c, pl.ds(h * part_rows, part_rows)], mv_s.at[h], mv_r.at[h], sib)))

        for x in m_x:
            x.wait_recv()
        first = mt * rt
        tot = part[first // cr, :, pl.ds(pl.multiple_of(first % cr, 8), rt), :]
        for k in range(tensors - 1):
            tot = tot + came_m[k]
        mixed_ref[...] = tot.astype(BF)

        remote(x_away, x_ref.at[1 - c], x_s, x_r, sib).wait_recv()
        for k in range(1, tensors):
            src = (mt + tensors - k) % tensors
            remote(fc_own, fc_ref.at[src], f_s.at[k - 1], f_r.at[k - 1], me, src).wait_recv()
        for h in range(2):
            remote(away.at[h], moved_ref.at[:, 1 - c, pl.ds(h * part_rows, part_rows)], mv_s.at[h], mv_r.at[h], sib).wait_recv()
        for x in sends:
            x.wait_send()
        for drain in ends:
            drain()
        for p in range(count):
            for h in range(2):

                @pl.when(can_up)
                def _(p=p, h=h):
                    hop(p, h, 1).wait_send()

                @pl.when(can_dn)
                def _(p=p, h=h):
                    hop(p, h, -1).wait_send()

    def vm(*shape, dtype=F32):
        return pltpu.VMEM(shape, dtype)

    def sem(*shape):
        return pltpu.SemaphoreType.DMA(shape) if shape else pltpu.SemaphoreType.DMA

    slots = [vm(cap, hc // 2, n, dtype=BF) for cap in caps for h in range(2)]
    few = chips - 1
    scratch = [
        vm(2, sr, hc), vm(2, sr, hc), vm(sr, small.shape[2]),
        vm(2, few, blk, hc, dtype=BF), vm(chips, blk, small.shape[2]),
        vm(2, few, blk, hc, dtype=BF), vm(few, blk, small.shape[2]),
        vm(blk, hc),
        vm(chips, blk, hc, dtype=BF), vm(2, chips, blk, small.shape[2]),
        vm(win_pad, hc, dtype=BF), vm(win_rows, n), vm(chips, win_blk, hc, dtype=BF), vm(2, chips, win_blk, n),
        vm(*w_out.shape, dtype=BF),
        vm(2, 2, hc, n), vm(cr, hc, n, dtype=BF), vm(rd, hc, n, dtype=BF),
        *slots, *slots, *slots, *slots,
        vm(n_win * cr, hc), vm(n_new * cr, hc), vm(n_new, cr, hc),
        vm(2 * sr, cr * n, dtype=BF), vm(tile, cr * n, dtype=BF),
        vm(chips, blk, hc), vm(few, blk, hc, dtype=BF), vm(few, blk, hc, dtype=BF), vm(blk, hc),
        vm(blk, LANES), vm(1 + len(pairs), blk, LANES), vm(2, chips, blk, hc, dtype=BF),
        vm(chips, steps, cr, width), vm(tensors - 1, steps, rt, width),
        vm(2, rd, hc // 2, n, dtype=BF), vm(n_out, rd, hc), vm(past * rd, 2 * n),
        sem(2), sem(2), sem(4), sem(4), sem(2, 2, few), sem(2, 2, few), sem(), sem(),
        sem(3, few), sem(3, few), sem(2, few), sem(2, few), sem(3), sem(3), sem(few), sem(few),
        sem(1 + len(pairs)), sem(1 + len(pairs)), sem(tensors - 1), sem(tensors - 1), sem(1, 2, few), sem(1, 2, few),
        sem(tensors - 1), sem(tensors - 1), sem(), sem(), sem(2), sem(2),
        sem(len(caps), 2), sem(len(caps), 2), sem(len(caps), 2), sem(len(caps), 2),
        sem(1, 2, few), sem(1, 2, few),
    ]
    in_vm = pl.BlockSpec(memory_space=pltpu.VMEM)
    in_any = pl.BlockSpec(memory_space=pl.ANY)
    return pl.pallas_call(
        kernel,
        out_shape=(
            jax.ShapeDtypeStruct((steps, rt, width), BF),
            jax.ShapeDtypeStruct((rd, 2, hc, n), BF),
            jax.ShapeDtypeStruct((2, n_out, rd, hc), F32),
            jax.ShapeDtypeStruct((steps, rd, n), F32),
            jax.ShapeDtypeStruct((tensors, past * rd, 2 * n), F32),
        ),
        in_specs=[pl.BlockSpec(memory_space=pltpu.SMEM), in_vm, in_any, in_vm, in_vm, in_vm, in_any]
        + [in_vm] * 8
        + [in_any],
        out_specs=[in_vm] * 5,
        scratch_shapes=scratch,
        compiler_params=pltpu.CompilerParams(
            collective_id=ident, has_side_effects=True, vmem_limit_bytes=60 * 1024 * 1024
        ),
        name=f"engine{count}",
    )(tab, cols, proj, small, win, wc, state, kern_x, bias_x, kern_c, bias_c, step_b, log_r, skip_g, gain, w_out)


def finish(moved, x_out, b_out, fade):
    rd, _, hc, n = moved.shape
    steps = b_out.shape[0]

    per = hc // fade.shape[2]

    def kernel(fade_ref, moved_ref, x_ref, b_ref, out_ref):
        r = pl.program_id(0)
        b_hi, b_lo = halves(jnp.concatenate([b_ref[t, pl.ds(r, 1), :] for t in range(steps)], axis=0))
        right = jnp.concatenate([b_hi, b_hi, b_lo], axis=0)
        for j in range(2):
            hi, lo = halves(jnp.concatenate([x_ref[j, t, pl.ds(r, 1), :] for t in range(steps)], axis=0))
            left = jnp.concatenate([hi, lo, hi], axis=0)
            more = lax.dot_general(left, right, (((0,), (0,)), ((), ())), preferred_element_type=F32)
            for k in range(hc // per):
                at = slice(k * per, (k + 1) * per)
                out_ref[0, j, at] = fade_ref[j, r, k] * moved_ref[0, j, at].astype(F32) + more[at]

    return pl.pallas_call(
        kernel,
        grid=(rd,),
        out_shape=jax.ShapeDtypeStruct(moved.shape, F32),
        in_specs=[
            pl.BlockSpec(memory_space=pltpu.SMEM),
            pl.BlockSpec((1, 2, hc, n), lambda r: (r, 0, 0, 0)),
            pl.BlockSpec((2, steps, rd, hc), lambda r: (0, 0, 0, 0)),
            pl.BlockSpec((steps, rd, n), lambda r: (0, 0, 0)),
        ],
        out_specs=pl.BlockSpec((1, 2, hc, n), lambda r: (r, 0, 0, 0)),
        name="finish",
    )(fade, moved, x_out, b_out)


def fetch(every, index):
    count = index.shape[0]

    def kernel(index_ref, every_ref, out_ref, sems):
        for i in range(count):
            pltpu.make_async_copy(every_ref.at[index_ref[i]], out_ref.at[i], sems.at[i]).start()
        for i in range(count):
            pltpu.make_async_copy(every_ref.at[0], out_ref.at[i], sems.at[i]).wait()

    return pl.pallas_call(
        kernel,
        out_shape=jax.ShapeDtypeStruct((count,) + every.shape[1:], every.dtype),
        in_specs=[pl.BlockSpec(memory_space=pltpu.SMEM), pl.BlockSpec(memory_space=pl.ANY)],
        out_specs=pl.BlockSpec(memory_space=pltpu.VMEM),
        scratch_shapes=[pltpu.SemaphoreType.DMA((count,))],
        name="fetch",
    )(index, every)


def local(
    hidden,
    parents,
    input_weight,
    coeff_weight,
    step_weight,
    kernel_x,
    kernel_bias_x,
    kernel_coeff,
    kernel_bias_coeff,
    step_bias,
    log_rate,
    skip_gain,
    norm_gain,
    output_weight,
    scan_state,
    window_x,
    window_coeff,
):
    rows_dev, heads, head_dim, n = scan_state.shape
    steps, rows, depth = hidden.shape
    taps = kernel_x.shape[0]
    past = taps - 1
    chans = heads * head_dim
    half = chans // 2
    replicas = lax.axis_size("replica")
    tensors = lax.axis_size("tensor")
    chips = replicas // 2
    chip_rows = 2 * rows_dev
    me = lax.axis_index("replica")
    mt = lax.axis_index("tensor")
    heads_all = heads * tensors
    groups = kernel_bias_coeff.shape[1] // n
    my_group = mt * heads * groups // heads_all
    coeff_at = my_group * n
    win_rows = past * rows_dev
    win_pad = -(-win_rows // 16) * 16

    def own_group(v):
        return lax.dynamic_slice_in_dim(v, coeff_at, n, axis=v.ndim - 1)

    tab, cols = plan(parents.astype(I32), replicas, past)

    win = window_x.transpose(1, 0, 2).reshape(win_rows, chans).astype(BF)
    win = jnp.pad(win, ((0, win_pad - win_rows), (0, 0)))
    wc = own_group(window_coeff).transpose(1, 0, 2, 3).reshape(win_rows, 2 * n)

    h = hidden.reshape(steps, chips, chip_rows, depth).transpose(1, 0, 2, 3)
    h = h.reshape(steps * rows, depth)
    proj = jnp.einsum("rd,dkc->krc", h, input_weight, preferred_element_type=F32)
    coef = jnp.einsum("rd,dkc->krc", h, own_group(coeff_weight), preferred_element_type=F32)
    raw = dot(h, step_weight).reshape(steps * rows, 2, heads // 2).transpose(1, 0, 2)
    small = jnp.concatenate([coef, jnp.pad(raw, ((0, 0), (0, 0), (0, LANES - heads // 2)))], axis=2)

    operands = (
        tab, cols, proj, small, win, wc, scan_state.reshape(rows_dev, 2, half, n), kernel_x,
        kernel_bias_x.reshape(1, chans), kernel_coeff, kernel_bias_coeff, step_bias.reshape(1, heads),
        log_rate.reshape(1, heads), skip_gain.reshape(1, heads), norm_gain.reshape(1, chans), output_weight,
    )
    dims = dict(steps=steps, past=past, groups=groups, replicas=replicas, tensors=tensors, head_dim=head_dim)
    most = len(phase_caps(chips))
    needed = tab[3, 0]

    def slow(x_out, b_out, fade):
        every = lax.all_gather(scan_state.astype(BF).reshape(rows_dev, 2, half, n), "replica", axis=0, tiled=True)
        first = jnp.arange(rows, dtype=I32)
        for s in range(steps - 1, -1, -1):
            first = jnp.take(parents[s], first)
        return finish(fetch(every, lax.dynamic_slice_in_dim(first, me * rows_dev, rows_dev)), x_out, b_out, fade)

    def run(count, ident):
        mixed, moved, x_out, b_out, fc = engine(*operands, dims, count, ident)
        fade = x_out[:, steps, :, : heads // 2]
        if count < most:
            final = finish(moved, x_out, b_out, fade)
        else:
            final = lax.cond(
                needed > most, lambda: slow(x_out, b_out, fade), lambda: finish(moved, x_out, b_out, fade)
            )
        return mixed, final, x_out, fc

    counts = (most - 2, most - 1, most)
    mixed, final, x_out, fc = lax.switch(
        jnp.clip(needed - counts[0], 0, 2), [functools.partial(run, k, i) for i, k in enumerate(counts)]
    )
    mixed = mixed.reshape(steps, rows // tensors, -1)
    final = final.reshape(rows_dev, heads, head_dim, n)
    final_x = x_out[:, steps + 1 :].transpose(2, 1, 0, 3).reshape(rows_dev, past, chans)
    final_c = fc.reshape(groups, tensors // groups, past, rows_dev, 2, n)[:, 0]
    final_c = final_c.transpose(2, 1, 3, 0, 4).reshape(rows_dev, past, 2, groups * n)
    return (mixed, final, final_x, final_c)


def solution(mesh):
    placed = (
        P(None, None, "replica"),
        P(),
        P("replica", None, "tensor"),
        P("replica", None, None),
        P("replica", "tensor"),
        P(None, "tensor"),
        P("tensor"),
        P(),
        P(),
        P("tensor"),
        P("tensor"),
        P("tensor"),
        P("tensor"),
        P("tensor", "replica"),
        P("replica", "tensor", None, None),
        P("replica", None, "tensor"),
        P("replica", None, None, None),
    )
    return jax.shard_map(
        local,
        mesh=mesh,
        in_specs=placed,
        out_specs=(
            P(None, "tensor", "replica"),
            P("replica", "tensor", None, None),
            P("replica", None, "tensor"),
            P("replica", None, None, None),
        ),
        check_vma=False,
    )
```
